32 devices in a mesh: wide: 4 (over y, x), seq: 8 (over z, core).
Axes of the slice: x: 2, y: 2, z: 4, core: 2. Of those that a mesh axis runs over, the one named last changes fastest.
Arguments:
- inputs: bfloat16 [2, 4, 512, 2048], P(None, 'wide', 'seq'), may hold values from -6 to 6
- documents: int32 [2, 4, 512], P(None, 'wide'), may hold values from 0 to 10, as said below
- cotangent: bfloat16 [2, 4, 512, 2048], P(None, 'wide', 'seq'), may hold values from -6 to 6
- query_weight: bfloat16 [2048, 2048], P(('wide', 'seq')), may hold values from -0.125 to 0.125
- key_weight: bfloat16 [2048, 2048], P(('wide', 'seq')), may hold values from -0.125 to 0.125
- value_weight: bfloat16 [2048, 2048], P(('wide', 'seq')), may hold values from -0.125 to 0.125
- output_weight: bfloat16 [2048, 2048], P(('wide', 'seq')), may hold values from -0.125 to 0.125
- query_gain: bfloat16 [2048], P(('wide', 'seq')), may hold values from 0.25 to 1.75
- key_gain: bfloat16 [2048], P(('wide', 'seq')), may hold values from 0.25 to 1.75
- attention_gain: bfloat16 [2048], P(('wide', 'seq')), may hold values from 0.25 to 1.75
- gate_weight: bfloat16 [2048, 8192], P(('wide', 'seq')), may hold values from -0.125 to 0.125
- up_weight: bfloat16 [2048, 8192], P(('wide', 'seq')), may hold values from -0.125 to 0.125
- down_weight: bfloat16 [8192, 2048], P(('wide', 'seq')), may hold values from -0.0625 to 0.0625
- feed_gain: bfloat16 [2048], P(('wide', 'seq')), may hold values from 0.25 to 1.75
Outputs:
- layer_out: bfloat16 [2, 4, 512, 2048], P(None, 'wide', 'seq')
- input_grad: float32 [2, 4, 512, 2048], P(None, 'wide', 'seq')
- query_weight_grad: float32 [2048, 2048], P(('wide', 'seq'))
- key_weight_grad: float32 [2048, 2048], P(('wide', 'seq'))
- value_weight_grad: float32 [2048, 2048], P(('wide', 'seq'))
- output_weight_grad: float32 [2048, 2048], P(('wide', 'seq'))
- query_gain_grad: float32 [2048], P(('wide', 'seq'))
- key_gain_grad: float32 [2048], P(('wide', 'seq'))
- attention_gain_grad: float32 [2048], P(('wide', 'seq'))
- gate_weight_grad: float32 [2048, 8192], P(('wide', 'seq'))
- up_weight_grad: float32 [2048, 8192], P(('wide', 'seq'))
- down_weight_grad: float32 [8192, 2048], P(('wide', 'seq'))
- feed_gain_grad: float32 [2048], P(('wide', 'seq'))
The draws below stay inside these ranges and needn't reach their ends.
Inputs may be any that keep to these rules, and one draw needn't show every extreme that they name: Along each row the numbers start at 0 and rise by 0 or 1 from one position to the next; every row holds exactly 11 documents, and one document covers positions 63 to 448.
All inputs are finite; a program needn't handle non-finite values.
Results may differ from the reference program's by a relative error of at most 0.019.
Values may be sent and summed in bfloat16 or wider, within the bound.
A program may use at most 640 MiB of HBM per device.

```python
import jax
import jax.numpy as jnp
from jax import lax

D = 2048
HEADS = 16
HEAD_DIM = 128
FF = 8192
GROUP = 64
MICRO = 2
ROWS = 4
LEN = 512


def pick_starts(key, shape, count, chosen):
    scores = jax.random.randint(key, shape + (count,), 0, 65536) * count + jnp.arange(count, dtype=jnp.int32)
    order = jnp.argsort(scores, axis=-1, stable=True)
    ranks = jnp.argsort(order, axis=-1, stable=True)
    return (ranks < chosen).astype(jnp.int32)


def draw_documents(key, part):
    key_front, key_back = jax.random.split(key, 2)
    shape = (MICRO, ROWS)
    chosen = GROUP // 16 + 1
    front = pick_starts(key_front, shape, GROUP - 1, chosen)
    back = pick_starts(key_back, shape, GROUP - 1, chosen)
    first = jnp.ones(shape + (1,), jnp.int32)
    middle = jnp.zeros(shape + (LEN - 2 * GROUP + 1,), jnp.int32)
    starts = jnp.concatenate([first, front, middle, back], axis=-1)
    return (jnp.cumsum(starts, axis=-1) - 1).astype(jnp.int32)


def raised(drawn, stream_key, source, target, parts, factor):
    owner, partner = [(jnp.arange(drawn.shape[axis_at]) // (drawn.shape[axis_at] // parts)).reshape([-1 if axis == axis_at else 1 for axis in range(drawn.ndim)]) for axis_at in (source, target)]
    chosen = jax.random.permutation(stream_key, parts)[partner]
    strong = (owner == chosen) | (owner == (partner + parts // 2) % parts)
    return jnp.where(strong, factor * drawn, drawn)


def level_of(rng, shape, pieces, smallest, top_value):
    loudness = 1.0
    for position, shards_of in pieces:
        steps = jax.random.uniform(jax.random.fold_in(jax.random.fold_in(rng, 6), position), (shards_of,), jnp.float32, smallest / len(pieces), top_value / len(pieces))
        loudness = loudness * jnp.repeat(jnp.exp(steps), shape[position] // shards_of).reshape((-1,) + (1,) * (len(shape) - 1 - position))
    return loudness


def bell_draw(key, shape, spread, most, cuts=(), kind=jnp.bfloat16):
    level = level_of(key, shape, cuts, -0.22, 0.18) if cuts else 1.0
    values = jax.random.normal(key, shape, jnp.float32) * spread * level
    return jnp.minimum(jnp.maximum(values, -most), most).astype(kind)


def noise_with(stream_key, dims, width, most, cuts, heavy, held_as=jnp.bfloat16):
    values = width * jax.random.normal(stream_key, dims, jnp.float32)
    if cuts:
        values = values * level_of(stream_key, dims, cuts, -0.22, 0.18)
    return jnp.clip(raised(values, jax.random.fold_in(stream_key, 3), *heavy), -most, most).astype(held_as)


def setup_inputs(seed: int = 0) -> dict:
    seeds = jax.random.split(jax.random.key(seed), 15)
    inputs = noise_with(seeds[0], (MICRO, ROWS, LEN, D), 1.0, 6.0, ((1, 4), (2, 8)), (2, 3, 8, 2.0))
    documents = draw_documents(jax.random.fold_in(seeds[14], 71), 0)
    cotangent = bell_draw(seeds[2], (MICRO, ROWS, LEN, D), 1.0, 6.0, ((1, 4), (2, 8)))
    query_weight = bell_draw(seeds[3], (D, D), D ** -0.5, 0.125, ((0, 32),))
    key_weight = bell_draw(seeds[4], (D, D), D ** -0.5, 0.125, ((0, 32),))
    value_weight = bell_draw(seeds[5], (D, D), D ** -0.5, 0.125, ((0, 32),))
    output_weight = bell_draw(seeds[6], (D, D), D ** -0.5, 0.125, ((0, 32),))
    query_gain = jnp.clip(1.0 + 0.15 * jax.random.normal(seeds[7], (D,), jnp.float32), 0.25, 1.75).astype(jnp.bfloat16)
    key_gain = jnp.clip(1.0 + 0.15 * jax.random.normal(seeds[8], (D,), jnp.float32), 0.25, 1.75).astype(jnp.bfloat16)
    attention_gain = jnp.clip(1.0 + 0.15 * jax.random.normal(seeds[9], (D,), jnp.float32), 0.25, 1.75).astype(jnp.bfloat16)
    gate_weight = bell_draw(seeds[10], (D, FF), D ** -0.5, 0.125, ((0, 32),))
    up_weight = bell_draw(seeds[11], (D, FF), D ** -0.5, 0.125, ((0, 32),))
    down_weight = bell_draw(seeds[12], (FF, D), FF ** -0.5, 0.0625, ((0, 32),))
    feed_gain = jnp.clip(1.0 + 0.15 * jax.random.normal(seeds[13], (D,), jnp.float32), 0.25, 1.75).astype(jnp.bfloat16)
    return dict(inputs=inputs, documents=documents, cotangent=cotangent, query_weight=query_weight, key_weight=key_weight, value_weight=value_weight, output_weight=output_weight, query_gain=query_gain, key_gain=key_gain, attention_gain=attention_gain, gate_weight=gate_weight, up_weight=up_weight, down_weight=down_weight, feed_gain=feed_gain)


eps_norm = 1e-06
rope_base = 500000.0
masked_value = -1e+30

@jax.custom_vjp
def low(v):
    return lax.optimization_barrier(v.astype(jnp.bfloat16)).astype(jnp.float32)

@jax.custom_vjp
def low_back(v):
    return v

def low_keep(v):
    return (low(v), None)

def low_pass(kept, grad):
    return (grad,)

def back_keep(v):
    return (v, None)

def back_low(kept, grad):
    return (low(grad),)
low.defvjp(low_keep, low_pass)
low_back.defvjp(back_keep, back_low)

def product(left, right):
    return jnp.dot(left, right, precision=lax.Precision.HIGHEST, preferred_element_type=jnp.float32)

def normalize(values, gain_vec):
    inverse = lax.rsqrt(lax.optimization_barrier(jnp.mean(values * values, axis=-1, keepdims=True)) + eps_norm)
    return values * inverse * gain_vec

def rotate(values, positions):
    half_dim = HEAD_DIM // 2
    frequency = rope_base ** (-jnp.arange(half_dim, dtype=jnp.float32) * 2.0 / HEAD_DIM)
    angles = positions.astype(jnp.float32)[:, None] * frequency[None, :]
    cosine = jnp.cos(angles)[:, None, :]
    sine_table = jnp.sin(angles)[:, None, :]
    first_half = values[..., :half_dim]
    second_half = values[..., half_dim:]
    return jnp.concatenate([first_half * cosine - second_half * sine_table, second_half * cosine + first_half * sine_table], axis=-1)

def sequence_layer(inputs, doc_ids, weights):
    query_weight, key_weight, value_weight, output_weight, query_gain, key_gain, attention_gain, gate_weight, up_weight, down_weight, feed_gain = weights
    length = inputs.shape[0]
    positions = jnp.arange(length, dtype=jnp.int32)
    query_lin = low_back(product(inputs, query_weight))
    key_lin = low_back(product(inputs, key_weight))
    value_lin = low_back(product(inputs, value_weight))
    queries = low(rotate(normalize(query_lin, query_gain).reshape(length, HEADS, HEAD_DIM), positions))
    key_rows = low(rotate(normalize(key_lin, key_gain).reshape(length, HEADS, HEAD_DIM), positions))
    values = low(value_lin).reshape(length, HEADS, HEAD_DIM)
    block_len = min(512, length)
    score_scale = HEAD_DIM ** (-0.5)

    def query_block(start_row):
        row_block = lax.dynamic_slice_in_dim(queries, start_row, block_len, 0)
        row_docs = lax.dynamic_slice_in_dim(doc_ids, start_row, block_len, 0)
        row_pos = start_row + jnp.arange(block_len, dtype=jnp.int32)
        raw_scores = low_back(jnp.einsum('qhd,khd->hqk', row_block, key_rows, precision=lax.Precision.HIGHEST) * score_scale)
        allowed = (positions[None, :] <= row_pos[:, None]) & (doc_ids[None, :] == row_docs[:, None])
        probability = jax.nn.softmax(jnp.where(allowed[None], raw_scores, masked_value), axis=-1)
        return jnp.einsum('hqk,khd->qhd', low(probability), values, precision=lax.Precision.HIGHEST)
    starts = (jnp.arange(length // block_len, dtype=jnp.int32) * block_len).astype(jnp.int32)
    blocks = lax.map(jax.checkpoint(query_block), starts)
    attended = low(low_back(blocks.reshape(length, HEADS * HEAD_DIM)))
    mixed_lin = low_back(product(attended, output_weight))
    hidden = inputs + normalize(mixed_lin, attention_gain)
    hidden_low = low(hidden)
    gate_lin = low_back(product(hidden_low, gate_weight))
    upward = low_back(product(hidden_low, up_weight))
    active = low(jax.nn.silu(gate_lin) * upward)
    down_lin = low_back(product(active, down_weight))
    return hidden + normalize(down_lin, feed_gain)

def reference(inputs, documents, cotangent, query_weight, key_weight, value_weight, output_weight, query_gain, key_gain, attention_gain, gate_weight, up_weight, down_weight, feed_gain):
    weights = tuple((member.astype(jnp.float32) for member in (query_weight, key_weight, value_weight, output_weight, query_gain, key_gain, attention_gain, gate_weight, up_weight, down_weight, feed_gain)))
    flat_in = inputs.astype(jnp.float32).reshape(MICRO * ROWS, LEN, D)
    flat_docs = documents.reshape(MICRO * ROWS, LEN)
    layer = jax.checkpoint(sequence_layer)

    def forward(values, params):

        def advance(carried, member):
            return (carried, layer(member[0], member[1], params))
        unused, outputs = lax.scan(advance, jnp.zeros((), jnp.float32), (values, flat_docs))
        return outputs
    result, pullback = jax.vjp(forward, flat_in, weights)
    input_grad, weight_grads = pullback(cotangent.astype(jnp.float32).reshape(MICRO * ROWS, LEN, D))
    return (result.astype(jnp.bfloat16).reshape(MICRO, ROWS, LEN, D), input_grad.reshape(MICRO, ROWS, LEN, D), weight_grads[0], weight_grads[1], weight_grads[2], weight_grads[3], weight_grads[4], weight_grads[5], weight_grads[6], weight_grads[7], weight_grads[8], weight_grads[9], weight_grads[10])
```

```python
import jax
import jax.numpy as jnp
from jax import lax
from jax.sharding import PartitionSpec as P

HEADS = 16
HEAD_DIM = 128
eps_norm = 1e-06
rope_base = 500000.0
masked_value = -1e30
bf16 = jnp.bfloat16
f32 = jnp.float32


def dot(a, b):
    return jnp.dot(a, b, preferred_element_type=f32)


def dot_t(a, b):
    return lax.dot_general(a, b, (((1,), (1,)), ((), ())), preferred_element_type=f32)


def t_dot(a, b):
    return lax.dot_general(a, b, (((0,), (0,)), ((), ())), preferred_element_type=f32)


def inverse_rms(values):
    return lax.rsqrt(jnp.mean(values * values, axis=-1, keepdims=True) + eps_norm)


def normalize_back(grad_out, normed, inverse, gain_vec):
    scaled = grad_out * gain_vec
    grad_in = inverse * (scaled - normed * jnp.mean(scaled * normed, axis=-1, keepdims=True))
    return grad_in, jnp.sum(grad_out * normed, axis=0)


def rotation_tables(positions):
    half_dim = HEAD_DIM // 2
    frequency = rope_base ** (-jnp.arange(half_dim, dtype=f32) * 2.0 / HEAD_DIM)
    angles = positions.astype(f32)[:, None] * frequency[None, :]
    return jnp.cos(angles)[:, None, :], jnp.sin(angles)[:, None, :]


def rotate(values, cosine, sine_table):
    half_dim = values.shape[-1] // 2
    first_half = values[..., :half_dim]
    second_half = values[..., half_dim:]
    return jnp.concatenate(
        [
            first_half * cosine - second_half * sine_table,
            second_half * cosine + first_half * sine_table,
        ],
        axis=-1,
    )


def seq_gather(block):
    return lax.all_gather(block, "seq", axis=0, tiled=True)


def seq_scatter(partial):
    return lax.psum_scatter(partial.astype(bf16), "seq", scatter_dimension=0, tiled=True).astype(f32)


def wide_gather(block):
    return lax.all_gather(block, "wide", axis=0, tiled=True)


def wide_scatter(partial):
    return lax.psum_scatter(partial.astype(bf16), "wide", scatter_dimension=0, tiled=True)


def on_device(n_w, n_s, inputs, documents, cotangent, query_weight, key_weight, value_weight, output_weight,
              query_gain, key_gain, attention_gain, gate_weight, up_weight, down_weight, feed_gain):
    micro, _, local_len, width = inputs.shape
    tokens = micro * local_len
    heads = HEADS // n_s
    cols = heads * HEAD_DIM
    row_len = documents.shape[2]
    feed = gate_weight.shape[1]
    feed_block = feed // (n_w * n_s)
    rows = query_weight.shape[0]
    scale = HEAD_DIM ** (-0.5)
    s_index = lax.axis_index("seq")

    qkv = jnp.stack([query_weight, key_weight, value_weight], axis=1).reshape(rows, 3, n_s, cols)
    qkv = jnp.moveaxis(qkv, 2, 0).reshape(n_s * rows, 3 * cols)
    qkv = lax.all_to_all(qkv, "seq", 0, 0, tiled=True)
    qkv_all = wide_gather(qkv)
    gate_up = jnp.stack([gate_weight, up_weight], axis=1).reshape(rows, 2, n_w, n_s, feed_block)
    gate_up = jnp.moveaxis(gate_up, 3, 0).reshape(n_s * rows, 2 * n_w * feed_block)
    gate_up = lax.all_to_all(gate_up, "seq", 0, 0, tiled=True)
    gate_up_all = wide_gather(gate_up)
    down_all = wide_gather(down_weight)
    n_dev = n_w * n_s
    out_perm = [(b, (b % n_w) * n_s + b // n_w) for b in range(n_dev)]
    out_all = wide_gather(lax.ppermute(output_weight, ("wide", "seq"), out_perm))

    gains = lax.all_gather(jnp.stack([query_gain, key_gain, attention_gain, feed_gain]), ("wide", "seq"), axis=1, tiled=True).astype(f32)
    own_gains = lax.dynamic_slice_in_dim(gains, s_index * cols, cols, 1)

    flat = inputs.reshape(tokens, width)
    x_all = seq_gather(flat)
    lin = dot(x_all, qkv_all)
    q_lin, k_lin, v_lin = (lin[:, i * cols:(i + 1) * cols] for i in range(3))
    sums = lax.psum(jnp.stack([jnp.sum(q_lin * q_lin, 1), jnp.sum(k_lin * k_lin, 1)]), "seq")
    inv = lax.rsqrt(sums / width + eps_norm)

    def by_row(v):
        v = v.reshape(n_s, micro, local_len, -1)
        return jnp.swapaxes(v, 0, 1).reshape(micro, row_len, heads, HEAD_DIM)

    def by_token(v):
        v = v.reshape(micro, n_s, local_len, cols)
        return jnp.swapaxes(v, 0, 1).reshape(n_s * tokens, cols)

    cosine, sine = rotation_tables(jnp.arange(row_len, dtype=jnp.int32))
    q_n = q_lin * inv[0][:, None]
    k_n = k_lin * inv[1][:, None]
    queries = rotate(by_row(q_n * own_gains[0]), cosine, sine).astype(bf16)
    keys = rotate(by_row(k_n * own_gains[1]), cosine, sine).astype(bf16)
    values = by_row(v_lin).astype(bf16)
    docs = documents[:, 0, :]
    pos = jnp.arange(row_len)
    allowed = (pos[None, :] <= pos[:, None])[None] & (docs[:, None, :] == docs[:, :, None])
    scores = jnp.einsum("mqhd,mkhd->mhqk", queries, keys, preferred_element_type=f32) * scale
    scores = jnp.where(allowed[:, None], scores, masked_value)
    top = jnp.max(scores, -1, keepdims=True)
    e = jnp.exp(scores - top)
    probs = e / jnp.sum(e, -1, keepdims=True)
    probs_low = probs.astype(bf16)
    attended = by_token(jnp.einsum("mhqk,mkhd->mqhd", probs_low, values, preferred_element_type=f32)).astype(bf16)

    mixed = seq_scatter(dot(attended, out_all))
    mixed_inv = inverse_rms(mixed)
    mixed_n = mixed * mixed_inv
    hidden = flat.astype(f32) + mixed_n * gains[2]
    hidden_all = seq_gather(hidden.astype(bf16))
    gate_up_lin = dot(hidden_all, gate_up_all)
    half = n_w * feed_block
    gate_lin, upward = gate_up_lin[:, :half], gate_up_lin[:, half:]
    sigma = jax.nn.sigmoid(gate_lin)
    silu_gate = gate_lin * sigma
    active = (silu_gate * upward).astype(bf16)
    down = seq_scatter(dot(active, down_all))
    down_inv = inverse_rms(down)
    down_n = down * down_inv
    layer_out = (hidden + down_n * gains[3]).astype(bf16).reshape(inputs.shape)

    grad_out = cotangent.reshape(tokens, width).astype(f32)
    d_down, feed_term = normalize_back(grad_out, down_n, down_inv, gains[3])
    d_down_all = seq_gather(d_down.astype(bf16))
    down_grad = wide_scatter(t_dot(active, d_down_all)).astype(f32)
    d_active = dot_t(d_down_all, down_all)
    d_gate = (d_active * upward * sigma * (1.0 + gate_lin * (1.0 - sigma))).astype(bf16)
    d_up = (d_active * silu_gate).astype(bf16)
    d_gate_up = jnp.concatenate([d_gate, d_up], axis=1)
    mlp_grad = wide_scatter(t_dot(hidden_all, d_gate_up))
    d_hidden = grad_out + seq_scatter(dot_t(d_gate_up, gate_up_all))
    d_mixed, attention_term = normalize_back(d_hidden, mixed_n, mixed_inv, gains[2])
    d_mixed_all = seq_gather(d_mixed.astype(bf16))
    out_grad = wide_scatter(t_dot(attended, d_mixed_all))
    d_attended = by_row(dot_t(d_mixed_all, out_all)).astype(bf16)

    d_probs = jnp.einsum("mqhd,mkhd->mhqk", d_attended, values, preferred_element_type=f32)
    delta = jnp.sum(probs * d_probs, -1, keepdims=True)
    d_scores = (probs * (d_probs - delta)).astype(bf16)
    d_q = jnp.einsum("mhqk,mkhd->mqhd", d_scores, keys, preferred_element_type=f32) * scale
    d_k = jnp.einsum("mhqk,mqhd->mkhd", d_scores, queries, preferred_element_type=f32) * scale
    d_v = jnp.einsum("mhqk,mqhd->mkhd", probs_low, d_attended, preferred_element_type=f32)
    d_q = by_token(rotate(d_q, cosine, -sine))
    d_k = by_token(rotate(d_k, cosine, -sine))
    d_qg = d_q * own_gains[0]
    d_kg = d_k * own_gains[1]
    means = lax.psum(jnp.stack([jnp.sum(d_qg * q_n, 1), jnp.sum(d_kg * k_n, 1)]), "seq") / width
    query_term = jnp.sum(d_q * q_n, 0)
    key_term = jnp.sum(d_k * k_n, 0)
    d_q_lin = (inv[0][:, None] * (d_qg - q_n * means[0][:, None])).astype(bf16)
    d_k_lin = (inv[1][:, None] * (d_kg - k_n * means[1][:, None])).astype(bf16)
    d_lin = jnp.concatenate([d_q_lin, d_k_lin, by_token(d_v).astype(bf16)], axis=1)
    input_back = seq_scatter(dot_t(d_lin, qkv_all))
    input_grad = (d_hidden + input_back).reshape(inputs.shape)
    qkv_grad = wide_scatter(t_dot(x_all, d_lin))

    qkv_grad = lax.all_to_all(qkv_grad, "seq", 0, 0, tiled=True).reshape(n_s, rows, 3, cols)
    qkv_grad = jnp.moveaxis(qkv_grad, 0, 2).reshape(rows, 3, width).astype(f32)
    mlp_grad = lax.all_to_all(mlp_grad, "seq", 0, 0, tiled=True).reshape(n_s, rows, 2, n_w, feed_block)
    mlp_grad = jnp.moveaxis(mlp_grad, 0, 3).reshape(rows, 2, feed).astype(f32)
    out_grad = lax.ppermute(out_grad, ("wide", "seq"), [(b, a) for a, b in out_perm]).astype(f32)

    zero = jnp.zeros((width,), f32)
    terms = jnp.stack([
        lax.dynamic_update_slice_in_dim(zero, query_term, s_index * cols, 0),
        lax.dynamic_update_slice_in_dim(zero, key_term, s_index * cols, 0),
        attention_term,
        feed_term,
    ])
    gain_grads = lax.psum_scatter(terms, ("wide", "seq"), scatter_dimension=1, tiled=True)
    return (layer_out, input_grad, qkv_grad[:, 0], qkv_grad[:, 1], qkv_grad[:, 2], out_grad,
            gain_grads[0], gain_grads[1], gain_grads[2], mlp_grad[:, 0], mlp_grad[:, 1], down_grad, gain_grads[3])


def solution(mesh):
    tok = P(None, "wide", "seq", None)
    docs = P(None, "wide", None)
    mat = P(("wide", "seq"), None)
    vec = P(("wide", "seq"))

    def body(*args):
        return on_device(mesh.shape["wide"], mesh.shape["seq"], *args)

    return jax.shard_map(
        body, mesh=mesh,
        in_specs=(tok, docs, tok, mat, mat, mat, mat, vec, vec, vec, mat, mat, mat, vec),
        out_specs=(tok, tok, mat, mat, mat, mat, vec, vec, vec, mat, mat, mat, vec),
        check_vma=False,
    )
```

```python
import functools

import jax
import jax.numpy as jnp
from jax import lax
from jax.experimental import pallas as pl
from jax.experimental.pallas import tpu as pltpu
from jax.sharding import PartitionSpec as P

HEADS = 16
HEAD_DIM = 128
eps_norm = 1e-06
rope_base = 500000.0
masked_value = -1e30
bf16 = jnp.bfloat16
f32 = jnp.float32
MESH = pl.DeviceIdType.MESH
ANY = pl.BlockSpec(memory_space=pl.ANY)
VM = pl.BlockSpec(memory_space=pltpu.VMEM)


def greet(barrier, targets):
    count = 0
    for cond, dev in targets:
        if cond is None:
            pl.semaphore_signal(barrier, inc=1, device_id=dev, device_id_type=MESH)
            count = count + 1
        else:
            @pl.when(cond)
            def _():
                pl.semaphore_signal(barrier, inc=1, device_id=dev, device_id_type=MESH)
            count = count + cond.astype(jnp.int32)
    pl.semaphore_wait(barrier, count)

def gather_kernel(n_s, chunks, x_ref, o_ref, send, recv, mate_send, mate_recv, local_sem):
    s = lax.axis_index("seq")
    nz = n_s // 2
    z, c = s // 2, s % 2
    mate = {"seq": s + 1 - 2 * c}
    rows = x_ref.shape[0] // chunks
    ups = {1: z < nz - 1, -1: z > 0}
    greet(pltpu.get_barrier_semaphore(), [(ups[1], {"seq": s + 2}), (ups[-1], {"seq": s - 2}), (None, mate)])

    def part(ref, slot, k):
        return ref.at[slot, pl.ds(k * rows, rows)]

    def hop(d, direction, k, slot):
        i = 0 if direction == 1 else 1
        src = x_ref.at[pl.ds(k * rows, rows)] if d == 0 else part(o_ref, slot, k)
        return pltpu.make_async_remote_copy(src, part(o_ref, slot, k), send.at[i, d, k], recv.at[i, d, k],
                                            device_id={"seq": s + 2 * direction}, device_id_type=MESH)

    def share(i, d, k, slot):
        src = x_ref.at[pl.ds(k * rows, rows)] if d == 0 else part(o_ref, slot, k)
        return pltpu.make_async_remote_copy(src, part(o_ref, slot, k), mate_send.at[i, d, k], mate_recv.at[i, d, k],
                                            device_id=mate, device_id_type=MESH)

    own = pltpu.make_async_copy(x_ref, o_ref.at[s], local_sem)
    for k in range(chunks):
        for direction in (1, -1):
            @pl.when(ups[direction])
            def _():
                hop(0, direction, k, s).start()
    for k in range(chunks):
        share(0, 0, k, s).start()
    own.start()
    for d in range(1, nz):
        for k in range(chunks):
            for i, direction in enumerate((1, -1)):
                origin = z - direction * d
                there = (origin >= 0) & (origin < nz)
                slot = 2 * origin + c
                @pl.when(there)
                def _():
                    hop(d - 1, direction, k, slot).wait_recv()
                    share(i, d, k, slot).start()
                    if d < nz - 1:
                        @pl.when(ups[direction])
                        def _():
                            hop(d, direction, k, slot).start()
    for k in range(chunks):
        share(0, 0, k, s + 1 - 2 * c).wait_recv()
    for d in range(1, nz):
        for k in range(chunks):
            for i, direction in enumerate((1, -1)):
                origin = z - direction * d
                there = (origin >= 0) & (origin < nz)
                @pl.when(there)
                def _():
                    share(i, d, k, 2 * origin + 1 - c).wait_recv()
    own.wait()
    for k in range(chunks):
        share(0, 0, k, s).wait_send()
        for direction in (1, -1):
            @pl.when(ups[direction])
            def _():
                hop(0, direction, k, s).wait_send()
    for d in range(1, nz):
        for k in range(chunks):
            for i, direction in enumerate((1, -1)):
                origin = z - direction * d
                there = (origin >= 0) & (origin < nz)
                slot = 2 * origin + c
                @pl.when(there)
                def _():
                    share(i, d, k, slot).wait_send()
                    if d < nz - 1:
                        @pl.when(ups[direction])
                        def _():
                            hop(d, direction, k, slot).wait_send()

def seq_gather(x, n_s, cid, chunks=2):
    rows, width = x.shape
    nz = n_s // 2
    sem = pltpu.SemaphoreType.DMA((2, nz, chunks))
    out = pl.pallas_call(
        functools.partial(gather_kernel, n_s, chunks),
        out_shape=jax.ShapeDtypeStruct((n_s, rows, width), x.dtype),
        in_specs=[pl.BlockSpec(memory_space=pl.ANY)],
        out_specs=pl.BlockSpec(memory_space=pl.ANY),
        scratch_shapes=[sem, sem, sem, sem, pltpu.SemaphoreType.DMA],
        compiler_params=pltpu.CompilerParams(collective_id=cid, has_side_effects=True),
    )(x)
    return out.reshape(n_s * rows, width)

def scatter_kernel(n_s, chunks, p_ref, o_ref, from_mate, run, send, recv, mate_send, mate_recv):
    s = lax.axis_index("seq")
    nz = n_s // 2
    z, c = s // 2, s % 2
    mate = {"seq": s + 1 - 2 * c}
    rows = p_ref.shape[1] // chunks
    ups = {1: z < nz - 1, -1: z > 0}
    greet(pltpu.get_barrier_semaphore(), [(ups[1], {"seq": s + 2}), (ups[-1], {"seq": s - 2}), (None, mate)])

    def give(zd, k):
        rs = pl.ds(k * rows, rows)
        return pltpu.make_async_remote_copy(p_ref.at[2 * zd + 1 - c, rs], from_mate.at[zd, rs], mate_send.at[zd, k], mate_recv.at[zd, k],
                                            device_id=mate, device_id_type=MESH)

    def hop(i, zd, k):
        rs = pl.ds(k * rows, rows)
        return pltpu.make_async_remote_copy(run.at[i, zd, rs], run.at[i, zd, rs], send.at[i, zd, k], recv.at[i, zd, k],
                                            device_id={"seq": s + (2 if i == 0 else -2)}, device_id_type=MESH)

    order = []
    for a in range((nz + 1) // 2):
        order += [nz - 1 - a] if nz - 1 - a == a else [nz - 1 - a, a]
    for zd in order:
        for k in range(chunks):
            give(zd, k).start()

    def pair(zd, k):
        rs = pl.ds(k * rows, rows)
        return p_ref[2 * zd + c, rs].astype(f32) + from_mate[zd, rs].astype(f32)

    for step in range(nz - 1):
        for k in range(chunks):
            rs = pl.ds(k * rows, rows)
            for i, zd in ((0, nz - 1 - step), (1, step)):
                going = z < zd if i == 0 else z > zd
                behind = z > 0 if i == 0 else z < nz - 1
                @pl.when(going)
                def _():
                    give(zd, k).wait_recv()
                    @pl.when(behind)
                    def _():
                        hop(i, zd, k).wait_recv()
                        run[i, zd, rs] = (pair(zd, k) + run[i, zd, rs].astype(f32)).astype(bf16)
                    @pl.when(jnp.logical_not(behind))
                    def _():
                        run[i, zd, rs] = pair(zd, k).astype(bf16)
                    hop(i, zd, k).start()
    for zd in range(nz):
        @pl.when(z == zd)
        def _():
            for k in range(chunks):
                rs = pl.ds(k * rows, rows)
                give(zd, k).wait_recv()
                total = pair(zd, k)
                if zd > 0:
                    hop(0, zd, k).wait_recv()
                    total = total + run[0, zd, rs].astype(f32)
                if zd < nz - 1:
                    hop(1, zd, k).wait_recv()
                    total = total + run[1, zd, rs].astype(f32)
                o_ref[rs] = total
    for zd in range(nz):
        for k in range(chunks):
            give(zd, k).wait_send()
    for step in range(nz - 1):
        for k in range(chunks):
            for i, zd in ((0, nz - 1 - step), (1, step)):
                going = z < zd if i == 0 else z > zd
                @pl.when(going)
                def _():
                    hop(i, zd, k).wait_send()

def seq_scatter(p, n_s, cid, chunks=2):
    rows, width = p.shape[0] // n_s, p.shape[1]
    nz = n_s // 2
    sem = pltpu.SemaphoreType.DMA((2, nz, chunks))
    msem = pltpu.SemaphoreType.DMA((nz, chunks))
    vm = pl.BlockSpec(memory_space=pltpu.VMEM)
    return pl.pallas_call(
        functools.partial(scatter_kernel, n_s, chunks),
        out_shape=jax.ShapeDtypeStruct((rows, width), f32),
        in_specs=[vm], out_specs=vm,
        scratch_shapes=[pltpu.VMEM((nz, rows, width), bf16), pltpu.VMEM((2, nz, rows, width), bf16), sem, sem, msem, msem],
        compiler_params=pltpu.CompilerParams(collective_id=cid, has_side_effects=True, vmem_limit_bytes=40 * 2**20),
    )(p.astype(bf16).reshape(n_s, rows, width))

def swap_kernel(n_s, x_ref, o_ref, send, recv, local_sem):
    s = lax.axis_index("seq")
    others = [lax.rem(s + k, n_s) for k in range(1, n_s)]
    greet(pltpu.get_barrier_semaphore(), [(None, {"seq": o}) for o in others])
    own = pltpu.make_async_copy(x_ref.at[s], o_ref.at[s], local_sem)
    def copy(k):
        to = lax.rem(s + k, n_s)
        return pltpu.make_async_remote_copy(x_ref.at[to], o_ref.at[s], send.at[k], recv.at[k], device_id={"seq": to}, device_id_type=MESH)
    for k in range(1, n_s):
        copy(k).start()
    own.start()
    for k in range(1, n_s):
        copy(k).wait()
    own.wait()

def seq_swap(x, n_s, cid):
    sem = pltpu.SemaphoreType.DMA((n_s,))
    anys = pl.BlockSpec(memory_space=pl.ANY)
    return pl.pallas_call(
        functools.partial(swap_kernel, n_s),
        out_shape=jax.ShapeDtypeStruct(x.shape, x.dtype),
        in_specs=[anys], out_specs=anys,
        scratch_shapes=[sem, sem, pltpu.SemaphoreType.DMA],
        compiler_params=pltpu.CompilerParams(collective_id=cid, has_side_effects=True),
    )(x)

def share_kernel(n_w, n_s, whole, x_ref, o_ref, send, recv, local_sem):
    w, s = lax.axis_index("wide"), lax.axis_index("seq")
    wides = range(n_w) if whole else (0,)
    steps = [(a, b) for a in wides for b in range(n_s) if a or b]

    def at(a, b):
        return (lax.rem(w + a, n_w), lax.rem(s + b, n_s))

    def name(place):
        return {"wide": place[0], "seq": place[1]}

    greet(pltpu.get_barrier_semaphore(), [(None, name(at(a, b))) for a, b in steps])
    me = w * n_s + s if whole else s
    swap = len(x_ref.shape) == 3

    def block(place):
        return x_ref.at[place[0] * n_s + place[1] if whole else place[1]] if swap else x_ref

    own = pltpu.make_async_copy(block((w, s)), o_ref.at[me], local_sem)

    def copy(a, b):
        to = at(a, b)
        i = a * n_s + b
        return pltpu.make_async_remote_copy(
            block(to), o_ref.at[me], send.at[i], recv.at[i], device_id=name(to), device_id_type=MESH
        )

    for a, b in steps:
        copy(a, b).start()
    own.start()
    for a, b in steps:
        copy(a, b).wait()
    own.wait()


def exchange(x, n_w, n_s, whole, cid):
    count = n_w * n_s if whole else n_s
    sem = pltpu.SemaphoreType.DMA((count,))
    return pl.pallas_call(
        functools.partial(share_kernel, n_w, n_s, whole),
        out_shape=jax.ShapeDtypeStruct((count, *x.shape[-2:]), x.dtype),
        in_specs=[VM],
        out_specs=VM,
        scratch_shapes=[sem, sem, pltpu.SemaphoreType.DMA],
        compiler_params=pltpu.CompilerParams(collective_id=cid, has_side_effects=True),
    )(x)


def columns_kernel(n_s, plan, to_rows, *refs):
    n = len(plan)
    *arrays, send, recv, local_sem = refs
    split, joined = (arrays[:n], arrays[n]) if not to_rows else (arrays[1:], arrays[0])
    s = lax.axis_index("seq")
    greet(pltpu.get_barrier_semaphore(), [(None, {"seq": lax.rem(s + k, n_s)}) for k in range(1, n_s)])

    def pieces(k):
        there = lax.rem(s + k, n_s)
        for array, parts in zip(split, plan):
            for step, offset, width, column in parts:
                if to_rows:
                    src = joined.at[there, :, pl.ds(column, width)]
                    dst = array.at[:, pl.ds(pl.multiple_of(s * step + offset, 128), width)]
                else:
                    src = array.at[:, pl.ds(pl.multiple_of(there * step + offset, 128), width)]
                    dst = joined.at[s, :, pl.ds(column, width)]
                yield src, dst, {"seq": there}

    for k in range(1, n_s):
        for src, dst, dev in pieces(k):
            pltpu.make_async_remote_copy(src, dst, send.at[k], recv.at[k], device_id=dev, device_id_type=MESH).start()
    for src, dst, dev in pieces(0):
        pltpu.make_async_copy(src, dst, local_sem).start()
    slot = joined.at[0]
    for k in range(1, n_s):
        done = pltpu.make_async_remote_copy(slot, slot, send.at[k], recv.at[k], device_id={"seq": lax.rem(s + k, n_s)}, device_id_type=MESH)
        done.wait_recv()
        done.wait_send()
    pltpu.make_async_copy(slot, slot, local_sem).wait()


def columns_call(arrays, shapes, n_s, plan, to_rows, cid):
    sem = pltpu.SemaphoreType.DMA((n_s,))
    return pl.pallas_call(
        functools.partial(columns_kernel, n_s, plan, to_rows),
        out_shape=shapes,
        in_specs=[ANY] * len(arrays),
        out_specs=[ANY] * len(shapes) if to_rows else ANY,
        scratch_shapes=[sem, sem, pltpu.SemaphoreType.DMA],
        compiler_params=pltpu.CompilerParams(collective_id=cid, has_side_effects=True),
    )(*arrays)


def dot(a, b):
    return jnp.dot(a, b, preferred_element_type=f32)


def dot_t(a, b):
    return lax.dot_general(a, b, (((1,), (1,)), ((), ())), preferred_element_type=f32)


def t_dot(a, b):
    return lax.dot_general(a, b, (((0,), (0,)), ((), ())), preferred_element_type=f32)


def turn(v, cosine, sine):
    return v * cosine + pltpu.roll(v, HEAD_DIM // 2, 1) * sine


def allowed_pairs(doc_q, doc_k, length):
    rows = lax.broadcasted_iota(jnp.int32, (length, length), 0)
    cols = lax.broadcasted_iota(jnp.int32, (length, length), 1)
    return (cols <= rows) & (doc_q == doc_k)


def attend_kernel(scale, ql, kl, vl, inv, gq, gk, cos, sin, doc_q, doc_k, att, q_out, k_out, v_out, lse):
    length = cos.shape[0]

    def flat(ref):
        return ref[...].reshape(length, -1)

    scales = flat(inv)
    q = turn(flat(ql) * scales[:, 0:1] * gq[...], cos[...], sin[...]).astype(bf16)
    k = turn(flat(kl) * scales[:, 1:2] * gk[...], cos[...], sin[...]).astype(bf16)
    v = flat(vl).astype(bf16)
    q_out[...] = q.reshape(q_out.shape)
    k_out[...] = k.reshape(k_out.shape)
    v_out[...] = v.reshape(v_out.shape)
    allowed = allowed_pairs(doc_q[0], doc_k[0], length)
    scores = jnp.where(allowed, dot_t(q, k) * scale, masked_value)
    top = jnp.max(scores, 1, keepdims=True)
    e = jnp.exp(scores - top)
    total = jnp.sum(e, 1, keepdims=True)
    probs = (e * (1.0 / total)).astype(bf16)
    att[...] = dot(probs, v).astype(bf16).reshape(att.shape)
    lse[...] = (top + jnp.log(total)).reshape(lse.shape)


def attend_back_kernel(scale, q, k, v, lse, da, cos, sin, doc_q, doc_k, dq_out, dk_out, dv_out):
    length = cos.shape[0]

    def flat(ref):
        return ref[...].reshape(length, -1)

    queries, keys, values, d_att = flat(q), flat(k), flat(v), flat(da)
    allowed = allowed_pairs(doc_q[0], doc_k[0], length)
    scores = jnp.where(allowed, dot_t(queries, keys) * scale, masked_value)
    probs = jnp.exp(scores - flat(lse))
    d_probs = dot_t(d_att, values)
    delta = jnp.sum(probs * d_probs, 1, keepdims=True)
    d_scores = (probs * (d_probs - delta)).astype(bf16)
    d_q = dot(d_scores, keys) * scale
    d_k = t_dot(d_scores, queries) * scale
    dv_out[...] = t_dot(probs.astype(bf16), d_att).astype(bf16).reshape(dv_out.shape)
    dq_out[...] = turn(d_q, cos[...], -sin[...]).reshape(dq_out.shape)
    dk_out[...] = turn(d_k, cos[...], -sin[...]).reshape(dk_out.shape)


def attention_specs(n_s, local, length):
    def tok(first):
        return pl.BlockSpec((n_s, 1, local, HEAD_DIM), lambda m, h: (0, m, 0, first + h))

    gain = pl.BlockSpec((1, HEAD_DIM), lambda m, h: (0, h))
    table = pl.BlockSpec((length, HEAD_DIM), lambda m, h: (0, 0))
    doc_q = pl.BlockSpec((1, length, 1), lambda m, h: (m, 0, 0))
    doc_k = pl.BlockSpec((1, 1, length), lambda m, h: (m, 0, 0))
    col = pl.BlockSpec((1, n_s, 1, local, 1), lambda m, h: (h, 0, m, 0, 0))
    return tok, gain, table, doc_q, doc_k, col


def attend(lin, inv, gains, tables, docs, heads, scale):
    n_s, micro, local, _ = lin.shape
    length = n_s * local
    tok, gain, table, doc_q, doc_k, col = attention_specs(n_s, local, length)
    inv_spec = pl.BlockSpec((n_s, 1, local, 2), lambda m, h: (0, m, 0, 0))
    out = jax.ShapeDtypeStruct((n_s, micro, local, heads * HEAD_DIM), bf16)
    return pl.pallas_call(
        functools.partial(attend_kernel, scale),
        grid=(micro, heads),
        out_shape=[out, out, out, out, jax.ShapeDtypeStruct((heads, n_s, micro, local, 1), f32)],
        in_specs=[tok(0), tok(heads), tok(2 * heads), inv_spec, gain, gain, table, table, doc_q, doc_k],
        out_specs=[tok(0)] * 4 + [col],
        compiler_params=pltpu.CompilerParams(vmem_limit_bytes=48 * 2**20),
    )(lin, lin, lin, inv, gains[0:1], gains[1:2], *tables, docs[:, :, None], docs[:, None, :])


def attend_back(q, k, v, lse, d_att, tables, docs, heads, scale):
    n_s, micro, local, width = q.shape
    length = n_s * local
    tok, gain, table, doc_q, doc_k, col = attention_specs(n_s, local, length)
    return pl.pallas_call(
        functools.partial(attend_back_kernel, scale),
        grid=(micro, heads),
        out_shape=[jax.ShapeDtypeStruct(q.shape, f32)] * 2 + [jax.ShapeDtypeStruct(q.shape, bf16)],
        in_specs=[tok(0)] * 3 + [col, tok(0), table, table, doc_q, doc_k],
        out_specs=[tok(0)] * 3,
        compiler_params=pltpu.CompilerParams(vmem_limit_bytes=48 * 2**20),
    )(q, k, v, lse, d_att, *tables, docs[:, :, None], docs[:, None, :])


def inverse_rms(values):
    return lax.rsqrt(jnp.mean(values * values, axis=-1, keepdims=True) + eps_norm)


def normalize_back(grad_out, normed, inverse, gain_vec):
    scaled = grad_out * gain_vec
    grad_in = inverse * (scaled - normed * jnp.mean(scaled * normed, axis=-1, keepdims=True))
    return grad_in, jnp.sum(grad_out * normed, axis=0)


def rotation_tables(positions):
    half_dim = HEAD_DIM // 2
    frequency = rope_base ** (-jnp.arange(half_dim, dtype=f32) * 2.0 / HEAD_DIM)
    angles = positions.astype(f32)[:, None] * frequency[None, :]
    cosine, sine = jnp.cos(angles), jnp.sin(angles)
    return jnp.concatenate([cosine, cosine], 1), jnp.concatenate([-sine, sine], 1)


def wide_gather(block):
    return lax.all_gather(block, "wide", axis=0, tiled=True)


def wide_scatter(partial):
    return lax.psum_scatter(partial.astype(bf16), "wide", scatter_dimension=0, tiled=True)


def on_device(n_w, n_s, inputs, documents, cotangent, query_weight, key_weight, value_weight, output_weight,
              query_gain, key_gain, attention_gain, gate_weight, up_weight, down_weight, feed_gain):
    micro, _, local, width = inputs.shape
    tokens = micro * local
    n_dev = n_w * n_s
    heads = HEADS // n_s
    cols = heads * HEAD_DIM
    row_len = documents.shape[2]
    feed = gate_weight.shape[1]
    feed_block = feed // n_dev
    half = n_w * feed_block
    rows = query_weight.shape[0]
    scale = HEAD_DIM ** (-0.5)
    s_index = lax.axis_index("seq")

    flat = inputs.reshape(tokens, width)
    qkv_plan = [[(cols, 0, cols, i * cols)] for i in range(3)]
    own_blocks = feed_block % 128 == 0
    moves = [(b, (b % n_w) * n_s + b // n_w) for b in range(n_dev)]
    back_moves = [(b, a) for a, b in moves]
    if own_blocks:
        feed_plan = [[(feed_block, a * n_s * feed_block, feed_block, i * half + a * feed_block) for a in range(n_w)] for i in range(2)]
    else:
        feed_plan = [[(half, 0, half, i * half)] for i in range(2)]
    qkv = columns_call((query_weight, key_weight, value_weight), jax.ShapeDtypeStruct((n_s, rows, 3 * cols), bf16), n_s, qkv_plan, False, 0)
    qkv_all = wide_gather(qkv.reshape(n_s * rows, 3 * cols))
    x_all = seq_gather(flat, n_s, 1)
    gate_up = columns_call((gate_weight, up_weight), jax.ShapeDtypeStruct((n_s, rows, 2 * half), bf16), n_s, feed_plan, False, 2)
    gate_up_all = wide_gather(gate_up.reshape(n_s * rows, 2 * half))
    down_all = wide_gather(down_weight if own_blocks else lax.ppermute(down_weight, ("wide", "seq"), moves))
    out_all = wide_gather(lax.ppermute(output_weight, ("wide", "seq"), moves))

    own_gain = jnp.stack([query_gain, key_gain, attention_gain, feed_gain]).astype(f32)
    own_gain = jnp.pad(own_gain, ((0, 4), (0, 128 - rows)))
    gains = exchange(own_gain, n_w, n_s, True, 3)[:, :4, :rows]
    gains = jnp.swapaxes(gains, 0, 1).reshape(4, width)
    own_gains = lax.dynamic_slice_in_dim(gains, s_index * cols, cols, 1)

    lin = dot(x_all, qkv_all)
    q_lin, k_lin = lin[:, :cols], lin[:, cols:2 * cols]

    def seq_sums(a, b, cid):
        return jnp.sum(exchange(jnp.stack([a, b] + [jnp.zeros_like(a)] * 6), n_w, n_s, False, cid), 0)[:2]

    inv = lax.rsqrt(seq_sums(jnp.sum(q_lin * q_lin, 1), jnp.sum(k_lin * k_lin, 1), 4) / width + eps_norm).T
    tables = rotation_tables(jnp.arange(row_len, dtype=jnp.int32))
    docs = documents[:, 0, :]
    shape4 = (n_s, micro, local, -1)
    attended, q, k, v, lse = attend(lin.reshape(shape4), inv.reshape(shape4), own_gains, tables, docs, heads, scale)
    attended = attended.reshape(n_s * tokens, cols)

    mixed = seq_scatter(dot(attended, out_all), n_s, 5)
    mixed_inv = inverse_rms(mixed)
    mixed_n = mixed * mixed_inv
    hidden = flat.astype(f32) + mixed_n * gains[2]
    hidden_all = seq_gather(hidden.astype(bf16), n_s, 6)
    gate_up_lin = dot(hidden_all, gate_up_all)
    gate_lin, upward = gate_up_lin[:, :half], gate_up_lin[:, half:]
    sigma = jax.nn.sigmoid(gate_lin)
    silu_gate = gate_lin * sigma
    active = (silu_gate * upward).astype(bf16)
    down = seq_scatter(dot(active, down_all), n_s, 7)
    down_inv = inverse_rms(down)
    down_n = down * down_inv
    layer_out = (hidden + down_n * gains[3]).astype(bf16).reshape(inputs.shape)

    grad_out = cotangent.reshape(tokens, width).astype(f32)
    d_down, feed_term = normalize_back(grad_out, down_n, down_inv, gains[3])
    d_down_all = seq_gather(d_down.astype(bf16), n_s, 8)
    down_grad = wide_scatter(t_dot(active, d_down_all))
    if not own_blocks:
        down_grad = lax.ppermute(down_grad, ("wide", "seq"), back_moves)
    down_grad = down_grad.astype(f32)
    d_active = dot_t(d_down_all, down_all)
    d_gate = (d_active * upward * sigma * (1.0 + gate_lin * (1.0 - sigma))).astype(bf16)
    d_up = (d_active * silu_gate).astype(bf16)
    d_gate_up = jnp.concatenate([d_gate, d_up], axis=1)
    mlp_grad = wide_scatter(t_dot(hidden_all, d_gate_up))
    d_hidden = grad_out + seq_scatter(dot_t(d_gate_up, gate_up_all), n_s, 9)
    d_mixed, attention_term = normalize_back(d_hidden, mixed_n, mixed_inv, gains[2])
    d_mixed_all = seq_gather(d_mixed.astype(bf16), n_s, 10)
    out_grad = wide_scatter(t_dot(attended, d_mixed_all))
    d_attended = dot_t(d_mixed_all, out_all).astype(bf16).reshape(shape4)

    d_q, d_k, d_v = attend_back(q, k, v, lse, d_attended, tables, docs, heads, scale)
    d_q, d_k, d_v = (t.reshape(n_s * tokens, cols) for t in (d_q, d_k, d_v))
    q_n, k_n = q_lin * inv[:, 0:1], k_lin * inv[:, 1:2]
    d_qg, d_kg = d_q * own_gains[0], d_k * own_gains[1]
    means = seq_sums(jnp.sum(d_qg * q_n, 1), jnp.sum(d_kg * k_n, 1), 11).T / width
    query_term = jnp.sum(d_q * q_n, 0)
    key_term = jnp.sum(d_k * k_n, 0)
    d_q_lin = (inv[:, 0:1] * (d_qg - q_n * means[:, 0:1])).astype(bf16)
    d_k_lin = (inv[:, 1:2] * (d_kg - k_n * means[:, 1:2])).astype(bf16)
    d_lin = jnp.concatenate([d_q_lin, d_k_lin, d_v], axis=1)
    input_back = seq_scatter(dot_t(d_lin, qkv_all), n_s, 12)
    input_grad = (d_hidden + input_back).reshape(inputs.shape)
    qkv_grad = wide_scatter(t_dot(x_all, d_lin))

    mat = jax.ShapeDtypeStruct((rows, width), bf16)
    wide_mat = jax.ShapeDtypeStruct((rows, feed), bf16)
    gate_grad, up_grad = columns_call((mlp_grad.reshape(n_s, rows, 2 * half),), [wide_mat] * 2, n_s, feed_plan, True, 13)
    query_grad, key_grad, value_grad = columns_call((qkv_grad.reshape(n_s, rows, 3 * cols),), [mat] * 3, n_s, qkv_plan, True, 14)
    out_grad = lax.ppermute(out_grad, ("wide", "seq"), back_moves)

    zero = jnp.zeros((width,), f32)
    terms = jnp.stack([
        lax.dynamic_update_slice_in_dim(zero, query_term, s_index * cols, 0),
        lax.dynamic_update_slice_in_dim(zero, key_term, s_index * cols, 0),
        attention_term,
        feed_term,
    ])
    terms = jnp.swapaxes(terms.reshape(4, n_dev, rows), 0, 1)
    terms = jnp.pad(terms, ((0, 0), (0, 4), (0, 128 - rows)))
    gain_grads = jnp.sum(exchange(terms, n_w, n_s, True, 15), 0)[:4, :rows]
    return (layer_out, input_grad, *(g.astype(f32) for g in (query_grad, key_grad, value_grad, out_grad)),
            gain_grads[0], gain_grads[1], gain_grads[2], gate_grad.astype(f32), up_grad.astype(f32), down_grad, gain_grads[3])


def solution(mesh):
    tok = P(None, "wide", "seq", None)
    docs = P(None, "wide", None)
    mat = P(("wide", "seq"), None)
    vec = P(("wide", "seq"))

    def body(*args):
        return on_device(mesh.shape["wide"], mesh.shape["seq"], *args)

    return jax.shard_map(
        body,
        mesh=mesh,
        in_specs=(tok, docs, tok, mat, mat, mat, mat, vec, vec, vec, mat, mat, mat, vec),
        out_specs=(tok, tok, mat, mat, mat, mat, vec, vec, vec, mat, mat, mat, vec),
        check_vma=False,
    )
```

```python
import functools

import jax
import jax.numpy as jnp
from jax import lax
from jax.experimental import pallas as pl
from jax.experimental.pallas import tpu as pltpu
from jax.sharding import PartitionSpec as P

HEADS = 16
HEAD_DIM = 128
eps_norm = 1e-06
rope_base = 500000.0
masked_value = -1e30
bf16 = jnp.bfloat16
f32 = jnp.float32
MESH = pl.DeviceIdType.MESH
ANY = pl.BlockSpec(memory_space=pl.ANY)
VM = pl.BlockSpec(memory_space=pltpu.VMEM)
DMA = pltpu.SemaphoreType.DMA
PACE = 1
CHUNKS = 4
SUB = 4


def params(cid, megabytes=None):
    limit = {} if megabytes is None else {"vmem_limit_bytes": megabytes * 2**20}
    return pltpu.CompilerParams(collective_id=cid, has_side_effects=True, **limit)


def cost(microseconds):
    return pl.CostEstimate(flops=0, transcendentals=0, bytes_accessed=int(microseconds * 3e6))


def remote(src, dst, send, recv, device):
    return pltpu.make_async_remote_copy(src, dst, send, recv, device_id=device, device_id_type=MESH)


def greet(targets):
    barrier = pltpu.get_barrier_semaphore()
    count = 0
    for cond, dev in targets:
        if cond is None:
            pl.semaphore_signal(barrier, inc=1, device_id=dev, device_id_type=MESH)
            count = count + 1
        else:

            @pl.when(cond)
            def _():
                pl.semaphore_signal(barrier, inc=1, device_id=dev, device_id_type=MESH)

            count = count + cond.astype(jnp.int32)
    pl.semaphore_wait(barrier, count)


class Line:
    def __init__(self, n_s):
        self.s = lax.axis_index("seq")
        self.nz = n_s // 2
        self.z, self.c = self.s // 2, self.s % 2
        self.mate_slot = self.s + 1 - 2 * self.c
        self.mate = {"seq": self.mate_slot}
        self.steps = (1, -1)
        self.more = (self.z < self.nz - 1, self.z > 0)
        self.next = ({"seq": self.s + 2}, {"seq": self.s - 2})

    def neighbours(self):
        return [(self.more[0], self.next[0]), (self.more[1], self.next[1]), (None, self.mate)]


class Gather:
    def __init__(self, line, own, out, chunks, send, recv, mate_send, mate_recv):
        self.line, self.own, self.out = line, own, out
        self.chunks, self.rows = chunks, own.shape[0] // chunks
        self.send, self.recv, self.mate_send, self.mate_recv = send, recv, mate_send, mate_recv

    def part(self, slot, k):
        return self.out.at[slot, pl.ds(k * self.rows, self.rows)]

    def source(self, d, k, slot):
        return self.own.at[pl.ds(k * self.rows, self.rows)] if d == 0 else self.part(slot, k)

    def hop(self, i, d, k, slot):
        return remote(self.source(d, k, slot), self.part(slot, k), self.send.at[i, d, k], self.recv.at[i, d, k], self.line.next[i])

    def share(self, i, d, k, slot):
        return remote(self.source(d, k, slot), self.part(slot, k), self.mate_send.at[i, d, k], self.mate_recv.at[i, d, k], self.line.mate)

    def start(self, k):
        line = self.line
        for i in range(2):

            @pl.when(line.more[i])
            def _():
                self.hop(i, 0, k, line.s).start()

        self.share(0, 0, k, line.s).start()

    def each(self, d, mine=True):
        line = self.line
        for i in range(2):
            origin = line.z - line.steps[i] * d
            yield i, (origin >= 0) & (origin < line.nz), 2 * origin + (line.c if mine else 1 - line.c)

    def pass_on(self, d, k):
        for i, there, slot in self.each(d):

            @pl.when(there)
            def _():
                self.hop(i, d - 1, k, slot).wait_recv()
                if d < self.line.nz - 1:

                    @pl.when(self.line.more[i])
                    def _():
                        self.hop(i, d, k, slot).start()

                self.share(i, d, k, slot).start()

    def finish(self):
        line = self.line
        for k in range(self.chunks):
            self.share(0, 0, k, line.mate_slot).wait_recv()
            for d in range(1, line.nz):
                for i, there, slot in self.each(d, False):

                    @pl.when(there)
                    def _():
                        self.share(i, d, k, slot).wait_recv()

        for k in range(self.chunks):
            self.share(0, 0, k, line.s).wait_send()
            for i in range(2):

                @pl.when(line.more[i])
                def _():
                    self.hop(i, 0, k, line.s).wait_send()

            for d in range(1, line.nz):
                for i, there, slot in self.each(d):

                    @pl.when(there)
                    def _():
                        self.share(i, d, k, slot).wait_send()
                        if d < line.nz - 1:

                            @pl.when(line.more[i])
                            def _():
                                self.hop(i, d, k, slot).wait_send()


class Scatter:
    def __init__(self, line, part, from_mate, run, chunks, send, recv, mate_send, mate_recv):
        self.line, self.part, self.from_mate, self.run = line, part, from_mate, run
        self.chunks, self.rows = chunks, part.shape[1] // chunks
        self.send, self.recv, self.mate_send, self.mate_recv = send, recv, mate_send, mate_recv
        self.steps = line.nz - 1
        self.groups = chunks // SUB
        self.count = self.steps * self.groups

    def span(self, k):
        return pl.ds(pl.multiple_of(k * self.rows, self.rows), self.rows)

    def give(self, zd, k):
        line, rs = self.line, self.span(k)
        return remote(self.part.at[2 * zd + 1 - line.c, rs], self.from_mate.at[zd, rs], self.mate_send.at[zd, k], self.mate_recv.at[zd, k], line.mate)

    def hop(self, i, zd, k):
        ref = self.run.at[i, zd, self.span(k)]
        return remote(ref, ref, self.send.at[i, zd, k], self.recv.at[i, zd, k], self.line.next[i])

    def pair(self, zd, k):
        rs = self.span(k)
        return self.part[2 * zd + self.line.c, rs].astype(f32) + self.from_mate[zd, rs].astype(f32)

    def start(self, k):
        nz = self.line.nz
        for zd in sorted(range(nz), key=lambda zd: (min(zd, nz - 1 - zd), -zd)):
            self.give(zd, k).start()

    def item(self, i, q, j):
        group, step = q // self.steps, lax.rem(q, self.steps)
        return (self.line.nz - 1 - step if i == 0 else step), group * SUB + j

    def slot(self, t):
        line = self.line
        for j, i in ((j, i) for j in range(SUB) for i in range(2)):
            q = t - (line.z if i == 0 else line.nz - 1 - line.z)
            behind = line.z > 0 if i == 0 else line.z < line.nz - 1
            zd, k = self.item(i, jnp.clip(q, 0, self.count - 1), j)
            going = (q >= 0) & (q < self.count) & (line.z < zd if i == 0 else line.z > zd)

            @pl.when(going)
            def _():
                rs = self.span(k)
                self.give(zd, k).wait_recv()

                @pl.when(behind)
                def _():
                    self.hop(i, zd, k).wait_recv()
                    self.run[i, zd, rs] = (self.pair(zd, k) + self.run[i, zd, rs].astype(f32)).astype(bf16)

                @pl.when(jnp.logical_not(behind))
                def _():
                    self.run[i, zd, rs] = self.pair(zd, k).astype(bf16)
                    if t >= PACE:
                        self.hop(i, *self.item(i, jnp.int32(t - PACE), j)).wait_send()

                self.hop(i, zd, k).start()

    def total(self, k, use):
        line, rs = self.line, self.span(k)
        for zd in range(line.nz):

            @pl.when(line.z == zd)
            def _():
                self.give(zd, k).wait_recv()
                total = self.pair(zd, k)
                if zd > 0:
                    self.hop(0, zd, k).wait_recv()
                    total = total + self.run[0, zd, rs].astype(f32)
                if zd < line.nz - 1:
                    self.hop(1, zd, k).wait_recv()
                    total = total + self.run[1, zd, rs].astype(f32)
                use(total)

    def finish(self):
        line = self.line
        for k in range(self.chunks):
            for zd in range(line.nz):
                self.give(zd, k).wait_send()
        for q in range(self.count):
            step = q % self.steps
            for i, zd in ((0, line.nz - 1 - step), (1, step)):
                going = line.z < zd if i == 0 else line.z > zd
                behind = line.z > 0 if i == 0 else line.z < line.nz - 1

                @pl.when(going & behind if q < self.count - PACE else going)
                def _():
                    for j in range(SUB):
                        self.hop(i, zd, q // self.steps * SUB + j).wait_send()


def line_sems(nz, chunks):
    return [DMA((2, nz, chunks))] * 4


def scatter_scratch(n_s, rows, width, chunks):
    nz = n_s // 2
    sums = [pltpu.VMEM((nz, rows, width), bf16), pltpu.VMEM((2, nz, rows, width), bf16)]
    return sums + [DMA((2, nz, chunks))] * 2 + [DMA((nz, chunks))] * 2


def mixed_rows(rs, total, x, gain, hidden, normed, inverse, low):
    inv = inverse_rms(total)
    n = total * inv
    out = x[rs].astype(f32) + n * gain[...]
    hidden[rs] = out
    normed[rs] = n
    inverse[rs] = inv
    low[rs] = out.astype(bf16)


def down_rows(rs, total, hidden, cotangent, gain, out, term, low):
    inv = inverse_rms(total)
    n = total * inv
    g = gain[...]
    out[rs] = (hidden[rs] + n * g).astype(bf16)
    grad = cotangent[rs].astype(f32)
    low[rs], more = back_rows(grad, n, inv, g)
    term[...] += more


def hidden_rows(rs, total, cotangent, normed, inverse, gain, d_hidden, term, low):
    grad = cotangent[rs].astype(f32) + total
    d_hidden[rs] = grad
    low[rs], more = back_rows(grad, normed[rs], inverse[rs], gain[...])
    term[...] += more


def back_rows(grad, n, inv, gain):
    scaled = grad * gain
    d = inv * (scaled - n * jnp.mean(scaled * n, axis=-1, keepdims=True))
    return d.astype(bf16), jnp.sum(grad * n, axis=0, keepdims=True)


def run_slots(scatter, use, gather=None):
    steps, groups = scatter.steps, scatter.groups
    for t in range(steps * (groups + (1 if gather else 0)) + 1):
        if t < steps * (groups + 1):
            scatter.slot(t)
        if gather:
            for group in range(groups):
                if 1 <= t - steps * (group + 1) <= steps:
                    for j in range(SUB):
                        gather.pass_on(t - steps * (group + 1), group * SUB + j)
        if t and t % steps == 0 and t // steps <= groups:
            for k in range((t // steps - 1) * SUB, t // steps * SUB):
                scatter.total(k, lambda total: use(k, total))
                if gather:
                    gather.start(k)


def around_kernel(n_s, chunks, rows_fn, n_in, n_out, adds, *refs):
    part, extra = refs[0], refs[1 : 1 + n_in]
    gathered, outs = refs[1 + n_in], refs[2 + n_in : 2 + n_in + n_out]
    low, local, from_mate, run, *sems = refs[2 + n_in + n_out :]
    line = Line(n_s)
    scatter = Scatter(line, part, from_mate, run, chunks, *sems[:4])
    gather = Gather(line, low, gathered, chunks, *sems[4:])
    greet(line.neighbours())
    for k in range(chunks):
        scatter.start(k)
    if adds:
        outs[-1][...] = jnp.zeros_like(outs[-1])
    run_slots(scatter, lambda k, total: rows_fn(scatter.span(k), total, *extra, *outs, low), gather)
    own = pltpu.make_async_copy(low, gathered.at[line.s], local)
    own.start()
    gather.finish()
    scatter.finish()
    own.wait()


def around(terms, extra, rows_fn, outs, n_s, cid, adds, chunks=CHUNKS):
    rows, width = terms.shape[0] // n_s, terms.shape[1]
    return pl.pallas_call(
        functools.partial(around_kernel, n_s, chunks, rows_fn, len(extra), len(outs), adds),
        out_shape=[jax.ShapeDtypeStruct((n_s, rows, width), bf16)] + [jax.ShapeDtypeStruct(*o) for o in outs],
        in_specs=[VM] * (1 + len(extra)),
        out_specs=[ANY] + [VM] * len(outs),
        scratch_shapes=[pltpu.VMEM((rows, width), bf16), DMA] + scatter_scratch(n_s, rows, width, chunks) + line_sems(n_s // 2, chunks),
        compiler_params=params(cid, 48),
        cost_estimate=cost(70),
    )(terms.reshape(n_s, rows, width), *extra)


def last_kernel(n_s, chunks, part, d_hidden, out, from_mate, run, *sems):
    line = Line(n_s)
    scatter = Scatter(line, part, from_mate, run, chunks, *sems)
    greet(line.neighbours())
    for k in range(chunks):
        scatter.start(k)

    def use(k, total):
        out[scatter.span(k)] = d_hidden[scatter.span(k)] + total

    run_slots(scatter, use)
    scatter.finish()


def last_sum(terms, d_hidden, n_s, cid, chunks=CHUNKS):
    rows, width = terms.shape[0] // n_s, terms.shape[1]
    return pl.pallas_call(
        functools.partial(last_kernel, n_s, chunks),
        out_shape=jax.ShapeDtypeStruct((rows, width), f32),
        in_specs=[VM, VM],
        out_specs=VM,
        scratch_shapes=scatter_scratch(n_s, rows, width, chunks),
        compiler_params=params(cid, 48),
        cost_estimate=cost(40),
    )(terms.reshape(n_s, rows, width), d_hidden)


class Columns:
    def __init__(self, n_s, plan, arrays, slots, back, send, recv, local):
        self.n_s, self.plan, self.arrays, self.slots, self.back = n_s, plan, arrays, slots, back
        self.send, self.recv, self.local = send, recv, local
        self.s = lax.axis_index("seq")

    def place(self, k):
        return lax.rem(self.s + k, self.n_s)

    def pieces(self, k):
        there = self.place(k)
        for array, parts in zip(self.arrays, self.plan):
            for first, width, column in parts:
                at = pl.ds(column, width)
                if self.back:
                    yield self.slots.at[there, :, at], array.at[:, pl.ds(pl.multiple_of(first(self.s), 128), width)]
                else:
                    yield array.at[:, pl.ds(pl.multiple_of(first(there), 128), width)], self.slots.at[self.s, :, at]

    def start(self):
        for k in range(1, self.n_s):
            for src, dst in self.pieces(k):
                remote(src, dst, self.send.at[k], self.recv.at[k], {"seq": self.place(k)}).start()
        for src, dst in self.pieces(0):
            pltpu.make_async_copy(src, dst, self.local).start()

    def finish(self):
        slot = self.slots.at[0]
        for k in range(1, self.n_s):
            done = remote(slot, slot, self.send.at[k], self.recv.at[k], {"seq": self.place(k)})
            done.wait_recv()
            done.wait_send()
        pltpu.make_async_copy(slot, slot, self.local).wait()


def columns_sems(n_s):
    return [DMA((n_s,)), DMA((n_s,)), DMA]


def seq_others(n_s):
    s = lax.axis_index("seq")
    return [(None, {"seq": lax.rem(s + k, n_s)}) for k in range(1, n_s)]


class Share:
    def __init__(self, n_w, n_s, whole, x, out, send, recv, local):
        self.n_w, self.n_s, self.whole = n_w, n_s, whole
        self.x, self.out, self.send, self.recv, self.local = x, out, send, recv, local
        self.w, self.s = lax.axis_index("wide"), lax.axis_index("seq")
        self.steps = [(a, b) for a in (range(n_w) if whole else (0,)) for b in range(n_s) if a or b]

    def at(self, a, b):
        return lax.rem(self.w + a, self.n_w), lax.rem(self.s + b, self.n_s)

    def number(self, a, b):
        w, s = self.at(a, b)
        return w * self.n_s + s if self.whole else s

    def name(self, a, b):
        w, s = self.at(a, b)
        return {"wide": w, "seq": s}

    def others(self):
        return [(None, self.name(a, b)) for a, b in self.steps]

    def block(self, a, b):
        return self.x.at[self.number(a, b)] if len(self.x.shape) == 3 else self.x

    def copy(self, a, b):
        i = a * self.n_s + b
        return remote(self.block(a, b), self.out.at[self.number(0, 0)], self.send.at[i], self.recv.at[i], self.name(a, b))

    def own(self):
        return pltpu.make_async_copy(self.block(0, 0), self.out.at[self.number(0, 0)], self.local)

    def start(self):
        for a, b in self.steps:
            self.copy(a, b).start()
        self.own().start()

    def finish(self):
        for a, b in self.steps:
            self.copy(a, b).wait()
        self.own().wait()


def share_kernel(n_w, n_s, whole, x_ref, o_ref, send, recv, local_sem):
    share = Share(n_w, n_s, whole, x_ref, o_ref, send, recv, local_sem)
    greet(share.others())
    share.start()
    share.finish()


def exchange(x, n_w, n_s, whole, cid):
    count = n_w * n_s if whole else n_s
    return pl.pallas_call(
        functools.partial(share_kernel, n_w, n_s, whole),
        out_shape=jax.ShapeDtypeStruct((count, *x.shape[-2:]), x.dtype),
        in_specs=[VM],
        out_specs=VM,
        scratch_shapes=[DMA((count,)), DMA((count,)), DMA],
        compiler_params=params(cid),
        cost_estimate=cost(10),
    )(x)


class Halves:
    def __init__(self, n_w, natural, heads, back, send, recv, local):
        s = lax.axis_index("seq")
        c = lax.rem(s, 2)
        self.back, self.count = back, n_w // 2
        self.send, self.recv, self.local = send, recv, local
        mate = {"seq": s + 1 - 2 * c}
        self.away, self.stay = [], []
        for i in range(self.count):
            mine, his = c * self.count + i, (1 - c) * self.count + i
            if back:
                pair = heads.at[i, 1 - c], natural.at[mine]
                own = heads.at[i, c], natural.at[mine]
            else:
                pair = natural.at[his], heads.at[i, c]
                own = natural.at[mine], heads.at[i, c]
            self.away.append(remote(*pair, send.at[i], recv.at[i], mate))
            self.stay.append(pltpu.make_async_copy(*own, local.at[i]))

    def start(self):
        for copy in self.away + self.stay:
            copy.start()

    def finish(self):
        for copy in self.away + self.stay:
            copy.wait()


def halves_sems(n_w):
    return [DMA((n_w // 2,))] * 3


def first_kernel(n_s, plan, qw, kw, vw, qkv, *sems):
    columns = Columns(n_s, plan, (qw, kw, vw), qkv, False, *sems)
    greet(seq_others(n_s))
    columns.start()
    columns.finish()


def first_exchange(weights, plan, cols, n_s, cid):
    return pl.pallas_call(
        functools.partial(first_kernel, n_s, plan),
        out_shape=jax.ShapeDtypeStruct((n_s, weights[0].shape[0], cols), bf16),
        in_specs=[ANY] * 3,
        out_specs=ANY,
        scratch_shapes=columns_sems(n_s),
        compiler_params=params(cid),
        cost_estimate=cost(20),
    )(*weights)


def second_kernel(n_w, n_s, chunks, plan, x, gw, uw, gain, x_all, slots, gains, own_sem, *sems):
    line = Line(n_s)
    gather = Gather(line, x, x_all, chunks, *sems[:4])
    columns = Columns(n_s, plan, (gw, uw), slots, False, *sems[4:7])
    share = Share(n_w, n_s, True, gain, gains, *sems[7:])
    greet(share.others())
    own = pltpu.make_async_copy(x, x_all.at[line.s], own_sem)
    for k in range(chunks):
        gather.start(k)
    own.start()
    share.start()
    columns.start()
    for d in range(1, line.nz):
        for k in range(chunks):
            gather.pass_on(d, k)
    gather.finish()
    own.wait()
    share.finish()
    columns.finish()


def second_exchange(x, weights, gain, plan, cols, n_w, n_s, cid, chunks=2):
    rows, width = x.shape
    count = n_w * n_s
    return pl.pallas_call(
        functools.partial(second_kernel, n_w, n_s, chunks, plan),
        out_shape=[
            jax.ShapeDtypeStruct((n_s, rows, width), bf16),
            jax.ShapeDtypeStruct((n_s, weights[0].shape[0], cols), bf16),
            jax.ShapeDtypeStruct((count, *gain.shape), gain.dtype),
        ],
        in_specs=[ANY] * 3 + [VM],
        out_specs=[ANY, ANY, VM],
        scratch_shapes=[DMA] + line_sems(n_s // 2, chunks) + columns_sems(n_s) + [DMA((count,)), DMA((count,)), DMA],
        compiler_params=params(cid),
        cost_estimate=cost(80),
    )(x, *weights, gain)


def back_kernel(n_s, plan, *refs):
    slots, arrays, sems = refs[0], refs[1 : 1 + len(plan)], refs[1 + len(plan) :]
    columns = Columns(n_s, plan, arrays, slots, True, *sems)
    greet(seq_others(n_s))
    columns.start()
    columns.finish()


def columns_back(slots, shapes, plan, n_s, cid):
    return pl.pallas_call(
        functools.partial(back_kernel, n_s, plan),
        out_shape=[jax.ShapeDtypeStruct(s, bf16) for s in shapes],
        in_specs=[ANY],
        out_specs=[ANY] * len(shapes),
        scratch_shapes=columns_sems(n_s),
        compiler_params=params(cid),
        cost_estimate=cost(40),
    )(slots)


def sums_kernel(n_w, n_s, back, x, given, all_x, made, *sems):
    share = Share(n_w, n_s, False, x, all_x, *sems[:3])
    halves = Halves(n_w, *((made, given) if back else (given, made)), back, *sems[3:])
    greet(share.others())
    share.start()
    halves.start()
    share.finish()
    halves.finish()


def sums_exchange(x, given, back, n_w, n_s, cid):
    rows, width = given.shape[-2:]
    made = (n_w, rows, width) if back else (n_w // 2, 2, rows, width)
    return pl.pallas_call(
        functools.partial(sums_kernel, n_w, n_s, back),
        out_shape=[jax.ShapeDtypeStruct((n_s, *x.shape), x.dtype), jax.ShapeDtypeStruct(made, bf16)],
        in_specs=[VM, VM],
        out_specs=[VM, VM],
        scratch_shapes=[DMA((n_s,)), DMA((n_s,)), DMA] + halves_sems(n_w),
        compiler_params=params(cid),
        cost_estimate=cost(10),
    )(x, given)


def final_kernel(n_w, n_s, plan, slots, terms, q, k, v, all_terms, *sems):
    columns = Columns(n_s, plan, (q, k, v), slots, True, *sems[:3])
    share = Share(n_w, n_s, True, terms, all_terms, *sems[3:])
    greet(share.others())
    share.start()
    columns.start()
    share.finish()
    columns.finish()


def final_exchange(slots, terms, width, plan, n_w, n_s, cid):
    mat = jax.ShapeDtypeStruct((slots.shape[1], width), bf16)
    return pl.pallas_call(
        functools.partial(final_kernel, n_w, n_s, plan),
        out_shape=[mat, mat, mat, jax.ShapeDtypeStruct(terms.shape, terms.dtype)],
        in_specs=[ANY, VM],
        out_specs=[ANY] * 3 + [VM],
        scratch_shapes=columns_sems(n_s) + [DMA((n_w * n_s,)), DMA((n_w * n_s,)), DMA],
        compiler_params=params(cid),
        cost_estimate=cost(20),
    )(slots, terms)


def dot(a, b):
    return jnp.dot(a, b, preferred_element_type=f32)


def dot_t(a, b):
    return lax.dot_general(a, b, (((1,), (1,)), ((), ())), preferred_element_type=f32)


def t_dot(a, b):
    return lax.dot_general(a, b, (((0,), (0,)), ((), ())), preferred_element_type=f32)


def turn(v, cosine, sine):
    return v * cosine + pltpu.roll(v, HEAD_DIM // 2, 1) * sine


def allowed_pairs(doc_q, doc_k, length):
    rows = lax.broadcasted_iota(jnp.int32, (length, length), 0)
    cols = lax.broadcasted_iota(jnp.int32, (length, length), 1)
    return (cols <= rows) & (doc_q == doc_k)


def attend_kernel(scale, ql, kl, vl, inv, gq, gk, cos, sin, doc_q, doc_k, att, q_out, k_out, v_out, lse):
    length = cos.shape[0]

    def flat(ref):
        return ref[...].reshape(length, -1)

    scales = flat(inv)
    q = turn(flat(ql) * scales[:, 0:1] * gq[...], cos[...], sin[...]).astype(bf16)
    k = turn(flat(kl) * scales[:, 1:2] * gk[...], cos[...], sin[...]).astype(bf16)
    v = flat(vl).astype(bf16)
    q_out[...] = q.reshape(q_out.shape)
    k_out[...] = k.reshape(k_out.shape)
    v_out[...] = v.reshape(v_out.shape)
    allowed = allowed_pairs(doc_q[0], doc_k[0], length)
    scores = jnp.where(allowed, dot_t(q, k) * scale, masked_value)
    top = jnp.max(scores, 1, keepdims=True)
    e = jnp.exp(scores - top)
    total = jnp.sum(e, 1, keepdims=True)
    probs = (e * (1.0 / total)).astype(bf16)
    att[...] = dot(probs, v).astype(bf16).reshape(att.shape)
    lse[...] = (top + jnp.log(total)).reshape(lse.shape)


def attend_back_kernel(scale, q, k, v, lse, da, cos, sin, doc_q, doc_k, dq_out, dk_out, dv_out):
    length = cos.shape[0]

    def flat(ref):
        return ref[...].reshape(length, -1)

    queries, keys, values, d_att = flat(q), flat(k), flat(v), flat(da)
    allowed = allowed_pairs(doc_q[0], doc_k[0], length)
    scores = jnp.where(allowed, dot_t(queries, keys) * scale, masked_value)
    probs = jnp.exp(scores - flat(lse))
    d_probs = dot_t(d_att, values)
    delta = jnp.sum(probs * d_probs, 1, keepdims=True)
    d_scores = (probs * (d_probs - delta)).astype(bf16)
    d_q = dot(d_scores, keys) * scale
    d_k = t_dot(d_scores, queries) * scale
    dv_out[...] = t_dot(probs.astype(bf16), d_att).astype(bf16).reshape(dv_out.shape)
    dq_out[...] = turn(d_q, cos[...], -sin[...]).reshape(dq_out.shape)
    dk_out[...] = turn(d_k, cos[...], -sin[...]).reshape(dk_out.shape)


def attention_specs(n_s, local, length):
    def tok(first):
        return pl.BlockSpec((n_s, 1, local, HEAD_DIM), lambda m, h: (0, m, 0, first + h))

    gain = pl.BlockSpec((1, HEAD_DIM), lambda m, h: (0, h))
    table = pl.BlockSpec((length, HEAD_DIM), lambda m, h: (0, 0))
    doc_q = pl.BlockSpec((1, length, 1), lambda m, h: (m, 0, 0))
    doc_k = pl.BlockSpec((1, 1, length), lambda m, h: (m, 0, 0))
    col = pl.BlockSpec((1, n_s, 1, local, 1), lambda m, h: (h, 0, m, 0, 0))
    return tok, gain, table, doc_q, doc_k, col


def attend(lin, inv, gains, tables, docs, heads, scale):
    n_s, micro, local, _ = lin.shape
    length = n_s * local
    tok, gain, table, doc_q, doc_k, col = attention_specs(n_s, local, length)
    inv_spec = pl.BlockSpec((n_s, 1, local, 2), lambda m, h: (0, m, 0, 0))
    out = jax.ShapeDtypeStruct((n_s, micro, local, heads * HEAD_DIM), bf16)
    return pl.pallas_call(
        functools.partial(attend_kernel, scale),
        grid=(micro, heads),
        out_shape=[out, out, out, out, jax.ShapeDtypeStruct((heads, n_s, micro, local, 1), f32)],
        in_specs=[tok(0), tok(heads), tok(2 * heads), inv_spec, gain, gain, table, table, doc_q, doc_k],
        out_specs=[tok(0)] * 4 + [col],
        compiler_params=pltpu.CompilerParams(vmem_limit_bytes=48 * 2**20),
    )(lin, lin, lin, inv, gains[0:1], gains[1:2], *tables, docs[:, :, None], docs[:, None, :])


def attend_back(q, k, v, lse, d_att, tables, docs, heads, scale):
    n_s, micro, local, width = q.shape
    length = n_s * local
    tok, gain, table, doc_q, doc_k, col = attention_specs(n_s, local, length)
    return pl.pallas_call(
        functools.partial(attend_back_kernel, scale),
        grid=(micro, heads),
        out_shape=[jax.ShapeDtypeStruct(q.shape, f32)] * 2 + [jax.ShapeDtypeStruct(q.shape, bf16)],
        in_specs=[tok(0)] * 3 + [col, tok(0), table, table, doc_q, doc_k],
        out_specs=[tok(0)] * 3,
        compiler_params=pltpu.CompilerParams(vmem_limit_bytes=48 * 2**20),
    )(q, k, v, lse, d_att, *tables, docs[:, :, None], docs[:, None, :])


def inverse_rms(values):
    return lax.rsqrt(jnp.mean(values * values, axis=-1, keepdims=True) + eps_norm)


def rotation_tables(positions):
    half_dim = HEAD_DIM // 2
    frequency = rope_base ** (-jnp.arange(half_dim, dtype=f32) * 2.0 / HEAD_DIM)
    angles = positions.astype(f32)[:, None] * frequency[None, :]
    cosine, sine = jnp.cos(angles), jnp.sin(angles)
    return jnp.concatenate([cosine, cosine], 1), jnp.concatenate([-sine, sine], 1)


def wide_gather(block):
    return lax.all_gather(block, "wide", axis=0, tiled=True)


def wide_scatter(partial):
    return lax.psum_scatter(partial.astype(bf16), "wide", scatter_dimension=0, tiled=True)


def after(value, *others):
    return lax.optimization_barrier((value, *others))[0]


def on_device(n_w, n_s, inputs, documents, cotangent, query_weight, key_weight, value_weight, output_weight,
              query_gain, key_gain, attention_gain, gate_weight, up_weight, down_weight, feed_gain):
    micro, _, local, width = inputs.shape
    tokens = micro * local
    all_tokens = n_s * tokens
    n_dev = n_w * n_s
    heads = HEADS // n_s
    cols = heads * HEAD_DIM
    row_len = documents.shape[2]
    feed = gate_weight.shape[1]
    feed_block = feed // n_dev
    half = n_w * feed_block
    rows = query_weight.shape[0]
    scale = HEAD_DIM ** (-0.5)
    s_index = lax.axis_index("seq")

    flat = inputs.reshape(tokens, width)
    cot = cotangent.reshape(tokens, width)
    halves = 2 * rows == HEAD_DIM and n_w == 2 * heads

    def head_of(s, i):
        return s // 2 + n_s // 2 * (lax.rem(s, 2) * heads + i) if halves else s * heads + i

    def head_column(i):
        return lambda s: head_of(s, i) * HEAD_DIM

    qkv_plan = [[(head_column(h), HEAD_DIM, i * cols + h * HEAD_DIM) for h in range(heads)] for i in range(3)]
    own_blocks = feed_block % 128 == 0
    moves = [(b, (b % n_w) * n_s + b // n_w) for b in range(n_dev)]
    back_moves = [(b, a) for a, b in moves]
    if own_blocks:
        feed_plan = [[(lambda s, a=a: (a * n_s + s) * feed_block, feed_block, i * half + a * feed_block) for a in range(n_w)] for i in range(2)]
    else:
        feed_plan = [[(lambda s: s * half, half, i * half)] for i in range(2)]

    own_gain = jnp.stack([query_gain, key_gain, attention_gain, feed_gain]).astype(f32)
    own_gain = jnp.pad(own_gain, ((0, 4), (0, 128 - rows)))
    qkv = first_exchange((query_weight, key_weight, value_weight), qkv_plan, 3 * cols, n_s, 0)
    qkv_all = wide_gather(qkv.reshape(n_s * rows, 3 * cols))
    if halves:
        out_halves = wide_gather(after(output_weight, qkv)).reshape(n_w, rows, width)
    else:
        out_all = wide_gather(lax.ppermute(output_weight, ("wide", "seq"), moves))
    x_all, gate_up, gains = second_exchange(after(flat, qkv), (gate_weight, up_weight), own_gain, feed_plan, 2 * half, n_w, n_s, 1)
    x_all = x_all.reshape(all_tokens, width)
    gate_up_all = wide_gather(gate_up.reshape(n_s * rows, 2 * half))
    down_block = after(down_weight, gate_up)
    if not own_blocks:
        down_block = lax.ppermute(down_block, ("wide", "seq"), moves)
    down_all = wide_gather(down_block)

    gains = jnp.swapaxes(gains[:, :4, :rows], 0, 1).reshape(4, width)

    def own_heads(v):
        return jnp.concatenate([lax.dynamic_slice_in_dim(v, head_of(s_index, i) * HEAD_DIM, HEAD_DIM, 1) for i in range(heads)], 1)

    own_gains = own_heads(gains)

    lin = dot(x_all, qkv_all)
    q_lin, k_lin = lin[:, :cols], lin[:, cols : 2 * cols]

    def stack_sums(a, b):
        return jnp.stack([a, b] + [jnp.zeros_like(a)] * 6)

    sums = stack_sums(jnp.sum(q_lin * q_lin, 1), jnp.sum(k_lin * k_lin, 1))
    if halves:
        sums, out_all = sums_exchange(sums, out_halves, False, n_w, n_s, 2)
        out_all = out_all.reshape(cols, width)
    else:
        sums = exchange(sums, n_w, n_s, False, 2)
    inv = lax.rsqrt(jnp.sum(sums, 0)[:2] / width + eps_norm).T
    tables = rotation_tables(jnp.arange(row_len, dtype=jnp.int32))
    docs = documents[:, 0, :]
    shape4 = (n_s, micro, local, -1)
    attended, q, k, v, lse = attend(lin.reshape(shape4), inv.reshape(shape4), own_gains, tables, docs, heads, scale)
    attended = attended.reshape(all_tokens, cols)

    own_f32 = ((tokens, width), f32)
    vec_f32 = ((1, width), f32)
    hidden_all, hidden, mixed_n, mixed_inv = around(
        dot(attended, out_all).astype(bf16), (flat, gains[2:3]), mixed_rows, [own_f32, own_f32, ((tokens, 1), f32)], n_s, 3, False
    )
    hidden_all = hidden_all.reshape(all_tokens, width)
    gate_up_lin = dot(hidden_all, gate_up_all)
    gate_lin, upward = gate_up_lin[:, :half], gate_up_lin[:, half:]
    sigma = jax.nn.sigmoid(gate_lin)
    silu_gate = gate_lin * sigma
    active = (silu_gate * upward).astype(bf16)
    d_down_all, layer_out, feed_term = around(
        dot(active, down_all).astype(bf16), (hidden, cot, gains[3:4]), down_rows, [((tokens, width), bf16), vec_f32], n_s, 4, True
    )
    d_down_all = d_down_all.reshape(all_tokens, width)
    down_part = t_dot(active, d_down_all).astype(bf16)
    down_grad = wide_scatter(down_part)
    d_active = dot_t(after(d_down_all, down_part), down_all)
    d_gate = (d_active * upward * sigma * (1.0 + gate_lin * (1.0 - sigma))).astype(bf16)
    d_up = (d_active * silu_gate).astype(bf16)
    d_gate_up = jnp.concatenate([d_gate, d_up], axis=1)
    mlp_part = t_dot(hidden_all, d_gate_up).astype(bf16)
    mlp_grad = wide_scatter(mlp_part)
    d_mixed_all, d_hidden, attention_term = around(
        dot_t(after(d_gate_up, mlp_part), gate_up_all).astype(bf16), (cot, mixed_n, mixed_inv, gains[2:3]), hidden_rows, [own_f32, vec_f32], n_s, 5, True
    )
    d_mixed_all = d_mixed_all.reshape(all_tokens, width)
    out_part = t_dot(attended, d_mixed_all).astype(bf16)
    d_attended = dot_t(d_mixed_all, out_all).astype(bf16).reshape(shape4)

    d_q, d_k, d_v = attend_back(q, k, v, lse, d_attended, tables, docs, heads, scale)
    d_q, d_k, d_v = (t.reshape(all_tokens, cols) for t in (d_q, d_k, d_v))
    q_n, k_n = q_lin * inv[:, 0:1], k_lin * inv[:, 1:2]
    d_qg, d_kg = d_q * own_gains[0], d_k * own_gains[1]
    mean_sums = stack_sums(jnp.sum(d_qg * q_n, 1), jnp.sum(d_kg * k_n, 1))
    if halves:
        mean_sums, out_part = sums_exchange(mean_sums, out_part.reshape(heads, 2, rows, width), True, n_w, n_s, 6)
    else:
        mean_sums = exchange(mean_sums, n_w, n_s, False, 6)
    means = jnp.sum(mean_sums, 0)[:2].T / width
    query_term = jnp.sum(d_q * q_n, 0)
    key_term = jnp.sum(d_k * k_n, 0)
    d_q_lin = (inv[:, 0:1] * (d_qg - q_n * means[:, 0:1])).astype(bf16)
    d_k_lin = (inv[:, 1:2] * (d_kg - k_n * means[:, 1:2])).astype(bf16)
    d_lin = jnp.concatenate([d_q_lin, d_k_lin, d_v], axis=1)
    qkv_part = t_dot(x_all, d_lin).astype(bf16)
    mlp_grad, down_grad, qkv_part, out_part = lax.optimization_barrier((mlp_grad, down_grad, qkv_part, out_part))
    input_grad = last_sum(dot_t(after(d_lin, qkv_part), qkv_all).astype(bf16), d_hidden, n_s, 7).reshape(inputs.shape)
    qkv_grad = wide_scatter(qkv_part)
    out_grad = wide_scatter(out_part.reshape(cols, width))
    if not halves:
        out_grad = lax.ppermute(out_grad, ("wide", "seq"), back_moves)

    gate_grad, up_grad = columns_back(
        after(mlp_grad, input_grad).reshape(n_s, rows, 2 * half), [(rows, feed)] * 2, feed_plan, n_s, 8
    )
    def spread(term):
        full = jnp.zeros((width,), f32)
        for i in range(heads):
            full = lax.dynamic_update_slice_in_dim(full, term[i * HEAD_DIM : (i + 1) * HEAD_DIM], head_of(s_index, i) * HEAD_DIM, 0)
        return full

    terms = jnp.stack([spread(query_term), spread(key_term), attention_term[0], feed_term[0]])
    terms = jnp.swapaxes(terms.reshape(4, n_dev, rows), 0, 1)
    terms = jnp.pad(terms, ((0, 0), (0, 4), (0, 128 - rows)))
    query_grad, key_grad, value_grad, all_terms = final_exchange(
        after(qkv_grad, gate_grad).reshape(n_s, rows, 3 * cols), terms, width, qkv_plan, n_w, n_s, 9
    )
    gain_grads = jnp.sum(all_terms, 0)[:4, :rows]
    if not own_blocks:
        down_grad = lax.ppermute(down_grad, ("wide", "seq"), back_moves)
    return (layer_out.reshape(inputs.shape), input_grad, *(g.astype(f32) for g in (query_grad, key_grad, value_grad, out_grad)),
            gain_grads[0], gain_grads[1], gain_grads[2], gate_grad.astype(f32), up_grad.astype(f32), down_grad.astype(f32), gain_grads[3])


def solution(mesh):
    tok = P(None, "wide", "seq", None)
    docs = P(None, "wide", None)
    mat = P(("wide", "seq"), None)
    vec = P(("wide", "seq"))

    def body(*args):
        return on_device(mesh.shape["wide"], mesh.shape["seq"], *args)

    return jax.shard_map(
        body,
        mesh=mesh,
        in_specs=(tok, docs, tok, mat, mat, mat, mat, vec, vec, vec, mat, mat, mat, vec),
        out_specs=(tok, tok, mat, mat, mat, mat, vec, vec, vec, mat, mat, mat, vec),
        check_vma=False,
    )
```

```python
import functools

import jax
import jax.numpy as jnp
from jax import lax
from jax.experimental import pallas as pl
from jax.experimental.pallas import tpu as pltpu
from jax.sharding import PartitionSpec as P

HEADS = 16
HEAD_DIM = 128
eps_norm = 1e-06
rope_base = 500000.0
masked_value = -1e30
bf16 = jnp.bfloat16
f32 = jnp.float32
MESH = pl.DeviceIdType.MESH
ANY = pl.BlockSpec(memory_space=pl.ANY)
VM = pl.BlockSpec(memory_space=pltpu.VMEM)
DMA = pltpu.SemaphoreType.DMA
PACE = 1
CHUNKS = 4
SUB = 4


def params(cid, megabytes=None):
    limit = {} if megabytes is None else {"vmem_limit_bytes": megabytes * 2**20}
    return pltpu.CompilerParams(collective_id=cid, has_side_effects=True, **limit)


def cost(microseconds):
    return pl.CostEstimate(flops=0, transcendentals=0, bytes_accessed=int(microseconds * 3e6))


def far_first(n_s):
    return sorted(range(n_s), key=lambda k: -min(k, n_s - k))


def remote(src, dst, send, recv, device):
    return pltpu.make_async_remote_copy(src, dst, send, recv, device_id=device, device_id_type=MESH)


def greet(targets):
    barrier = pltpu.get_barrier_semaphore()
    count = 0
    for cond, dev in targets:
        if cond is None:
            pl.semaphore_signal(barrier, inc=1, device_id=dev, device_id_type=MESH)
            count = count + 1
        else:

            @pl.when(cond)
            def _():
                pl.semaphore_signal(barrier, inc=1, device_id=dev, device_id_type=MESH)

            count = count + cond.astype(jnp.int32)
    pl.semaphore_wait(barrier, count)


class Line:
    def __init__(self, n_s):
        self.s = lax.axis_index("seq")
        self.nz = n_s // 2
        self.z, self.c = self.s // 2, self.s % 2
        self.mate_slot = self.s + 1 - 2 * self.c
        self.mate = {"seq": self.mate_slot}
        self.steps = (1, -1)
        self.more = (self.z < self.nz - 1, self.z > 0)
        self.next = ({"seq": self.s + 2}, {"seq": self.s - 2})

    def neighbours(self):
        return [(self.more[0], self.next[0]), (self.more[1], self.next[1]), (None, self.mate)]


class Gather:
    def __init__(self, line, own, out, chunks, send, recv, mate_send, mate_recv):
        self.line, self.own, self.out = line, own, out
        self.chunks, self.rows = chunks, own.shape[0] // chunks
        self.send, self.recv, self.mate_send, self.mate_recv = send, recv, mate_send, mate_recv

    def part(self, slot, k):
        return self.out.at[slot, pl.ds(k * self.rows, self.rows)]

    def source(self, d, k, slot):
        return self.own.at[pl.ds(k * self.rows, self.rows)] if d == 0 else self.part(slot, k)

    def hop(self, i, d, k, slot):
        return remote(self.source(d, k, slot), self.part(slot, k), self.send.at[i, d, k], self.recv.at[i, d, k], self.line.next[i])

    def share(self, i, d, k, slot):
        return remote(self.source(d, k, slot), self.part(slot, k), self.mate_send.at[i, d, k], self.mate_recv.at[i, d, k], self.line.mate)

    def start(self, k):
        line = self.line
        for i in range(2):

            @pl.when(line.more[i])
            def _():
                self.hop(i, 0, k, line.s).start()

        self.share(0, 0, k, line.s).start()

    def each(self, d, mine=True):
        line = self.line
        for i in range(2):
            origin = line.z - line.steps[i] * d
            yield i, (origin >= 0) & (origin < line.nz), 2 * origin + (line.c if mine else 1 - line.c)

    def pass_on(self, d, k):
        for i, there, slot in self.each(d):

            @pl.when(there)
            def _():
                self.hop(i, d - 1, k, slot).wait_recv()
                if d < self.line.nz - 1:

                    @pl.when(self.line.more[i])
                    def _():
                        self.hop(i, d, k, slot).start()

                self.share(i, d, k, slot).start()

    def finish(self):
        line = self.line
        for k in range(self.chunks):
            self.share(0, 0, k, line.mate_slot).wait_recv()
            for d in range(1, line.nz):
                for i, there, slot in self.each(d, False):

                    @pl.when(there)
                    def _():
                        self.share(i, d, k, slot).wait_recv()

        for k in range(self.chunks):
            self.share(0, 0, k, line.s).wait_send()
            for i in range(2):

                @pl.when(line.more[i])
                def _():
                    self.hop(i, 0, k, line.s).wait_send()

            for d in range(1, line.nz):
                for i, there, slot in self.each(d):

                    @pl.when(there)
                    def _():
                        self.share(i, d, k, slot).wait_send()
                        if d < line.nz - 1:

                            @pl.when(line.more[i])
                            def _():
                                self.hop(i, d, k, slot).wait_send()


class Scatter:
    def __init__(self, line, part, from_mate, run, chunks, send, recv, mate_send, mate_recv):
        self.line, self.part, self.from_mate, self.run = line, part, from_mate, run
        self.chunks, self.rows = chunks, part.shape[1] // chunks
        self.send, self.recv, self.mate_send, self.mate_recv = send, recv, mate_send, mate_recv
        self.steps = line.nz - 1
        self.groups = chunks // SUB
        self.count = self.steps * self.groups

    def span(self, k):
        return pl.ds(pl.multiple_of(k * self.rows, self.rows), self.rows)

    def give(self, zd, k):
        line, rs = self.line, self.span(k)
        return remote(self.part.at[2 * zd + 1 - line.c, rs], self.from_mate.at[zd, rs], self.mate_send.at[zd, k], self.mate_recv.at[zd, k], line.mate)

    def hop(self, i, zd, k):
        ref = self.run.at[i, zd, self.span(k)]
        return remote(ref, ref, self.send.at[i, zd, k], self.recv.at[i, zd, k], self.line.next[i])

    def pair(self, zd, k):
        rs = self.span(k)
        return self.part[2 * zd + self.line.c, rs].astype(f32) + self.from_mate[zd, rs].astype(f32)

    def start(self, k):
        nz = self.line.nz
        for zd in sorted(range(nz), key=lambda zd: (min(zd, nz - 1 - zd), -zd)):
            self.give(zd, k).start()

    def item(self, i, q, j):
        group, step = q // self.steps, lax.rem(q, self.steps)
        return (self.line.nz - 1 - step if i == 0 else step), group * SUB + j

    def slot(self, t):
        line = self.line
        for j, i in ((j, i) for j in range(SUB) for i in range(2)):
            q = t - (line.z if i == 0 else line.nz - 1 - line.z)
            behind = line.z > 0 if i == 0 else line.z < line.nz - 1
            zd, k = self.item(i, jnp.clip(q, 0, self.count - 1), j)
            going = (q >= 0) & (q < self.count) & (line.z < zd if i == 0 else line.z > zd)

            @pl.when(going)
            def _():
                rs = self.span(k)
                self.give(zd, k).wait_recv()

                @pl.when(behind)
                def _():
                    self.hop(i, zd, k).wait_recv()
                    self.run[i, zd, rs] = (self.pair(zd, k) + self.run[i, zd, rs].astype(f32)).astype(bf16)

                @pl.when(jnp.logical_not(behind))
                def _():
                    self.run[i, zd, rs] = self.pair(zd, k).astype(bf16)
                    if t >= PACE:
                        self.hop(i, *self.item(i, jnp.int32(t - PACE), j)).wait_send()

                self.hop(i, zd, k).start()

    def total(self, k, use):
        line, rs = self.line, self.span(k)
        for zd in range(line.nz):

            @pl.when(line.z == zd)
            def _():
                self.give(zd, k).wait_recv()
                total = self.pair(zd, k)
                if zd > 0:
                    self.hop(0, zd, k).wait_recv()
                    total = total + self.run[0, zd, rs].astype(f32)
                if zd < line.nz - 1:
                    self.hop(1, zd, k).wait_recv()
                    total = total + self.run[1, zd, rs].astype(f32)
                use(total)

    def finish(self):
        line = self.line
        for k in range(self.chunks):
            for zd in range(line.nz):
                self.give(zd, k).wait_send()
        for q in range(self.count):
            step = q % self.steps
            for i, zd in ((0, line.nz - 1 - step), (1, step)):
                going = line.z < zd if i == 0 else line.z > zd
                behind = line.z > 0 if i == 0 else line.z < line.nz - 1

                @pl.when(going & behind if q < self.count - PACE else going)
                def _():
                    for j in range(SUB):
                        self.hop(i, zd, q // self.steps * SUB + j).wait_send()


def line_sems(nz, chunks):
    return [DMA((2, nz, chunks))] * 4


def scatter_scratch(n_s, rows, width, chunks):
    nz = n_s // 2
    sums = [pltpu.VMEM((nz, rows, width), bf16), pltpu.VMEM((2, nz, rows, width), bf16)]
    return sums + [DMA((2, nz, chunks))] * 2 + [DMA((nz, chunks))] * 2


def mixed_rows(rs, total, x, gain, hidden, normed, inverse, low):
    inv = inverse_rms(total)
    n = total * inv
    out = x[rs].astype(f32) + n * gain[...]
    hidden[rs] = out
    normed[rs] = n
    inverse[rs] = inv
    low[rs] = out.astype(bf16)


def down_rows(rs, total, hidden, cotangent, gain, out, term, low):
    inv = inverse_rms(total)
    n = total * inv
    g = gain[...]
    out[rs] = (hidden[rs] + n * g).astype(bf16)
    grad = cotangent[rs].astype(f32)
    low[rs], more = back_rows(grad, n, inv, g)
    term[...] += more


def hidden_rows(rs, total, cotangent, normed, inverse, gain, d_hidden, term, low):
    grad = cotangent[rs].astype(f32) + total
    d_hidden[rs] = grad
    low[rs], more = back_rows(grad, normed[rs], inverse[rs], gain[...])
    term[...] += more


def back_rows(grad, n, inv, gain):
    scaled = grad * gain
    d = inv * (scaled - n * jnp.mean(scaled * n, axis=-1, keepdims=True))
    return d.astype(bf16), jnp.sum(grad * n, axis=0, keepdims=True)


def run_slots(scatter, use, gather=None, work=None):
    steps, groups = scatter.steps, scatter.groups
    slots = steps * (groups + (1 if gather else 0)) + 1
    for t in range(slots):
        if t < steps * (groups + 1):
            scatter.slot(t)
        if gather:
            for group in range(groups):
                if 1 <= t - steps * (group + 1) <= steps:
                    for j in range(SUB):
                        gather.pass_on(t - steps * (group + 1), group * SUB + j)
        if t and t % steps == 0 and t // steps <= groups:
            for k in range((t // steps - 1) * SUB, t // steps * SUB):
                scatter.total(k, lambda total: use(k, total))
                if gather:
                    gather.start(k)
        if work:
            work(t, slots)


def product_work(left, right, out):
    size = 128
    count = out.shape[0] // size

    def work(t, slots):
        for i in range(count * t // slots, count * (t + 1) // slots):
            rs = pl.ds(i * size, size)
            out[rs] = lax.dot_general(left[:, rs], right[...], (((0,), (0,)), ((), ())), preferred_element_type=f32).astype(bf16)

    return work


def around_kernel(n_s, chunks, rows_fn, n_in, n_out, adds, with_work, *refs):
    part, extra = refs[0], refs[1 : 1 + n_in]
    refs = refs[1 + n_in :]
    work = None
    if with_work:
        left, right, gathered, *outs, made = refs[: 4 + n_out]
        work = product_work(left, right, made)
        refs = refs[4 + n_out :]
    else:
        gathered, *outs = refs[: 1 + n_out]
        refs = refs[1 + n_out :]
    low, local, from_mate, run, *sems = refs
    line = Line(n_s)
    scatter = Scatter(line, part, from_mate, run, chunks, *sems[:4])
    gather = Gather(line, low, gathered, chunks, *sems[4:])
    greet(line.neighbours())
    for k in range(chunks):
        scatter.start(k)
    if adds:
        outs[-1][...] = jnp.zeros_like(outs[-1])
    run_slots(scatter, lambda k, total: rows_fn(scatter.span(k), total, *extra, *outs, low), gather, work)
    own = pltpu.make_async_copy(low, gathered.at[line.s], local)
    own.start()
    gather.finish()
    scatter.finish()
    own.wait()


def around(terms, extra, rows_fn, outs, n_s, cid, adds, pair=(), chunks=CHUNKS):
    rows, width = terms.shape[0] // n_s, terms.shape[1]
    shapes = [((n_s, rows, width), bf16), *outs] + ([((pair[0].shape[1], pair[1].shape[1]), bf16)] if pair else [])
    return pl.pallas_call(
        functools.partial(around_kernel, n_s, chunks, rows_fn, len(extra), len(outs), adds, bool(pair)),
        out_shape=[jax.ShapeDtypeStruct(*o) for o in shapes],
        in_specs=[VM] * (1 + len(extra) + len(pair)),
        out_specs=[ANY] + [VM] * (len(shapes) - 1),
        scratch_shapes=[pltpu.VMEM((rows, width), bf16), DMA] + scatter_scratch(n_s, rows, width, chunks) + line_sems(n_s // 2, chunks),
        compiler_params=params(cid, 48),
        cost_estimate=cost(70),
    )(terms.reshape(n_s, rows, width), *extra, *pair)


def last_kernel(n_s, chunks, part, d_hidden, out, from_mate, run, *sems):
    line = Line(n_s)
    scatter = Scatter(line, part, from_mate, run, chunks, *sems)
    greet(line.neighbours())
    for k in range(chunks):
        scatter.start(k)

    def use(k, total):
        out[scatter.span(k)] = d_hidden[scatter.span(k)] + total

    run_slots(scatter, use)
    scatter.finish()


def last_sum(terms, d_hidden, n_s, cid, chunks=CHUNKS):
    rows, width = terms.shape[0] // n_s, terms.shape[1]
    return pl.pallas_call(
        functools.partial(last_kernel, n_s, chunks),
        out_shape=jax.ShapeDtypeStruct((rows, width), f32),
        in_specs=[VM, VM],
        out_specs=VM,
        scratch_shapes=scatter_scratch(n_s, rows, width, chunks),
        compiler_params=params(cid, 48),
        cost_estimate=cost(40),
    )(terms.reshape(n_s, rows, width), d_hidden)


class Columns:
    def __init__(self, n_s, plan, arrays, slots, back, send, recv, local):
        self.n_s, self.plan, self.arrays, self.slots, self.back = n_s, plan, arrays, slots, back
        self.send, self.recv, self.local = send, recv, local
        self.s = lax.axis_index("seq")

    def place(self, k):
        return lax.rem(self.s + k, self.n_s)

    def pieces(self, k):
        there = self.place(k)
        for array, parts in zip(self.arrays, self.plan):
            for first, width, column in parts:
                at = pl.ds(column, width)
                if self.back:
                    yield self.slots.at[there, :, at], array.at[:, pl.ds(pl.multiple_of(first(self.s), 128), width)]
                else:
                    yield array.at[:, pl.ds(pl.multiple_of(first(there), 128), width)], self.slots.at[self.s, :, at]

    def start(self):
        for k in far_first(self.n_s)[:-1]:
            for src, dst in self.pieces(k):
                remote(src, dst, self.send.at[k], self.recv.at[k], {"seq": self.place(k)}).start()
        for src, dst in self.pieces(0):
            pltpu.make_async_copy(src, dst, self.local).start()

    def finish(self):
        slot = self.slots.at[0]
        for k in range(1, self.n_s):
            done = remote(slot, slot, self.send.at[k], self.recv.at[k], {"seq": self.place(k)})
            done.wait_recv()
            done.wait_send()
        pltpu.make_async_copy(slot, slot, self.local).wait()


def columns_sems(n_s):
    return [DMA((n_s,)), DMA((n_s,)), DMA]


def seq_others(n_s):
    s = lax.axis_index("seq")
    return [(None, {"seq": lax.rem(s + k, n_s)}) for k in range(1, n_s)]


class Share:
    def __init__(self, n_w, n_s, whole, x, out, send, recv, local):
        self.n_w, self.n_s, self.whole = n_w, n_s, whole
        self.x, self.out, self.send, self.recv, self.local = x, out, send, recv, local
        self.w, self.s = lax.axis_index("wide"), lax.axis_index("seq")
        self.steps = [(a, b) for b in far_first(n_s) for a in (range(n_w) if whole else (0,)) if a or b]

    def at(self, a, b):
        return lax.rem(self.w + a, self.n_w), lax.rem(self.s + b, self.n_s)

    def number(self, a, b):
        w, s = self.at(a, b)
        return w * self.n_s + s if self.whole else s

    def name(self, a, b):
        w, s = self.at(a, b)
        return {"wide": w, "seq": s}

    def others(self):
        return [(None, self.name(a, b)) for a, b in self.steps]

    def block(self, a, b):
        return self.x.at[self.number(a, b)] if len(self.x.shape) == 3 else self.x

    def copy(self, a, b):
        i = a * self.n_s + b
        return remote(self.block(a, b), self.out.at[self.number(0, 0)], self.send.at[i], self.recv.at[i], self.name(a, b))

    def own(self):
        return pltpu.make_async_copy(self.block(0, 0), self.out.at[self.number(0, 0)], self.local)

    def start(self):
        for a, b in self.steps:
            self.copy(a, b).start()
        self.own().start()

    def finish(self):
        for a, b in self.steps:
            self.copy(a, b).wait()
        self.own().wait()


def share_kernel(n_w, n_s, whole, x_ref, o_ref, send, recv, local_sem):
    share = Share(n_w, n_s, whole, x_ref, o_ref, send, recv, local_sem)
    greet(share.others())
    share.start()
    share.finish()


def exchange(x, n_w, n_s, whole, cid):
    count = n_w * n_s if whole else n_s
    return pl.pallas_call(
        functools.partial(share_kernel, n_w, n_s, whole),
        out_shape=jax.ShapeDtypeStruct((count, *x.shape[-2:]), x.dtype),
        in_specs=[VM],
        out_specs=VM,
        scratch_shapes=[DMA((count,)), DMA((count,)), DMA],
        compiler_params=params(cid),
        cost_estimate=cost(10),
    )(x)


class Halves:
    def __init__(self, n_w, natural, heads, back, send, recv, local):
        s = lax.axis_index("seq")
        c = lax.rem(s, 2)
        self.back, self.count = back, n_w // 2
        self.send, self.recv, self.local = send, recv, local
        mate = {"seq": s + 1 - 2 * c}
        self.away, self.stay = [], []
        for i in range(self.count):
            mine, his = c * self.count + i, (1 - c) * self.count + i
            if back:
                pair = heads.at[i, 1 - c], natural.at[mine]
                own = heads.at[i, c], natural.at[mine]
            else:
                pair = natural.at[his], heads.at[i, c]
                own = natural.at[mine], heads.at[i, c]
            self.away.append(remote(*pair, send.at[i], recv.at[i], mate))
            self.stay.append(pltpu.make_async_copy(*own, local.at[i]))

    def start(self):
        for copy in self.away + self.stay:
            copy.start()

    def finish(self):
        for copy in self.away + self.stay:
            copy.wait()


def halves_sems(n_w):
    return [DMA((n_w // 2,))] * 3


def first_kernel(n_s, plan, qw, kw, vw, qkv, *sems):
    columns = Columns(n_s, plan, (qw, kw, vw), qkv, False, *sems)
    greet(seq_others(n_s))
    columns.start()
    columns.finish()


def first_exchange(weights, plan, cols, n_s, cid):
    return pl.pallas_call(
        functools.partial(first_kernel, n_s, plan),
        out_shape=jax.ShapeDtypeStruct((n_s, weights[0].shape[0], cols), bf16),
        in_specs=[ANY] * 3,
        out_specs=ANY,
        scratch_shapes=columns_sems(n_s),
        compiler_params=params(cid),
        cost_estimate=cost(20),
    )(*weights)


def second_kernel(n_w, n_s, chunks, plan, x, gw, uw, gain, x_all, slots, gains, own_sem, *sems):
    line = Line(n_s)
    gather = Gather(line, x, x_all, chunks, *sems[:4])
    columns = Columns(n_s, plan, (gw, uw), slots, False, *sems[4:7])
    share = Share(n_w, n_s, True, gain, gains, *sems[7:])
    greet(share.others())
    own = pltpu.make_async_copy(x, x_all.at[line.s], own_sem)
    for k in range(chunks):
        gather.start(k)
    own.start()
    share.start()
    columns.start()
    for d in range(1, line.nz):
        for k in range(chunks):
            gather.pass_on(d, k)
    gather.finish()
    own.wait()
    share.finish()
    columns.finish()


def second_exchange(x, weights, gain, plan, cols, n_w, n_s, cid, chunks=2):
    rows, width = x.shape
    count = n_w * n_s
    return pl.pallas_call(
        functools.partial(second_kernel, n_w, n_s, chunks, plan),
        out_shape=[
            jax.ShapeDtypeStruct((n_s, rows, width), bf16),
            jax.ShapeDtypeStruct((n_s, weights[0].shape[0], cols), bf16),
            jax.ShapeDtypeStruct((count, *gain.shape), gain.dtype),
        ],
        in_specs=[ANY] * 3 + [VM],
        out_specs=[ANY, ANY, VM],
        scratch_shapes=[DMA] + line_sems(n_s // 2, chunks) + columns_sems(n_s) + [DMA((count,)), DMA((count,)), DMA],
        compiler_params=params(cid),
        cost_estimate=cost(80),
    )(x, *weights, gain)


def unpack_kernel(n_s, plan, slots, *outs):
    for out, pieces in zip(outs, plan):
        for first, width, column in pieces:
            for s in range(n_s):
                out[:, first(s) : first(s) + width] = slots[s, :, column : column + width].astype(f32)


def unpack(slots, width, plan):
    n_s, rows, _ = slots.shape
    return pl.pallas_call(
        functools.partial(unpack_kernel, n_s, plan),
        out_shape=[jax.ShapeDtypeStruct((rows, width), f32)] * len(plan),
        in_specs=[VM],
        out_specs=[VM] * len(plan),
        compiler_params=pltpu.CompilerParams(vmem_limit_bytes=40 * 2**20),
        cost_estimate=cost(4),
    )(slots)


def sums_kernel(n_w, n_s, back, x, given, all_x, made, *sems):
    share = Share(n_w, n_s, False, x, all_x, *sems[:3])
    halves = Halves(n_w, *((made, given) if back else (given, made)), back, *sems[3:])
    greet(share.others())
    share.start()
    halves.start()
    share.finish()
    halves.finish()


def sums_exchange(x, given, back, n_w, n_s, cid):
    rows, width = given.shape[-2:]
    made = (n_w, rows, width) if back else (n_w // 2, 2, rows, width)
    return pl.pallas_call(
        functools.partial(sums_kernel, n_w, n_s, back),
        out_shape=[jax.ShapeDtypeStruct((n_s, *x.shape), x.dtype), jax.ShapeDtypeStruct(made, bf16)],
        in_specs=[VM, VM],
        out_specs=[VM, VM],
        scratch_shapes=[DMA((n_s,)), DMA((n_s,)), DMA] + halves_sems(n_w),
        compiler_params=params(cid),
        cost_estimate=cost(10),
    )(x, given)


def final_kernel(n_w, n_s, qkv, terms, qkv_own, all_terms, *sems):
    shares = [Share(n_w, n_s, True, terms, all_terms, *sems[:3]), Share(n_w, n_s, False, qkv, qkv_own, *sems[3:])]
    greet(shares[0].others())
    for share in shares:
        share.start()
    for share in shares:
        share.finish()


def final_exchange(qkv, terms, n_w, n_s, cid):
    return pl.pallas_call(
        functools.partial(final_kernel, n_w, n_s),
        out_shape=[jax.ShapeDtypeStruct(v.shape, v.dtype) for v in (qkv, terms)],
        in_specs=[ANY, VM],
        out_specs=[ANY, VM],
        scratch_shapes=[DMA((n_w * n_s,)), DMA((n_w * n_s,)), DMA, DMA((n_s,)), DMA((n_s,)), DMA],
        compiler_params=params(cid),
        cost_estimate=cost(20),
    )(qkv, terms)


def dot(a, b):
    return jnp.dot(a, b, preferred_element_type=f32)


def dot_t(a, b):
    return lax.dot_general(a, b, (((1,), (1,)), ((), ())), preferred_element_type=f32)


def t_dot(a, b):
    return lax.dot_general(a, b, (((0,), (0,)), ((), ())), preferred_element_type=f32)


def turn(v, cosine, sine):
    return v * cosine + pltpu.roll(v, HEAD_DIM // 2, 1) * sine


def allowed_pairs(doc_q, doc_k, length):
    rows = lax.broadcasted_iota(jnp.int32, (length, length), 0)
    cols = lax.broadcasted_iota(jnp.int32, (length, length), 1)
    return (cols <= rows) & (doc_q == doc_k)


def attend_kernel(scale, ql, kl, vl, inv, gq, gk, cos, sin, doc_q, doc_k, att, q_out, k_out, v_out, lse):
    length = cos.shape[0]

    def flat(ref):
        return ref[...].reshape(length, -1)

    scales = flat(inv)
    q = turn(flat(ql) * scales[:, 0:1] * gq[...], cos[...], sin[...]).astype(bf16)
    k = turn(flat(kl) * scales[:, 1:2] * gk[...], cos[...], sin[...]).astype(bf16)
    v = flat(vl).astype(bf16)
    q_out[...] = q.reshape(q_out.shape)
    k_out[...] = k.reshape(k_out.shape)
    v_out[...] = v.reshape(v_out.shape)
    allowed = allowed_pairs(doc_q[0], doc_k[0], length)
    scores = jnp.where(allowed, dot_t(q, k) * scale, masked_value)
    top = jnp.max(scores, 1, keepdims=True)
    e = jnp.exp(scores - top)
    total = jnp.sum(e, 1, keepdims=True)
    probs = (e * (1.0 / total)).astype(bf16)
    att[...] = dot(probs, v).astype(bf16).reshape(att.shape)
    lse[...] = (top + jnp.log(total)).reshape(lse.shape)


def attend_back_kernel(scale, q, k, v, lse, da, cos, sin, doc_q, doc_k, dq_out, dk_out, dv_out):
    length = cos.shape[0]

    def flat(ref):
        return ref[...].reshape(length, -1)

    queries, keys, values, d_att = flat(q), flat(k), flat(v), flat(da)
    allowed = allowed_pairs(doc_q[0], doc_k[0], length)
    scores = jnp.where(allowed, dot_t(queries, keys) * scale, masked_value)
    probs = jnp.exp(scores - flat(lse))
    d_probs = dot_t(d_att, values)
    delta = jnp.sum(probs * d_probs, 1, keepdims=True)
    d_scores = (probs * (d_probs - delta)).astype(bf16)
    d_q = dot(d_scores, keys) * scale
    d_k = t_dot(d_scores, queries) * scale
    dv_out[...] = t_dot(probs.astype(bf16), d_att).astype(bf16).reshape(dv_out.shape)
    dq_out[...] = turn(d_q, cos[...], -sin[...]).reshape(dq_out.shape)
    dk_out[...] = turn(d_k, cos[...], -sin[...]).reshape(dk_out.shape)


def attention_specs(n_s, local, length):
    def tok(first):
        return pl.BlockSpec((n_s, 1, local, HEAD_DIM), lambda m, h: (0, m, 0, first + h))

    gain = pl.BlockSpec((1, HEAD_DIM), lambda m, h: (0, h))
    table = pl.BlockSpec((length, HEAD_DIM), lambda m, h: (0, 0))
    doc_q = pl.BlockSpec((1, length, 1), lambda m, h: (m, 0, 0))
    doc_k = pl.BlockSpec((1, 1, length), lambda m, h: (m, 0, 0))
    col = pl.BlockSpec((1, n_s, 1, local, 1), lambda m, h: (h, 0, m, 0, 0))
    return tok, gain, table, doc_q, doc_k, col


def attend(lin, inv, gains, tables, docs, heads, scale):
    n_s, micro, local, _ = lin.shape
    length = n_s * local
    tok, gain, table, doc_q, doc_k, col = attention_specs(n_s, local, length)
    inv_spec = pl.BlockSpec((n_s, 1, local, 2), lambda m, h: (0, m, 0, 0))
    out = jax.ShapeDtypeStruct((n_s, micro, local, heads * HEAD_DIM), bf16)
    return pl.pallas_call(
        functools.partial(attend_kernel, scale),
        grid=(micro, heads),
        out_shape=[out, out, out, out, jax.ShapeDtypeStruct((heads, n_s, micro, local, 1), f32)],
        in_specs=[tok(0), tok(heads), tok(2 * heads), inv_spec, gain, gain, table, table, doc_q, doc_k],
        out_specs=[tok(0)] * 4 + [col],
        compiler_params=pltpu.CompilerParams(vmem_limit_bytes=48 * 2**20),
    )(lin, lin, lin, inv, gains[0:1], gains[1:2], *tables, docs[:, :, None], docs[:, None, :])


def attend_back(q, k, v, lse, d_att, tables, docs, heads, scale):
    n_s, micro, local, width = q.shape
    length = n_s * local
    tok, gain, table, doc_q, doc_k, col = attention_specs(n_s, local, length)
    return pl.pallas_call(
        functools.partial(attend_back_kernel, scale),
        grid=(micro, heads),
        out_shape=[jax.ShapeDtypeStruct(q.shape, f32)] * 2 + [jax.ShapeDtypeStruct(q.shape, bf16)],
        in_specs=[tok(0)] * 3 + [col, tok(0), table, table, doc_q, doc_k],
        out_specs=[tok(0)] * 3,
        compiler_params=pltpu.CompilerParams(vmem_limit_bytes=48 * 2**20),
    )(q, k, v, lse, d_att, *tables, docs[:, :, None], docs[:, None, :])


def inverse_rms(values):
    return lax.rsqrt(jnp.mean(values * values, axis=-1, keepdims=True) + eps_norm)


def rotation_tables(positions):
    half_dim = HEAD_DIM // 2
    frequency = rope_base ** (-jnp.arange(half_dim, dtype=f32) * 2.0 / HEAD_DIM)
    angles = positions.astype(f32)[:, None] * frequency[None, :]
    cosine, sine = jnp.cos(angles), jnp.sin(angles)
    return jnp.concatenate([cosine, cosine], 1), jnp.concatenate([-sine, sine], 1)


def wide_gather(block):
    return lax.all_gather(block, "wide", axis=0, tiled=True)


def wide_scatter(partial):
    return lax.psum_scatter(partial.astype(bf16), "wide", scatter_dimension=0, tiled=True)


def after(value, *others):
    return lax.optimization_barrier((value, *others))[0]


def on_device(n_w, n_s, inputs, documents, cotangent, query_weight, key_weight, value_weight, output_weight,
              query_gain, key_gain, attention_gain, gate_weight, up_weight, down_weight, feed_gain):
    micro, _, local, width = inputs.shape
    tokens = micro * local
    all_tokens = n_s * tokens
    n_dev = n_w * n_s
    heads = HEADS // n_s
    cols = heads * HEAD_DIM
    row_len = documents.shape[2]
    feed = gate_weight.shape[1]
    feed_block = feed // n_dev
    half = n_w * feed_block
    rows = query_weight.shape[0]
    scale = HEAD_DIM ** (-0.5)
    s_index = lax.axis_index("seq")

    flat = inputs.reshape(tokens, width)
    cot = cotangent.reshape(tokens, width)
    halves = 2 * rows == HEAD_DIM and n_w == 2 * heads

    def head_of(s, i):
        return s // 2 + n_s // 2 * (s % 2 * heads + i) if halves else s * heads + i

    def head_column(i):
        return lambda s: head_of(s, i) * HEAD_DIM

    qkv_plan = [[(head_column(h), HEAD_DIM, i * cols + h * HEAD_DIM) for h in range(heads)] for i in range(3)]
    own_blocks = feed_block % 128 == 0
    moves = [(b, (b % n_w) * n_s + b // n_w) for b in range(n_dev)]
    back_moves = [(b, a) for a, b in moves]
    if own_blocks:
        feed_plan = [[(lambda s, a=a: (a * n_s + s) * feed_block, feed_block, i * half + a * feed_block) for a in range(n_w)] for i in range(2)]
    else:
        feed_plan = [[(lambda s: s * half, half, i * half)] for i in range(2)]

    own_gain = jnp.stack([query_gain, key_gain, attention_gain, feed_gain]).astype(f32)
    own_gain = jnp.pad(own_gain, ((0, 4), (0, 128 - rows)))
    qkv = first_exchange((query_weight, key_weight, value_weight), qkv_plan, 3 * cols, n_s, 0)
    qkv_all = wide_gather(qkv.reshape(n_s * rows, 3 * cols))
    if halves:
        out_halves = wide_gather(after(output_weight, qkv)).reshape(n_w, rows, width)
    else:
        out_all = wide_gather(lax.ppermute(output_weight, ("wide", "seq"), moves))
    x_all, gate_up, gains = second_exchange(after(flat, qkv), (gate_weight, up_weight), own_gain, feed_plan, 2 * half, n_w, n_s, 1)
    x_all = x_all.reshape(all_tokens, width)
    gate_up_all = wide_gather(gate_up.reshape(n_s * rows, 2 * half))
    down_block = down_weight
    if not own_blocks:
        down_block = lax.ppermute(down_block, ("wide", "seq"), moves)
    down_all = wide_gather(down_block)

    gains = jnp.swapaxes(gains[:, :4, :rows], 0, 1).reshape(4, width)

    def own_heads(v):
        return jnp.concatenate([lax.dynamic_slice_in_dim(v, head_of(s_index, i) * HEAD_DIM, HEAD_DIM, 1) for i in range(heads)], 1)

    own_gains = own_heads(gains)

    lin = dot(x_all, qkv_all)
    q_lin, k_lin = lin[:, :cols], lin[:, cols : 2 * cols]

    def stack_sums(a, b):
        return jnp.stack([a, b] + [jnp.zeros_like(a)] * 6)

    sums = stack_sums(jnp.sum(q_lin * q_lin, 1), jnp.sum(k_lin * k_lin, 1))
    if halves:
        sums, out_all = sums_exchange(sums, out_halves, False, n_w, n_s, 2)
        out_all = out_all.reshape(cols, width)
    else:
        sums = exchange(sums, n_w, n_s, False, 2)
    inv = lax.rsqrt(jnp.sum(sums, 0)[:2] / width + eps_norm).T
    tables = rotation_tables(jnp.arange(row_len, dtype=jnp.int32))
    docs = documents[:, 0, :]
    shape4 = (n_s, micro, local, -1)
    attended, q, k, v, lse = attend(lin.reshape(shape4), inv.reshape(shape4), own_gains, tables, docs, heads, scale)
    attended = attended.reshape(all_tokens, cols)

    own_f32 = ((tokens, width), f32)
    vec_f32 = ((1, width), f32)
    hidden_all, hidden, mixed_n, mixed_inv = around(
        dot(attended, out_all).astype(bf16), (flat, gains[2:3]), mixed_rows, [own_f32, own_f32, ((tokens, 1), f32)], n_s, 3, False
    )
    hidden_all = hidden_all.reshape(all_tokens, width)
    gate_up_lin = dot(hidden_all, gate_up_all)
    gate_lin, upward = gate_up_lin[:, :half], gate_up_lin[:, half:]
    sigma = jax.nn.sigmoid(gate_lin)
    silu_gate = gate_lin * sigma
    active = (silu_gate * upward).astype(bf16)
    d_down_all, layer_out, feed_term = around(
        dot(active, down_all).astype(bf16), (hidden, cot, gains[3:4]), down_rows, [((tokens, width), bf16), vec_f32], n_s, 4, True
    )
    d_down_all = d_down_all.reshape(all_tokens, width)
    d_active = dot_t(d_down_all, down_all)
    d_gate = (d_active * upward * sigma * (1.0 + gate_lin * (1.0 - sigma))).astype(bf16)
    d_up = (d_active * silu_gate).astype(bf16)
    d_gate_up = jnp.concatenate([d_gate, d_up], axis=1)
    mlp_part = t_dot(hidden_all, d_gate_up).astype(bf16)
    mlp_grad = wide_scatter(mlp_part)
    d_mixed_all, d_hidden, attention_term, down_part = around(
        dot_t(after(d_gate_up, mlp_part), gate_up_all).astype(bf16), (cot, mixed_n, mixed_inv, gains[2:3]), hidden_rows, [own_f32, vec_f32],
        n_s, 5, True, (active, d_down_all),
    )
    mlp_grad, d_mixed_all, down_part = lax.optimization_barrier((mlp_grad, d_mixed_all, down_part))
    down_grad = wide_scatter(down_part)
    mlp_grad = lax.all_to_all(mlp_grad, "seq", 0, 0, tiled=True)
    d_mixed_all = d_mixed_all.reshape(all_tokens, width)
    out_part = t_dot(attended, d_mixed_all).astype(bf16)
    d_attended = dot_t(d_mixed_all, out_all).astype(bf16).reshape(shape4)

    d_q, d_k, d_v = attend_back(q, k, v, lse, d_attended, tables, docs, heads, scale)
    d_q, d_k, d_v = (t.reshape(all_tokens, cols) for t in (d_q, d_k, d_v))
    q_n, k_n = q_lin * inv[:, 0:1], k_lin * inv[:, 1:2]
    d_qg, d_kg = d_q * own_gains[0], d_k * own_gains[1]
    mean_sums = stack_sums(jnp.sum(d_qg * q_n, 1), jnp.sum(d_kg * k_n, 1))
    if halves:
        mean_sums, out_part = sums_exchange(mean_sums, out_part.reshape(heads, 2, rows, width), True, n_w, n_s, 6)
    else:
        mean_sums = exchange(mean_sums, n_w, n_s, False, 6)
    mean_sums, mlp_grad = lax.optimization_barrier((mean_sums, mlp_grad))
    means = jnp.sum(mean_sums, 0)[:2].T / width
    query_term = jnp.sum(d_q * q_n, 0)
    key_term = jnp.sum(d_k * k_n, 0)
    d_q_lin = (inv[:, 0:1] * (d_qg - q_n * means[:, 0:1])).astype(bf16)
    d_k_lin = (inv[:, 1:2] * (d_kg - k_n * means[:, 1:2])).astype(bf16)
    d_lin = jnp.concatenate([d_q_lin, d_k_lin, d_v], axis=1)
    qkv_part = t_dot(x_all, d_lin).astype(bf16)
    down_grad, qkv_part = lax.optimization_barrier((down_grad, qkv_part))
    input_grad = last_sum(dot_t(after(d_lin, qkv_part), qkv_all).astype(bf16), d_hidden, n_s, 7).reshape(inputs.shape)
    qkv_grad = wide_scatter(qkv_part)
    out_grad = wide_scatter(after(out_part, qkv_grad, input_grad).reshape(cols, width))
    if not halves:
        out_grad = lax.ppermute(out_grad, ("wide", "seq"), back_moves)

    def spread(term):
        full = jnp.zeros((width,), f32)
        for i in range(heads):
            full = lax.dynamic_update_slice_in_dim(full, term[i * HEAD_DIM : (i + 1) * HEAD_DIM], head_of(s_index, i) * HEAD_DIM, 0)
        return full

    terms = jnp.stack([spread(query_term), spread(key_term), attention_term[0], feed_term[0]])
    terms = jnp.swapaxes(terms.reshape(4, n_dev, rows), 0, 1)
    terms = jnp.pad(terms, ((0, 0), (0, 4), (0, 128 - rows)))
    qkv_grad, all_terms = final_exchange(qkv_grad.reshape(n_s, rows, 3 * cols), after(terms, input_grad), n_w, n_s, 8)
    gate_grad, up_grad = unpack(mlp_grad.reshape(n_s, rows, 2 * half), feed, feed_plan)
    query_grad, key_grad, value_grad = unpack(qkv_grad, width, qkv_plan)
    gain_grads = jnp.sum(all_terms, 0)[:4, :rows]
    if not own_blocks:
        down_grad = lax.ppermute(down_grad, ("wide", "seq"), back_moves)
    return (layer_out.reshape(inputs.shape), input_grad, query_grad, key_grad, value_grad, out_grad.astype(f32),
            gain_grads[0], gain_grads[1], gain_grads[2], gate_grad, up_grad, down_grad.astype(f32), gain_grads[3])


def solution(mesh):
    tok = P(None, "wide", "seq", None)
    docs = P(None, "wide", None)
    mat = P(("wide", "seq"), None)
    vec = P(("wide", "seq"))

    def body(*args):
        return on_device(mesh.shape["wide"], mesh.shape["seq"], *args)

    return jax.shard_map(
        body,
        mesh=mesh,
        in_specs=(tok, docs, tok, mat, mat, mat, mat, vec, vec, vec, mat, mat, mat, vec),
        out_specs=(tok, tok, mat, mat, mat, mat, vec, vec, vec, mat, mat, mat, vec),
        check_vma=False,
    )
```

```python
import functools

import jax
import jax.numpy as jnp
from jax import lax
from jax.experimental import pallas as pl
from jax.experimental.pallas import tpu as pltpu
from jax.sharding import PartitionSpec as P

HEADS = 16
HEAD_DIM = 128
eps_norm = 1e-06
rope_base = 500000.0
masked_value = -1e30
bf16 = jnp.bfloat16
f32 = jnp.float32
MESH = pl.DeviceIdType.MESH
ANY = pl.BlockSpec(memory_space=pl.ANY)
VM = pl.BlockSpec(memory_space=pltpu.VMEM)
DMA = pltpu.SemaphoreType.DMA
PACE = 1
CHUNKS = 4
SUB = 4


def params(cid, megabytes=None):
    limit = {} if megabytes is None else {"vmem_limit_bytes": megabytes * 2**20}
    return pltpu.CompilerParams(collective_id=cid, has_side_effects=True, **limit)


def cost(microseconds):
    return pl.CostEstimate(flops=0, transcendentals=0, bytes_accessed=int(microseconds * 3e6))


def far_first(n_s):
    return sorted(range(n_s), key=lambda k: -min(k, n_s - k))


def remote(src, dst, send, recv, device):
    return pltpu.make_async_remote_copy(src, dst, send, recv, device_id=device, device_id_type=MESH)


def greet(targets):
    barrier = pltpu.get_barrier_semaphore()
    count = 0
    for cond, dev in targets:
        if cond is None:
            pl.semaphore_signal(barrier, inc=1, device_id=dev, device_id_type=MESH)
            count = count + 1
        else:

            @pl.when(cond)
            def _():
                pl.semaphore_signal(barrier, inc=1, device_id=dev, device_id_type=MESH)

            count = count + cond.astype(jnp.int32)
    pl.semaphore_wait(barrier, count)


class Line:
    def __init__(self, n_s):
        self.s = lax.axis_index("seq")
        self.nz = n_s // 2
        self.z, self.c = self.s // 2, self.s % 2
        self.mate_slot = self.s + 1 - 2 * self.c
        self.mate = {"seq": self.mate_slot}
        self.steps = (1, -1)
        self.more = (self.z < self.nz - 1, self.z > 0)
        self.next = ({"seq": self.s + 2}, {"seq": self.s - 2})

    def neighbours(self):
        return [(self.more[0], self.next[0]), (self.more[1], self.next[1]), (None, self.mate)]


class Gather:
    def __init__(self, line, own, out, chunks, send, recv, mate_send, mate_recv):
        self.line, self.own, self.out = line, own, out
        self.chunks, self.rows = chunks, own.shape[0] // chunks
        self.send, self.recv, self.mate_send, self.mate_recv = send, recv, mate_send, mate_recv

    def part(self, slot, k):
        return self.out.at[slot, pl.ds(k * self.rows, self.rows)]

    def source(self, d, k, slot):
        return self.own.at[pl.ds(k * self.rows, self.rows)] if d == 0 else self.part(slot, k)

    def hop(self, i, d, k, slot):
        return remote(self.source(d, k, slot), self.part(slot, k), self.send.at[i, d, k], self.recv.at[i, d, k], self.line.next[i])

    def share(self, i, d, k, slot):
        return remote(self.source(d, k, slot), self.part(slot, k), self.mate_send.at[i, d, k], self.mate_recv.at[i, d, k], self.line.mate)

    def start(self, k):
        line = self.line
        for i in range(2):

            @pl.when(line.more[i])
            def _():
                self.hop(i, 0, k, line.s).start()

        self.share(0, 0, k, line.s).start()

    def each(self, d, mine=True):
        line = self.line
        for i in range(2):
            origin = line.z - line.steps[i] * d
            yield i, (origin >= 0) & (origin < line.nz), 2 * origin + (line.c if mine else 1 - line.c)

    def pass_on(self, d, k):
        for i, there, slot in self.each(d):

            @pl.when(there)
            def _():
                self.hop(i, d - 1, k, slot).wait_recv()
                if d < self.line.nz - 1:

                    @pl.when(self.line.more[i])
                    def _():
                        self.hop(i, d, k, slot).start()

                self.share(i, d, k, slot).start()

    def finish(self):
        line = self.line
        for k in range(self.chunks):
            self.share(0, 0, k, line.mate_slot).wait_recv()
            for d in range(1, line.nz):
                for i, there, slot in self.each(d, False):

                    @pl.when(there)
                    def _():
                        self.share(i, d, k, slot).wait_recv()

        for k in range(self.chunks):
            self.share(0, 0, k, line.s).wait_send()
            for i in range(2):

                @pl.when(line.more[i])
                def _():
                    self.hop(i, 0, k, line.s).wait_send()

            for d in range(1, line.nz):
                for i, there, slot in self.each(d):

                    @pl.when(there)
                    def _():
                        self.share(i, d, k, slot).wait_send()
                        if d < line.nz - 1:

                            @pl.when(line.more[i])
                            def _():
                                self.hop(i, d, k, slot).wait_send()


class Scatter:
    def __init__(self, line, part, from_mate, run, chunks, send, recv, mate_send, mate_recv):
        self.line, self.part, self.from_mate, self.run = line, part, from_mate, run
        self.chunks, self.rows = chunks, part.shape[1] // chunks
        self.send, self.recv, self.mate_send, self.mate_recv = send, recv, mate_send, mate_recv
        self.steps = line.nz - 1
        self.groups = chunks // SUB
        self.count = self.steps * self.groups

    def span(self, k):
        return pl.ds(pl.multiple_of(k * self.rows, self.rows), self.rows)

    def give(self, zd, k):
        line, rs = self.line, self.span(k)
        return remote(self.part.at[2 * zd + 1 - line.c, rs], self.from_mate.at[zd, rs], self.mate_send.at[zd, k], self.mate_recv.at[zd, k], line.mate)

    def hop(self, i, zd, k):
        ref = self.run.at[i, zd, self.span(k)]
        return remote(ref, ref, self.send.at[i, zd, k], self.recv.at[i, zd, k], self.line.next[i])

    def pair(self, zd, k):
        rs = self.span(k)
        return self.part[2 * zd + self.line.c, rs].astype(f32) + self.from_mate[zd, rs].astype(f32)

    def start(self, k):
        nz = self.line.nz
        for zd in sorted(range(nz), key=lambda zd: (min(zd, nz - 1 - zd), -zd)):
            self.give(zd, k).start()

    def item(self, i, q, j):
        group, step = q // self.steps, lax.rem(q, self.steps)
        return (self.line.nz - 1 - step if i == 0 else step), group * SUB + j

    def slot(self, t):
        line = self.line
        for j, i in ((j, i) for j in range(SUB) for i in range(2)):
            q = t - (line.z if i == 0 else line.nz - 1 - line.z)
            behind = line.z > 0 if i == 0 else line.z < line.nz - 1
            zd, k = self.item(i, jnp.clip(q, 0, self.count - 1), j)
            going = (q >= 0) & (q < self.count) & (line.z < zd if i == 0 else line.z > zd)

            @pl.when(going)
            def _():
                rs = self.span(k)
                self.give(zd, k).wait_recv()

                @pl.when(behind)
                def _():
                    self.hop(i, zd, k).wait_recv()
                    self.run[i, zd, rs] = (self.pair(zd, k) + self.run[i, zd, rs].astype(f32)).astype(bf16)

                @pl.when(jnp.logical_not(behind))
                def _():
                    self.run[i, zd, rs] = self.pair(zd, k).astype(bf16)
                    if t >= PACE:
                        self.hop(i, *self.item(i, jnp.int32(t - PACE), j)).wait_send()

                self.hop(i, zd, k).start()

    def total(self, k, use):
        line, rs = self.line, self.span(k)
        for zd in range(line.nz):

            @pl.when(line.z == zd)
            def _():
                self.give(zd, k).wait_recv()
                total = self.pair(zd, k)
                if zd > 0:
                    self.hop(0, zd, k).wait_recv()
                    total = total + self.run[0, zd, rs].astype(f32)
                if zd < line.nz - 1:
                    self.hop(1, zd, k).wait_recv()
                    total = total + self.run[1, zd, rs].astype(f32)
                use(total)

    def finish(self):
        line = self.line
        for k in range(self.chunks):
            for zd in range(line.nz):
                self.give(zd, k).wait_send()
        for q in range(self.count):
            step = q % self.steps
            for i, zd in ((0, line.nz - 1 - step), (1, step)):
                going = line.z < zd if i == 0 else line.z > zd
                behind = line.z > 0 if i == 0 else line.z < line.nz - 1

                @pl.when(going & behind if q < self.count - PACE else going)
                def _():
                    for j in range(SUB):
                        self.hop(i, zd, q // self.steps * SUB + j).wait_send()


def line_sems(nz, chunks):
    return [DMA((2, nz, chunks))] * 4


def scatter_scratch(n_s, rows, width, chunks):
    nz = n_s // 2
    sums = [pltpu.VMEM((nz, rows, width), bf16), pltpu.VMEM((2, nz, rows, width), bf16)]
    return sums + [DMA((2, nz, chunks))] * 2 + [DMA((nz, chunks))] * 2


def mixed_rows(rs, total, x, gain, hidden, normed, inverse, low):
    inv = inverse_rms(total)
    n = total * inv
    out = x[rs].astype(f32) + n * gain[...]
    hidden[rs] = out
    normed[rs] = n
    inverse[rs] = inv
    low[rs] = out.astype(bf16)


def down_rows(rs, total, hidden, cotangent, gain, out, term, low):
    inv = inverse_rms(total)
    n = total * inv
    g = gain[...]
    out[rs] = (hidden[rs] + n * g).astype(bf16)
    grad = cotangent[rs].astype(f32)
    low[rs], more = back_rows(grad, n, inv, g)
    term[...] += more


def hidden_rows(rs, total, cotangent, normed, inverse, gain, d_hidden, term, low):
    grad = cotangent[rs].astype(f32) + total
    d_hidden[rs] = grad
    low[rs], more = back_rows(grad, normed[rs], inverse[rs], gain[...])
    term[...] += more


def back_rows(grad, n, inv, gain):
    scaled = grad * gain
    d = inv * (scaled - n * jnp.mean(scaled * n, axis=-1, keepdims=True))
    return d.astype(bf16), jnp.sum(grad * n, axis=0, keepdims=True)


def run_slots(scatter, use, gather=None, work=None):
    steps, groups = scatter.steps, scatter.groups
    slots = steps * (groups + (1 if gather else 0)) + 1
    for t in range(slots):
        if t < steps * (groups + 1):
            scatter.slot(t)
        if gather:
            for group in range(groups):
                if 1 <= t - steps * (group + 1) <= steps:
                    for j in range(SUB):
                        gather.pass_on(t - steps * (group + 1), group * SUB + j)
        if t and t % steps == 0 and t // steps <= groups:
            for k in range((t // steps - 1) * SUB, t // steps * SUB):
                scatter.total(k, lambda total: use(k, total))
                if gather:
                    gather.start(k)
        if work:
            work(t, slots)


def product_work(left, right, out):
    size = 128
    count = out.shape[0] // size

    def work(t, slots):
        for i in range(count * t // slots, count * (t + 1) // slots):
            rs = pl.ds(i * size, size)
            out[rs] = lax.dot_general(left[:, rs], right[...], (((0,), (0,)), ((), ())), preferred_element_type=f32).astype(bf16)

    return work


def around_kernel(n_s, chunks, rows_fn, n_in, n_out, adds, with_work, *refs):
    part, extra = refs[0], refs[1 : 1 + n_in]
    refs = refs[1 + n_in :]
    work = None
    if with_work:
        left, right, gathered, *outs, made = refs[: 4 + n_out]
        work = product_work(left, right, made)
        refs = refs[4 + n_out :]
    else:
        gathered, *outs = refs[: 1 + n_out]
        refs = refs[1 + n_out :]
    low, local, from_mate, run, *sems = refs
    line = Line(n_s)
    scatter = Scatter(line, part, from_mate, run, chunks, *sems[:4])
    gather = Gather(line, low, gathered, chunks, *sems[4:])
    greet(line.neighbours())
    for k in range(chunks):
        scatter.start(k)
    if adds:
        outs[-1][...] = jnp.zeros_like(outs[-1])
    run_slots(scatter, lambda k, total: rows_fn(scatter.span(k), total, *extra, *outs, low), gather, work)
    own = pltpu.make_async_copy(low, gathered.at[line.s], local)
    own.start()
    gather.finish()
    scatter.finish()
    own.wait()


def around(terms, extra, rows_fn, outs, n_s, cid, adds, pair=(), chunks=CHUNKS):
    rows, width = terms.shape[0] // n_s, terms.shape[1]
    shapes = [((n_s, rows, width), bf16), *outs] + ([((pair[0].shape[1], pair[1].shape[1]), bf16)] if pair else [])
    return pl.pallas_call(
        functools.partial(around_kernel, n_s, chunks, rows_fn, len(extra), len(outs), adds, bool(pair)),
        out_shape=[jax.ShapeDtypeStruct(*o) for o in shapes],
        in_specs=[VM] * (1 + len(extra) + len(pair)),
        out_specs=[ANY] + [VM] * (len(shapes) - 1),
        scratch_shapes=[pltpu.VMEM((rows, width), bf16), DMA] + scatter_scratch(n_s, rows, width, chunks) + line_sems(n_s // 2, chunks),
        compiler_params=params(cid, 48),
        cost_estimate=cost(70),
    )(terms.reshape(n_s, rows, width), *extra, *pair)


def last_kernel(n_w, n_s, chunks, part, d_hidden, terms, out, all_terms, from_mate, run, *sems):
    line = Line(n_s)
    scatter = Scatter(line, part, from_mate, run, chunks, *sems[:4])
    share = Share(n_w, n_s, True, terms, all_terms, *sems[4:])
    greet(share.others())
    for k in range(chunks):
        scatter.start(k)

    def use(k, total):
        out[scatter.span(k)] = d_hidden[scatter.span(k)] + total

    share.start()
    run_slots(scatter, use)
    scatter.finish()
    share.finish()


def last_sum(part, d_hidden, terms, n_w, n_s, cid, chunks=CHUNKS):
    rows, width = part.shape[0] // n_s, part.shape[1]
    count = n_w * n_s
    return pl.pallas_call(
        functools.partial(last_kernel, n_w, n_s, chunks),
        out_shape=[jax.ShapeDtypeStruct((rows, width), f32), jax.ShapeDtypeStruct(terms.shape, terms.dtype)],
        in_specs=[VM] * 3,
        out_specs=[VM] * 2,
        scratch_shapes=scatter_scratch(n_s, rows, width, chunks) + [DMA((count,)), DMA((count,)), DMA],
        compiler_params=params(cid, 48),
        cost_estimate=cost(40),
    )(part.reshape(n_s, rows, width), d_hidden, terms)


class Columns:
    def __init__(self, n_s, plan, arrays, slots, back, send, recv, local):
        self.n_s, self.plan, self.arrays, self.slots, self.back = n_s, plan, arrays, slots, back
        self.send, self.recv, self.local = send, recv, local
        self.s = lax.axis_index("seq")

    def place(self, k):
        return lax.rem(self.s + k, self.n_s)

    def pieces(self, k):
        there = self.place(k)
        for array, parts in zip(self.arrays, self.plan):
            for first, width, column in parts:
                at = pl.ds(column, width)
                if self.back:
                    yield self.slots.at[there, :, at], array.at[:, pl.ds(pl.multiple_of(first(self.s), 128), width)]
                else:
                    yield array.at[:, pl.ds(pl.multiple_of(first(there), 128), width)], self.slots.at[self.s, :, at]

    def start(self):
        for k in far_first(self.n_s)[:-1]:
            for src, dst in self.pieces(k):
                remote(src, dst, self.send.at[k], self.recv.at[k], {"seq": self.place(k)}).start()
        for src, dst in self.pieces(0):
            pltpu.make_async_copy(src, dst, self.local).start()

    def finish(self):
        slot = self.slots.at[0]
        for k in range(1, self.n_s):
            done = remote(slot, slot, self.send.at[k], self.recv.at[k], {"seq": self.place(k)})
            done.wait_recv()
            done.wait_send()
        pltpu.make_async_copy(slot, slot, self.local).wait()


def columns_sems(n_s):
    return [DMA((n_s,)), DMA((n_s,)), DMA]


def seq_others(n_s):
    s = lax.axis_index("seq")
    return [(None, {"seq": lax.rem(s + k, n_s)}) for k in range(1, n_s)]


class Share:
    def __init__(self, n_w, n_s, whole, x, out, send, recv, local):
        self.n_w, self.n_s, self.whole = n_w, n_s, whole
        self.x, self.out, self.send, self.recv, self.local = x, out, send, recv, local
        self.w, self.s = lax.axis_index("wide"), lax.axis_index("seq")
        self.steps = [(a, b) for b in far_first(n_s) for a in (range(n_w) if whole else (0,)) if a or b]

    def at(self, a, b):
        return lax.rem(self.w + a, self.n_w), lax.rem(self.s + b, self.n_s)

    def number(self, a, b):
        w, s = self.at(a, b)
        return w * self.n_s + s if self.whole else s

    def name(self, a, b):
        w, s = self.at(a, b)
        return {"wide": w, "seq": s}

    def others(self):
        return [(None, self.name(a, b)) for a, b in self.steps]

    def block(self, a, b):
        return self.x.at[self.number(a, b)] if len(self.x.shape) == 3 else self.x

    def copy(self, a, b):
        i = a * self.n_s + b
        return remote(self.block(a, b), self.out.at[self.number(0, 0)], self.send.at[i], self.recv.at[i], self.name(a, b))

    def own(self):
        return pltpu.make_async_copy(self.block(0, 0), self.out.at[self.number(0, 0)], self.local)

    def start(self):
        for a, b in self.steps:
            self.copy(a, b).start()
        self.own().start()

    def finish(self):
        for a, b in self.steps:
            self.copy(a, b).wait()
        self.own().wait()


def share_kernel(n_w, n_s, whole, x_ref, o_ref, send, recv, local_sem):
    share = Share(n_w, n_s, whole, x_ref, o_ref, send, recv, local_sem)
    greet(share.others())
    share.start()
    share.finish()


def exchange(x, n_w, n_s, whole, cid):
    count = n_w * n_s if whole else n_s
    return pl.pallas_call(
        functools.partial(share_kernel, n_w, n_s, whole),
        out_shape=jax.ShapeDtypeStruct((count, *x.shape[-2:]), x.dtype),
        in_specs=[VM],
        out_specs=VM,
        scratch_shapes=[DMA((count,)), DMA((count,)), DMA],
        compiler_params=params(cid),
        cost_estimate=cost(10),
    )(x)


class Halves:
    def __init__(self, n_w, natural, heads, send, recv, local):
        s = lax.axis_index("seq")
        c = lax.rem(s, 2)
        mate = {"seq": s + 1 - 2 * c}
        self.copies = []
        for i in range(n_w // 2):
            there = natural.at[c * (n_w // 2) + i]
            self.copies.append(remote(heads.at[i, 1 - c], there, send.at[i], recv.at[i], mate))
            self.copies.append(pltpu.make_async_copy(heads.at[i, c], there, local.at[i]))

    def start(self):
        for copy in self.copies:
            copy.start()

    def finish(self):
        for copy in self.copies:
            copy.wait()


def halves_sems(n_w):
    return [DMA((n_w // 2,))] * 3


def first_kernel(n_s, plan, qw, kw, vw, qkv, *sems):
    columns = Columns(n_s, plan, (qw, kw, vw), qkv, False, *sems)
    greet(seq_others(n_s))
    columns.start()
    columns.finish()


def first_exchange(weights, plan, cols, n_s, cid):
    return pl.pallas_call(
        functools.partial(first_kernel, n_s, plan),
        out_shape=jax.ShapeDtypeStruct((n_s, weights[0].shape[0], cols), bf16),
        in_specs=[ANY] * 3,
        out_specs=ANY,
        scratch_shapes=columns_sems(n_s),
        compiler_params=params(cid),
        cost_estimate=cost(20),
    )(*weights)


class Heads:
    def __init__(self, n_w, block, heads, send, recv, local):
        w, s = lax.axis_index("wide"), lax.axis_index("seq")
        half = n_w // 2
        c = lax.rem(s, 2)
        core = w // half
        self.lane = core == c
        dst = heads.at[lax.rem(w, half), c]
        self.sends = []
        for k in range(n_w):
            device = {"wide": lax.rem(w + k, n_w), "seq": s - c + core}
            self.sends.append(remote(block, dst, send.at[k], recv.at[lax.rem(w, half), c], device))
        self.stay = pltpu.make_async_copy(block, dst, local)
        self.arrivals = []
        for i in range(half):
            for there in range(2):
                own = self.lane & (lax.rem(w, half) == i) & (c == there)
                ref = heads.at[i, there]
                self.arrivals.append((jnp.logical_not(own), remote(ref, ref, send.at[0], recv.at[i, there], {"seq": s + 1 - 2 * c})))

    def start(self):
        for copy in self.sends[1:]:
            copy.start()

        @pl.when(self.lane)
        def _():
            self.stay.start()

        @pl.when(jnp.logical_not(self.lane))
        def _():
            self.sends[0].start()

    def finish(self):
        for come, copy in self.arrivals:

            @pl.when(come)
            def _():
                copy.wait_recv()

        for copy in self.sends[1:]:
            copy.wait_send()

        @pl.when(self.lane)
        def _():
            self.stay.wait()

        @pl.when(jnp.logical_not(self.lane))
        def _():
            self.sends[0].wait_send()


def second_kernel(n_w, n_s, chunks, plan, heads, x, gw, uw, gain, *refs):
    if heads:
        out_block, x_all, slots, gains, out_heads, own_sem, *sems = refs
    else:
        x_all, slots, gains, own_sem, *sems = refs
    line = Line(n_s)
    gather = Gather(line, x, x_all, chunks, *sems[:4])
    others = [Share(n_w, n_s, True, gain, gains, *sems[4:7])]
    if heads:
        others.append(Heads(n_w, out_block, out_heads, *sems[7:10]))
    others.append(Columns(n_s, plan, (gw, uw), slots, False, *sems[-3:]))
    greet(others[0].others())
    own = pltpu.make_async_copy(x, x_all.at[line.s], own_sem)
    for k in range(chunks):
        gather.start(k)
    own.start()
    for other in others:
        other.start()
    for d in range(1, line.nz):
        for k in range(chunks):
            gather.pass_on(d, k)
    gather.finish()
    own.wait()
    for other in others:
        other.finish()


def second_exchange(x, weights, gain, out_block, plan, cols, n_w, n_s, cid, chunks=2):
    rows, width = x.shape
    count = n_w * n_s
    shapes = [((n_s, rows, width), bf16), ((n_s, weights[0].shape[0], cols), bf16), ((count, *gain.shape), gain.dtype)]
    sems = [DMA] + line_sems(n_s // 2, chunks) + [DMA((count,)), DMA((count,)), DMA]
    extra = []
    if out_block is not None:
        extra = [out_block]
        shapes.append(((n_w // 2, 2, *out_block.shape), bf16))
        sems += [DMA((n_w,)), DMA((n_w // 2, 2)), DMA]
    return pl.pallas_call(
        functools.partial(second_kernel, n_w, n_s, chunks, plan, bool(extra)),
        out_shape=[jax.ShapeDtypeStruct(*o) for o in shapes],
        in_specs=[ANY] * 3 + [VM] + [ANY] * len(extra),
        out_specs=[ANY, ANY, VM] + [ANY] * len(extra),
        scratch_shapes=sems + columns_sems(n_s),
        compiler_params=params(cid),
        cost_estimate=cost(80),
    )(x, *weights, gain, *extra)


def unpack_kernel(n_s, plan, slots, *outs):
    for out, pieces in zip(outs, plan):
        for first, width, column in pieces:
            for s in range(n_s):
                out[:, first(s) : first(s) + width] = slots[s, :, column : column + width].astype(f32)


def unpack(slots, width, plan):
    n_s, rows, _ = slots.shape
    return pl.pallas_call(
        functools.partial(unpack_kernel, n_s, plan),
        out_shape=[jax.ShapeDtypeStruct((rows, width), f32)] * len(plan),
        in_specs=[VM],
        out_specs=[VM] * len(plan),
        compiler_params=pltpu.CompilerParams(vmem_limit_bytes=40 * 2**20),
        cost_estimate=cost(4),
    )(slots)


def sums_kernel(n_w, n_s, x, heads, all_x, natural, *sems):
    share = Share(n_w, n_s, False, x, all_x, *sems[:3])
    halves = Halves(n_w, natural, heads, *sems[3:])
    greet(share.others())
    share.start()
    halves.start()
    share.finish()
    halves.finish()


def sums_exchange(x, heads, n_w, n_s, cid):
    return pl.pallas_call(
        functools.partial(sums_kernel, n_w, n_s),
        out_shape=[jax.ShapeDtypeStruct((n_s, *x.shape), x.dtype), jax.ShapeDtypeStruct((n_w, *heads.shape[2:]), bf16)],
        in_specs=[VM, VM],
        out_specs=[VM, VM],
        scratch_shapes=[DMA((n_s,)), DMA((n_s,)), DMA] + halves_sems(n_w),
        compiler_params=params(cid),
        cost_estimate=cost(10),
    )(x, heads)


def final_kernel(n_w, n_s, qkv, qkv_own, *sems):
    share = Share(n_w, n_s, False, qkv, qkv_own, *sems)
    greet(seq_others(n_s))
    share.start()
    share.finish()


def final_exchange(qkv, n_w, n_s, cid):
    return pl.pallas_call(
        functools.partial(final_kernel, n_w, n_s),
        out_shape=jax.ShapeDtypeStruct(qkv.shape, qkv.dtype),
        in_specs=[ANY],
        out_specs=ANY,
        scratch_shapes=[DMA((n_s,)), DMA((n_s,)), DMA],
        compiler_params=params(cid),
        cost_estimate=cost(20),
    )(qkv)


def feed_kernel(hidden, gate_w, up_w, active, slope, swish):
    rows = hidden.shape[0] // 4
    for i in range(4):
        rs = pl.ds(i * rows, rows)
        gate, up = dot(hidden[rs], gate_w[...]), dot(hidden[rs], up_w[...])
        sigma = jax.nn.sigmoid(gate)
        silu = gate * sigma
        active[rs] = (silu * up).astype(bf16)
        slope[rs] = (up * sigma * (1.0 + gate * (1.0 - sigma))).astype(bf16)
        swish[rs] = silu.astype(bf16)


def feed_forward(hidden, weights, tile=256):
    tokens, width = hidden.shape
    half = weights.shape[1] // 2
    steps = half // tile
    out = pl.BlockSpec((tokens, tile), lambda j: (0, j))
    return pl.pallas_call(
        feed_kernel,
        grid=(steps,),
        out_shape=[jax.ShapeDtypeStruct((tokens, half), bf16)] * 3,
        in_specs=[
            pl.BlockSpec((tokens, width), lambda j: (0, 0)),
            pl.BlockSpec((width, tile), lambda j: (0, j)),
            pl.BlockSpec((width, tile), lambda j: (0, j + steps)),
        ],
        out_specs=[out] * 3,
        compiler_params=pltpu.CompilerParams(vmem_limit_bytes=48 * 2**20),
        cost_estimate=pl.CostEstimate(flops=4 * tokens * width * half, transcendentals=0, bytes_accessed=2 * (tokens * width + 2 * width * half)),
    )(hidden, weights, weights)


def feed_back_kernel(d_down, down_w, slope, swish, out):
    tile = down_w.shape[0]
    half = out.shape[1] // 2
    d_active = dot_t(d_down[...], down_w[...])
    at = pl.multiple_of(pl.program_id(0) * tile, tile)
    out[:, pl.ds(at, tile)] = (d_active * slope[...].astype(f32)).astype(bf16)
    out[:, pl.ds(pl.multiple_of(at + half, tile), tile)] = (d_active * swish[...].astype(f32)).astype(bf16)


def feed_back(d_down, down_w, slope, swish, tile=256):
    tokens, width = d_down.shape
    half = down_w.shape[0]
    cols = pl.BlockSpec((tokens, tile), lambda j: (0, j))
    return pl.pallas_call(
        feed_back_kernel,
        grid=(half // tile,),
        out_shape=jax.ShapeDtypeStruct((tokens, 2 * half), bf16),
        in_specs=[pl.BlockSpec((tokens, width), lambda j: (0, 0)), pl.BlockSpec((tile, width), lambda j: (j, 0)), cols, cols],
        out_specs=pl.BlockSpec((tokens, 2 * half), lambda j: (0, 0)),
        compiler_params=pltpu.CompilerParams(vmem_limit_bytes=48 * 2**20),
        cost_estimate=pl.CostEstimate(flops=2 * tokens * width * half, transcendentals=0, bytes_accessed=2 * (tokens * width + width * half)),
    )(d_down, down_w, slope, swish)


def rows_kernel(a, b, out):
    out[...] = lax.dot_general(a[...], b[...], (((1,), (1,)), ((), ())), preferred_element_type=f32).astype(bf16)


def columns_product(a, b, tile=512):
    (m, k), n = a.shape, b.shape[0]
    return pl.pallas_call(
        rows_kernel,
        grid=(n // tile,),
        out_shape=jax.ShapeDtypeStruct((m, n), bf16),
        in_specs=[pl.BlockSpec((m, k), lambda j: (0, 0)), pl.BlockSpec((tile, k), lambda j: (j, 0))],
        out_specs=pl.BlockSpec((m, tile), lambda j: (0, j)),
        compiler_params=pltpu.CompilerParams(vmem_limit_bytes=48 * 2**20),
        cost_estimate=pl.CostEstimate(flops=2 * m * n * k, transcendentals=0, bytes_accessed=2 * (m * k + k * n + m * n)),
    )(a, b)


def terms_kernel(a, b, out):
    out[...] = lax.dot_general(a[...], b[...], (((0,), (0,)), ((), ())), preferred_element_type=f32).astype(bf16)


def weight_product(a, b, tile=512):
    (k, m), n = a.shape, b.shape[1]
    return pl.pallas_call(
        terms_kernel,
        grid=(m // tile,),
        out_shape=jax.ShapeDtypeStruct((m, n), bf16),
        in_specs=[pl.BlockSpec((k, tile), lambda i: (0, i)), pl.BlockSpec((k, n), lambda i: (0, 0))],
        out_specs=pl.BlockSpec((tile, n), lambda i: (i, 0)),
        compiler_params=pltpu.CompilerParams(vmem_limit_bytes=48 * 2**20),
        cost_estimate=pl.CostEstimate(flops=2 * m * n * k, transcendentals=0, bytes_accessed=2 * (m * k + k * n + m * n)),
    )(a, b)


def dot(a, b):
    return jnp.dot(a, b, preferred_element_type=f32)


def dot_t(a, b):
    return lax.dot_general(a, b, (((1,), (1,)), ((), ())), preferred_element_type=f32)


def t_dot(a, b):
    return lax.dot_general(a, b, (((0,), (0,)), ((), ())), preferred_element_type=f32)


def turn(v, cosine, sine):
    return v * cosine + pltpu.roll(v, HEAD_DIM // 2, 1) * sine


def allowed_pairs(doc_q, doc_k, length):
    rows = lax.broadcasted_iota(jnp.int32, (length, length), 0)
    cols = lax.broadcasted_iota(jnp.int32, (length, length), 1)
    return (cols <= rows) & (doc_q == doc_k)


def attend_kernel(scale, ql, kl, vl, inv, gq, gk, cos, sin, doc_q, doc_k, att, q_out, k_out, v_out, lse):
    length = cos.shape[0]

    def flat(ref):
        return ref[...].reshape(length, -1)

    scales = flat(inv)
    q = turn(flat(ql) * scales[:, 0:1] * gq[...], cos[...], sin[...]).astype(bf16)
    k = turn(flat(kl) * scales[:, 1:2] * gk[...], cos[...], sin[...]).astype(bf16)
    v = flat(vl).astype(bf16)
    q_out[...] = q.reshape(q_out.shape)
    k_out[...] = k.reshape(k_out.shape)
    v_out[...] = v.reshape(v_out.shape)
    allowed = allowed_pairs(doc_q[0], doc_k[0], length)
    scores = jnp.where(allowed, dot_t(q, k) * scale, masked_value)
    top = jnp.max(scores, 1, keepdims=True)
    e = jnp.exp(scores - top)
    total = jnp.sum(e, 1, keepdims=True)
    probs = (e * (1.0 / total)).astype(bf16)
    att[...] = dot(probs, v).astype(bf16).reshape(att.shape)
    lse[...] = (top + jnp.log(total)).reshape(lse.shape)


def attend_back_kernel(scale, q, k, v, lse, da, cos, sin, doc_q, doc_k, dq_out, dk_out, dv_out):
    length = cos.shape[0]

    def flat(ref):
        return ref[...].reshape(length, -1)

    queries, keys, values, d_att = flat(q), flat(k), flat(v), flat(da)
    allowed = allowed_pairs(doc_q[0], doc_k[0], length)
    scores = jnp.where(allowed, dot_t(queries, keys) * scale, masked_value)
    probs = jnp.exp(scores - flat(lse))
    d_probs = dot_t(d_att, values)
    delta = jnp.sum(probs * d_probs, 1, keepdims=True)
    d_scores = (probs * (d_probs - delta)).astype(bf16)
    d_q = dot(d_scores, keys) * scale
    d_k = t_dot(d_scores, queries) * scale
    dv_out[...] = t_dot(probs.astype(bf16), d_att).astype(bf16).reshape(dv_out.shape)
    dq_out[...] = turn(d_q, cos[...], -sin[...]).reshape(dq_out.shape)
    dk_out[...] = turn(d_k, cos[...], -sin[...]).reshape(dk_out.shape)


def attention_specs(n_s, local, length):
    def tok(first):
        return pl.BlockSpec((n_s, 1, local, HEAD_DIM), lambda m, h: (0, m, 0, first + h))

    gain = pl.BlockSpec((1, HEAD_DIM), lambda m, h: (0, h))
    table = pl.BlockSpec((length, HEAD_DIM), lambda m, h: (0, 0))
    doc_q = pl.BlockSpec((1, length, 1), lambda m, h: (m, 0, 0))
    doc_k = pl.BlockSpec((1, 1, length), lambda m, h: (m, 0, 0))
    col = pl.BlockSpec((1, n_s, 1, local, 1), lambda m, h: (h, 0, m, 0, 0))
    return tok, gain, table, doc_q, doc_k, col


def attend(lin, inv, gains, tables, docs, heads, scale):
    n_s, micro, local, _ = lin.shape
    length = n_s * local
    tok, gain, table, doc_q, doc_k, col = attention_specs(n_s, local, length)
    inv_spec = pl.BlockSpec((n_s, 1, local, 2), lambda m, h: (0, m, 0, 0))
    out = jax.ShapeDtypeStruct((n_s, micro, local, heads * HEAD_DIM), bf16)
    return pl.pallas_call(
        functools.partial(attend_kernel, scale),
        grid=(micro, heads),
        out_shape=[out, out, out, out, jax.ShapeDtypeStruct((heads, n_s, micro, local, 1), f32)],
        in_specs=[tok(0), tok(heads), tok(2 * heads), inv_spec, gain, gain, table, table, doc_q, doc_k],
        out_specs=[tok(0)] * 4 + [col],
        compiler_params=pltpu.CompilerParams(vmem_limit_bytes=48 * 2**20),
    )(lin, lin, lin, inv, gains[0:1], gains[1:2], *tables, docs[:, :, None], docs[:, None, :])


def attend_back(q, k, v, lse, d_att, tables, docs, heads, scale):
    n_s, micro, local, width = q.shape
    length = n_s * local
    tok, gain, table, doc_q, doc_k, col = attention_specs(n_s, local, length)
    return pl.pallas_call(
        functools.partial(attend_back_kernel, scale),
        grid=(micro, heads),
        out_shape=[jax.ShapeDtypeStruct(q.shape, f32)] * 2 + [jax.ShapeDtypeStruct(q.shape, bf16)],
        in_specs=[tok(0)] * 3 + [col, tok(0), table, table, doc_q, doc_k],
        out_specs=[tok(0)] * 3,
        compiler_params=pltpu.CompilerParams(vmem_limit_bytes=48 * 2**20),
    )(q, k, v, lse, d_att, *tables, docs[:, :, None], docs[:, None, :])


def inverse_rms(values):
    return lax.rsqrt(jnp.mean(values * values, axis=-1, keepdims=True) + eps_norm)


def rotation_tables(positions):
    half_dim = HEAD_DIM // 2
    frequency = rope_base ** (-jnp.arange(half_dim, dtype=f32) * 2.0 / HEAD_DIM)
    angles = positions.astype(f32)[:, None] * frequency[None, :]
    cosine, sine = jnp.cos(angles), jnp.sin(angles)
    return jnp.concatenate([cosine, cosine], 1), jnp.concatenate([-sine, sine], 1)


def wide_gather(block):
    return lax.all_gather(block, "wide", axis=0, tiled=True)


def wide_scatter(partial):
    return lax.psum_scatter(partial.astype(bf16), "wide", scatter_dimension=0, tiled=True)


def after(value, *others):
    return lax.optimization_barrier((value, *others))[0]


def on_device(n_w, n_s, inputs, documents, cotangent, query_weight, key_weight, value_weight, output_weight,
              query_gain, key_gain, attention_gain, gate_weight, up_weight, down_weight, feed_gain):
    micro, _, local, width = inputs.shape
    tokens = micro * local
    all_tokens = n_s * tokens
    n_dev = n_w * n_s
    heads = HEADS // n_s
    cols = heads * HEAD_DIM
    row_len = documents.shape[2]
    feed = gate_weight.shape[1]
    feed_block = feed // n_dev
    half = n_w * feed_block
    rows = query_weight.shape[0]
    scale = HEAD_DIM ** (-0.5)
    s_index = lax.axis_index("seq")

    flat = inputs.reshape(tokens, width)
    cot = cotangent.reshape(tokens, width)
    halves = 2 * rows == HEAD_DIM and n_w == 2 * heads

    def head_of(s, i):
        return s // 2 + n_s // 2 * (s % 2 * heads + i) if halves else s * heads + i

    def head_column(i):
        return lambda s: head_of(s, i) * HEAD_DIM

    qkv_plan = [[(head_column(h), HEAD_DIM, i * cols + h * HEAD_DIM) for h in range(heads)] for i in range(3)]
    own_blocks = feed_block % 128 == 0
    moves = [(b, (b % n_w) * n_s + b // n_w) for b in range(n_dev)]
    back_moves = [(b, a) for a, b in moves]
    if own_blocks:
        feed_plan = [[(lambda s, a=a: (a * n_s + s) * feed_block, feed_block, i * half + a * feed_block) for a in range(n_w)] for i in range(2)]
    else:
        feed_plan = [[(lambda s: s * half, half, i * half)] for i in range(2)]

    own_gain = jnp.stack([query_gain, key_gain, attention_gain, feed_gain]).astype(f32)
    own_gain = jnp.pad(own_gain, ((0, 4), (0, 128 - rows)))
    qkv = first_exchange((query_weight, key_weight, value_weight), qkv_plan, 3 * cols, n_s, 0)
    qkv_all = wide_gather(qkv.reshape(n_s * rows, 3 * cols))
    if not halves:
        out_all = wide_gather(lax.ppermute(output_weight, ("wide", "seq"), moves))
    x_all, gate_up, gains, *out_heads = second_exchange(
        after(flat, qkv), (gate_weight, up_weight), own_gain, output_weight if halves else None, feed_plan, 2 * half, n_w, n_s, 1
    )
    if halves:
        out_all = out_heads[0].reshape(cols, width)
    x_all = x_all.reshape(all_tokens, width)
    gate_up_all = wide_gather(gate_up.reshape(n_s * rows, 2 * half))
    down_block = down_weight
    if not own_blocks:
        down_block = lax.ppermute(down_block, ("wide", "seq"), moves)
    down_all = wide_gather(down_block)

    gains = jnp.swapaxes(gains[:, :4, :rows], 0, 1).reshape(4, width)

    def own_heads(v):
        return jnp.concatenate([lax.dynamic_slice_in_dim(v, head_of(s_index, i) * HEAD_DIM, HEAD_DIM, 1) for i in range(heads)], 1)

    own_gains = own_heads(gains)

    x_all, down_all = lax.optimization_barrier((x_all, down_all))
    lin = dot(x_all, qkv_all)
    q_lin, k_lin = lin[:, :cols], lin[:, cols : 2 * cols]

    def stack_sums(a, b):
        return jnp.stack([a, b] + [jnp.zeros_like(a)] * 6)

    sums = exchange(stack_sums(jnp.sum(q_lin * q_lin, 1), jnp.sum(k_lin * k_lin, 1)), n_w, n_s, False, 2)
    inv = lax.rsqrt(jnp.sum(sums, 0)[:2] / width + eps_norm).T
    tables = rotation_tables(jnp.arange(row_len, dtype=jnp.int32))
    docs = documents[:, 0, :]
    shape4 = (n_s, micro, local, -1)
    attended, q, k, v, lse = attend(lin.reshape(shape4), inv.reshape(shape4), own_gains, tables, docs, heads, scale)
    attended = attended.reshape(all_tokens, cols)

    own_f32 = ((tokens, width), f32)
    vec_f32 = ((1, width), f32)
    hidden_all, hidden, mixed_n, mixed_inv = around(
        dot(attended, out_all).astype(bf16), (flat, gains[2:3]), mixed_rows, [own_f32, own_f32, ((tokens, 1), f32)], n_s, 3, False
    )
    hidden_all = hidden_all.reshape(all_tokens, width)
    active, slope, swish = feed_forward(hidden_all, gate_up_all)
    d_down_all, layer_out, feed_term = around(
        dot(active, down_all).astype(bf16), (hidden, cot, gains[3:4]), down_rows, [((tokens, width), bf16), vec_f32], n_s, 4, True
    )
    d_down_all = d_down_all.reshape(all_tokens, width)
    d_gate_up = feed_back(d_down_all, down_all, slope, swish)
    mlp_part = t_dot(hidden_all, d_gate_up).astype(bf16)
    mlp_grad = wide_scatter(mlp_part)
    d_mixed_all, d_hidden, attention_term, down_part = around(
        dot_t(after(d_gate_up, mlp_part), gate_up_all).astype(bf16), (cot, mixed_n, mixed_inv, gains[2:3]), hidden_rows, [own_f32, vec_f32],
        n_s, 5, True, (active, d_down_all),
    )
    mlp_grad, d_mixed_all, down_part = lax.optimization_barrier((mlp_grad, d_mixed_all, down_part))
    down_grad = wide_scatter(down_part)
    d_mixed_all = d_mixed_all.reshape(all_tokens, width)
    out_part = t_dot(attended, d_mixed_all).astype(bf16)
    d_attended = dot_t(d_mixed_all, out_all).astype(bf16).reshape(shape4)

    d_q, d_k, d_v = attend_back(q, k, v, lse, d_attended, tables, docs, heads, scale)
    d_q, d_k, d_v = (t.reshape(all_tokens, cols) for t in (d_q, d_k, d_v))
    q_n, k_n = q_lin * inv[:, 0:1], k_lin * inv[:, 1:2]
    d_qg, d_kg = d_q * own_gains[0], d_k * own_gains[1]
    mean_sums = stack_sums(jnp.sum(d_qg * q_n, 1), jnp.sum(d_kg * k_n, 1))
    if halves:
        mean_sums, out_part = sums_exchange(mean_sums, out_part.reshape(heads, 2, rows, width), n_w, n_s, 6)
    else:
        mean_sums = exchange(mean_sums, n_w, n_s, False, 6)
    mean_sums, mlp_grad = lax.optimization_barrier((mean_sums, mlp_grad))
    mlp_grad = lax.all_to_all(mlp_grad, "seq", 0, 0, tiled=True)
    means = jnp.sum(mean_sums, 0)[:2].T / width
    query_term = jnp.sum(d_q * q_n, 0)
    key_term = jnp.sum(d_k * k_n, 0)
    d_q_lin = (inv[:, 0:1] * (d_qg - q_n * means[:, 0:1])).astype(bf16)
    d_k_lin = (inv[:, 1:2] * (d_kg - k_n * means[:, 1:2])).astype(bf16)
    d_lin = jnp.concatenate([d_q_lin, d_k_lin, d_v], axis=1)
    qkv_part = t_dot(x_all, d_lin).astype(bf16)
    d_hidden, down_grad = lax.optimization_barrier((d_hidden, down_grad))
    def spread(term):
        full = jnp.zeros((width,), f32)
        for i in range(heads):
            full = lax.dynamic_update_slice_in_dim(full, term[i * HEAD_DIM : (i + 1) * HEAD_DIM], head_of(s_index, i) * HEAD_DIM, 0)
        return full

    terms = jnp.stack([spread(query_term), spread(key_term), attention_term[0], feed_term[0]])
    terms = jnp.swapaxes(terms.reshape(4, n_dev, rows), 0, 1)
    terms = jnp.pad(terms, ((0, 0), (0, 4), (0, 128 - rows)))
    input_grad, all_terms = last_sum(dot_t(after(d_lin, qkv_part), qkv_all).astype(bf16), d_hidden, terms, n_w, n_s, 7)
    input_grad = input_grad.reshape(inputs.shape)
    qkv_grad = wide_scatter(qkv_part)
    out_grad = wide_scatter(after(out_part, qkv_grad, input_grad).reshape(cols, width))
    if not halves:
        out_grad = lax.ppermute(out_grad, ("wide", "seq"), back_moves)

    qkv_grad = final_exchange(after(qkv_grad, input_grad).reshape(n_s, rows, 3 * cols), n_w, n_s, 8)
    gate_grad, up_grad = unpack(mlp_grad.reshape(n_s, rows, 2 * half), feed, feed_plan)
    query_grad, key_grad, value_grad = unpack(qkv_grad, width, qkv_plan)
    gain_grads = jnp.sum(all_terms, 0)[:4, :rows]
    if not own_blocks:
        down_grad = lax.ppermute(down_grad, ("wide", "seq"), back_moves)
    return (layer_out.reshape(inputs.shape), input_grad, query_grad, key_grad, value_grad, out_grad.astype(f32),
            gain_grads[0], gain_grads[1], gain_grads[2], gate_grad, up_grad, down_grad.astype(f32), gain_grads[3])


def solution(mesh):
    tok = P(None, "wide", "seq", None)
    docs = P(None, "wide", None)
    mat = P(("wide", "seq"), None)
    vec = P(("wide", "seq"))

    def body(*args):
        return on_device(mesh.shape["wide"], mesh.shape["seq"], *args)

    return jax.shard_map(
        body,
        mesh=mesh,
        in_specs=(tok, docs, tok, mat, mat, mat, mat, vec, vec, vec, mat, mat, mat, vec),
        out_specs=(tok, tok, mat, mat, mat, mat, vec, vec, vec, mat, mat, mat, vec),
        check_vma=False,
    )
```

```python
import functools

import jax
import jax.numpy as jnp
from jax import lax
from jax.experimental import pallas as pl
from jax.experimental.pallas import tpu as pltpu
from jax.sharding import PartitionSpec as P

HEADS = 16
HEAD_DIM = 128
eps_norm = 1e-06
rope_base = 500000.0
masked_value = -1e30
bf16 = jnp.bfloat16
f32 = jnp.float32
MESH = pl.DeviceIdType.MESH
ANY = pl.BlockSpec(memory_space=pl.ANY)
VM = pl.BlockSpec(memory_space=pltpu.VMEM)
DMA = pltpu.SemaphoreType.DMA
PACE = 1
CHUNKS = 4
SUB = 4


def params(cid, megabytes=None):
    limit = {} if megabytes is None else {"vmem_limit_bytes": megabytes * 2**20}
    return pltpu.CompilerParams(collective_id=cid, has_side_effects=True, **limit)


def cost(microseconds):
    return pl.CostEstimate(flops=0, transcendentals=0, bytes_accessed=int(microseconds * 3e6))


def far_first(n_s):
    return sorted(range(n_s), key=lambda k: -min(k, n_s - k))


def remote(src, dst, send, recv, device):
    return pltpu.make_async_remote_copy(src, dst, send, recv, device_id=device, device_id_type=MESH)


def greet(targets):
    barrier = pltpu.get_barrier_semaphore()
    count = 0
    for cond, dev in targets:
        if cond is None:
            pl.semaphore_signal(barrier, inc=1, device_id=dev, device_id_type=MESH)
            count = count + 1
        else:

            @pl.when(cond)
            def _():
                pl.semaphore_signal(barrier, inc=1, device_id=dev, device_id_type=MESH)

            count = count + cond.astype(jnp.int32)
    pl.semaphore_wait(barrier, count)


class Line:
    def __init__(self, n_s):
        self.s = lax.axis_index("seq")
        self.nz = n_s // 2
        self.z, self.c = self.s // 2, self.s % 2
        self.mate_slot = self.s + 1 - 2 * self.c
        self.mate = {"seq": self.mate_slot}
        self.steps = (1, -1)
        self.more = (self.z < self.nz - 1, self.z > 0)
        self.next = ({"seq": self.s + 2}, {"seq": self.s - 2})

    def neighbours(self):
        return [(self.more[0], self.next[0]), (self.more[1], self.next[1]), (None, self.mate)]


class Gather:
    def __init__(self, line, own, out, chunks, send, recv, mate_send, mate_recv):
        self.line, self.own, self.out = line, own, out
        self.chunks, self.rows = chunks, own.shape[0] // chunks
        self.send, self.recv, self.mate_send, self.mate_recv = send, recv, mate_send, mate_recv

    def part(self, slot, k):
        return self.out.at[slot, pl.ds(k * self.rows, self.rows)]

    def source(self, d, k, slot):
        return self.own.at[pl.ds(k * self.rows, self.rows)] if d == 0 else self.part(slot, k)

    def hop(self, i, d, k, slot):
        return remote(self.source(d, k, slot), self.part(slot, k), self.send.at[i, d, k], self.recv.at[i, d, k], self.line.next[i])

    def share(self, i, d, k, slot):
        return remote(self.source(d, k, slot), self.part(slot, k), self.mate_send.at[i, d, k], self.mate_recv.at[i, d, k], self.line.mate)

    def start(self, k):
        line = self.line
        for i in range(2):

            @pl.when(line.more[i])
            def _():
                self.hop(i, 0, k, line.s).start()

        self.share(0, 0, k, line.s).start()

    def each(self, d, mine=True):
        line = self.line
        for i in range(2):
            origin = line.z - line.steps[i] * d
            yield i, (origin >= 0) & (origin < line.nz), 2 * origin + (line.c if mine else 1 - line.c)

    def pass_on(self, d, k):
        for i, there, slot in self.each(d):

            @pl.when(there)
            def _():
                self.hop(i, d - 1, k, slot).wait_recv()
                if d < self.line.nz - 1:

                    @pl.when(self.line.more[i])
                    def _():
                        self.hop(i, d, k, slot).start()

                self.share(i, d, k, slot).start()

    def finish(self):
        line = self.line
        for k in range(self.chunks):
            self.share(0, 0, k, line.mate_slot).wait_recv()
            for d in range(1, line.nz):
                for i, there, slot in self.each(d, False):

                    @pl.when(there)
                    def _():
                        self.share(i, d, k, slot).wait_recv()

        for k in range(self.chunks):
            self.share(0, 0, k, line.s).wait_send()
            for i in range(2):

                @pl.when(line.more[i])
                def _():
                    self.hop(i, 0, k, line.s).wait_send()

            for d in range(1, line.nz):
                for i, there, slot in self.each(d):

                    @pl.when(there)
                    def _():
                        self.share(i, d, k, slot).wait_send()
                        if d < line.nz - 1:

                            @pl.when(line.more[i])
                            def _():
                                self.hop(i, d, k, slot).wait_send()


class Scatter:
    def __init__(self, line, part, from_mate, run, chunks, send, recv, mate_send, mate_recv):
        self.line, self.part, self.from_mate, self.run = line, part, from_mate, run
        self.chunks, self.rows = chunks, part.shape[1] // chunks
        self.send, self.recv, self.mate_send, self.mate_recv = send, recv, mate_send, mate_recv
        self.steps = line.nz - 1
        self.groups = chunks // SUB
        self.count = self.steps * self.groups

    def span(self, k):
        return pl.ds(pl.multiple_of(k * self.rows, self.rows), self.rows)

    def give(self, zd, k):
        line, rs = self.line, self.span(k)
        return remote(self.part.at[2 * zd + 1 - line.c, rs], self.from_mate.at[zd, rs], self.mate_send.at[zd, k], self.mate_recv.at[zd, k], line.mate)

    def hop(self, i, zd, k):
        ref = self.run.at[i, zd, self.span(k)]
        return remote(ref, ref, self.send.at[i, zd, k], self.recv.at[i, zd, k], self.line.next[i])

    def pair(self, zd, k):
        rs = self.span(k)
        return self.part[2 * zd + self.line.c, rs].astype(f32) + self.from_mate[zd, rs].astype(f32)

    def start(self, k):
        nz = self.line.nz
        for zd in sorted(range(nz), key=lambda zd: (min(zd, nz - 1 - zd), -zd)):
            self.give(zd, k).start()

    def item(self, i, q, j):
        group, step = q // self.steps, lax.rem(q, self.steps)
        return (self.line.nz - 1 - step if i == 0 else step), group * SUB + j

    def slot(self, t):
        line = self.line
        for j, i in ((j, i) for j in range(SUB) for i in range(2)):
            q = t - (line.z if i == 0 else line.nz - 1 - line.z)
            behind = line.z > 0 if i == 0 else line.z < line.nz - 1
            zd, k = self.item(i, jnp.clip(q, 0, self.count - 1), j)
            going = (q >= 0) & (q < self.count) & (line.z < zd if i == 0 else line.z > zd)

            @pl.when(going)
            def _():
                rs = self.span(k)
                self.give(zd, k).wait_recv()

                @pl.when(behind)
                def _():
                    self.hop(i, zd, k).wait_recv()
                    self.run[i, zd, rs] = (self.pair(zd, k) + self.run[i, zd, rs].astype(f32)).astype(bf16)

                @pl.when(jnp.logical_not(behind))
                def _():
                    self.run[i, zd, rs] = self.pair(zd, k).astype(bf16)
                    if t >= PACE:
                        self.hop(i, *self.item(i, jnp.int32(t - PACE), j)).wait_send()

                self.hop(i, zd, k).start()

    def total(self, k, use):
        line, rs = self.line, self.span(k)
        for zd in range(line.nz):

            @pl.when(line.z == zd)
            def _():
                self.give(zd, k).wait_recv()
                total = self.pair(zd, k)
                if zd > 0:
                    self.hop(0, zd, k).wait_recv()
                    total = total + self.run[0, zd, rs].astype(f32)
                if zd < line.nz - 1:
                    self.hop(1, zd, k).wait_recv()
                    total = total + self.run[1, zd, rs].astype(f32)
                use(total)

    def finish(self):
        line = self.line
        for k in range(self.chunks):
            for zd in range(line.nz):
                self.give(zd, k).wait_send()
        for q in range(self.count):
            step = q % self.steps
            for i, zd in ((0, line.nz - 1 - step), (1, step)):
                going = line.z < zd if i == 0 else line.z > zd
                behind = line.z > 0 if i == 0 else line.z < line.nz - 1

                @pl.when(going & behind if q < self.count - PACE else going)
                def _():
                    for j in range(SUB):
                        self.hop(i, zd, q // self.steps * SUB + j).wait_send()


def line_sems(nz, chunks):
    return [DMA((2, nz, chunks))] * 4


def scatter_scratch(n_s, rows, width, chunks):
    nz = n_s // 2
    sums = [pltpu.VMEM((nz, rows, width), bf16), pltpu.VMEM((2, nz, rows, width), bf16)]
    return sums + [DMA((2, nz, chunks))] * 2 + [DMA((nz, chunks))] * 2


def mixed_rows(rs, total, x, gain, hidden, normed, inverse, low):
    inv = inverse_rms(total)
    n = total * inv
    out = x[rs].astype(f32) + n * gain[...]
    hidden[rs] = out
    normed[rs] = n
    inverse[rs] = inv
    low[rs] = out.astype(bf16)


def down_rows(rs, total, hidden, cotangent, gain, out, term, low):
    inv = inverse_rms(total)
    n = total * inv
    g = gain[...]
    out[rs] = (hidden[rs] + n * g).astype(bf16)
    grad = cotangent[rs].astype(f32)
    low[rs], more = back_rows(grad, n, inv, g)
    term[...] += more


def hidden_rows(rs, total, cotangent, normed, inverse, gain, d_hidden, term, low):
    grad = cotangent[rs].astype(f32) + total
    d_hidden[rs] = grad
    low[rs], more = back_rows(grad, normed[rs], inverse[rs], gain[...])
    term[...] += more


def back_rows(grad, n, inv, gain):
    scaled = grad * gain
    d = inv * (scaled - n * jnp.mean(scaled * n, axis=-1, keepdims=True))
    return d.astype(bf16), jnp.sum(grad * n, axis=0, keepdims=True)


def run_slots(scatter, use, gather=None, work=None):
    steps, groups = scatter.steps, scatter.groups
    slots = steps * (groups + (1 if gather else 0)) + 1
    for t in range(slots):
        if t < steps * (groups + 1):
            scatter.slot(t)
        if gather:
            for group in range(groups):
                if 1 <= t - steps * (group + 1) <= steps:
                    for j in range(SUB):
                        gather.pass_on(t - steps * (group + 1), group * SUB + j)
        if t and t % steps == 0 and t // steps <= groups:
            for k in range((t // steps - 1) * SUB, t // steps * SUB):
                scatter.total(k, lambda total: use(k, total))
                if gather:
                    gather.start(k)
        if work:
            work(t, slots)


def product_work(left, right, out):
    size = 128
    count = out.shape[0] // size

    def work(t, slots):
        for i in range(count * t // slots, count * (t + 1) // slots):
            rs = pl.ds(i * size, size)
            out[rs] = lax.dot_general(left[:, rs], right[...], (((0,), (0,)), ((), ())), preferred_element_type=f32).astype(bf16)

    return work


def around_kernel(n_s, chunks, rows_fn, n_in, n_out, adds, with_work, *refs):
    part, extra = refs[0], refs[1 : 1 + n_in]
    refs = refs[1 + n_in :]
    work = None
    if with_work:
        left, right, gathered, *outs, made = refs[: 4 + n_out]
        work = product_work(left, right, made)
        refs = refs[4 + n_out :]
    else:
        gathered, *outs = refs[: 1 + n_out]
        refs = refs[1 + n_out :]
    low, local, from_mate, run, *sems = refs
    line = Line(n_s)
    scatter = Scatter(line, part, from_mate, run, chunks, *sems[:4])
    gather = Gather(line, low, gathered, chunks, *sems[4:])
    greet(line.neighbours())
    for k in range(chunks):
        scatter.start(k)
    if adds:
        outs[-1][...] = jnp.zeros_like(outs[-1])
    run_slots(scatter, lambda k, total: rows_fn(scatter.span(k), total, *extra, *outs, low), gather, work)
    own = pltpu.make_async_copy(low, gathered.at[line.s], local)
    own.start()
    gather.finish()
    scatter.finish()
    own.wait()


def around(terms, extra, rows_fn, outs, n_s, cid, adds, pair=(), chunks=CHUNKS):
    rows, width = terms.shape[0] // n_s, terms.shape[1]
    shapes = [((n_s, rows, width), bf16), *outs] + ([((pair[0].shape[1], pair[1].shape[1]), bf16)] if pair else [])
    return pl.pallas_call(
        functools.partial(around_kernel, n_s, chunks, rows_fn, len(extra), len(outs), adds, bool(pair)),
        out_shape=[jax.ShapeDtypeStruct(*o) for o in shapes],
        in_specs=[VM] * (1 + len(extra) + len(pair)),
        out_specs=[ANY] + [VM] * (len(shapes) - 1),
        scratch_shapes=[pltpu.VMEM((rows, width), bf16), DMA] + scatter_scratch(n_s, rows, width, chunks) + line_sems(n_s // 2, chunks),
        compiler_params=params(cid, 48),
        cost_estimate=cost(70),
    )(terms.reshape(n_s, rows, width), *extra, *pair)


def last_kernel(n_w, n_s, chunks, part, d_hidden, terms, out, all_terms, from_mate, run, *sems):
    line = Line(n_s)
    scatter = Scatter(line, part, from_mate, run, chunks, *sems[:4])
    share = Share(n_w, n_s, True, terms, all_terms, *sems[4:])
    greet(share.others())
    for k in range(chunks):
        scatter.start(k)

    def use(k, total):
        out[scatter.span(k)] = d_hidden[scatter.span(k)] + total

    share.start()
    run_slots(scatter, use)
    scatter.finish()
    share.finish()


def last_sum(part, d_hidden, terms, n_w, n_s, cid, chunks=CHUNKS):
    rows, width = part.shape[0] // n_s, part.shape[1]
    count = n_w * n_s
    return pl.pallas_call(
        functools.partial(last_kernel, n_w, n_s, chunks),
        out_shape=[jax.ShapeDtypeStruct((rows, width), f32), jax.ShapeDtypeStruct(terms.shape, terms.dtype)],
        in_specs=[VM] * 3,
        out_specs=[VM] * 2,
        scratch_shapes=scatter_scratch(n_s, rows, width, chunks) + [DMA((count,)), DMA((count,)), DMA],
        compiler_params=params(cid, 48),
        cost_estimate=cost(40),
    )(part.reshape(n_s, rows, width), d_hidden, terms)


class Columns:
    def __init__(self, n_s, plan, arrays, slots, back, send, recv, local):
        self.n_s, self.plan, self.arrays, self.slots, self.back = n_s, plan, arrays, slots, back
        self.send, self.recv, self.local = send, recv, local
        self.s = lax.axis_index("seq")

    def place(self, k):
        return lax.rem(self.s + k, self.n_s)

    def pieces(self, k):
        there = self.place(k)
        for array, parts in zip(self.arrays, self.plan):
            for first, width, column in parts:
                at = pl.ds(column, width)
                if self.back:
                    yield self.slots.at[there, :, at], array.at[:, pl.ds(pl.multiple_of(first(self.s), 128), width)]
                else:
                    yield array.at[:, pl.ds(pl.multiple_of(first(there), 128), width)], self.slots.at[self.s, :, at]

    def start(self):
        for k in far_first(self.n_s)[:-1]:
            for src, dst in self.pieces(k):
                remote(src, dst, self.send.at[k], self.recv.at[k], {"seq": self.place(k)}).start()
        for src, dst in self.pieces(0):
            pltpu.make_async_copy(src, dst, self.local).start()

    def finish(self):
        slot = self.slots.at[0]
        for k in range(1, self.n_s):
            done = remote(slot, slot, self.send.at[k], self.recv.at[k], {"seq": self.place(k)})
            done.wait_recv()
            done.wait_send()
        pltpu.make_async_copy(slot, slot, self.local).wait()


def columns_sems(n_s):
    return [DMA((n_s,)), DMA((n_s,)), DMA]


def seq_others(n_s):
    s = lax.axis_index("seq")
    return [(None, {"seq": lax.rem(s + k, n_s)}) for k in range(1, n_s)]


class Share:
    def __init__(self, n_w, n_s, whole, x, out, send, recv, local):
        self.n_w, self.n_s, self.whole = n_w, n_s, whole
        self.x, self.out, self.send, self.recv, self.local = x, out, send, recv, local
        self.w, self.s = lax.axis_index("wide"), lax.axis_index("seq")
        self.steps = [(a, b) for b in far_first(n_s) for a in (range(n_w) if whole else (0,)) if a or b]

    def at(self, a, b):
        return lax.rem(self.w + a, self.n_w), lax.rem(self.s + b, self.n_s)

    def number(self, a, b):
        w, s = self.at(a, b)
        return w * self.n_s + s if self.whole else s

    def name(self, a, b):
        w, s = self.at(a, b)
        return {"wide": w, "seq": s}

    def others(self):
        return [(None, self.name(a, b)) for a, b in self.steps]

    def block(self, a, b):
        return self.x.at[self.number(a, b)] if len(self.x.shape) == 3 else self.x

    def copy(self, a, b):
        i = a * self.n_s + b
        return remote(self.block(a, b), self.out.at[self.number(0, 0)], self.send.at[i], self.recv.at[i], self.name(a, b))

    def own(self):
        return pltpu.make_async_copy(self.block(0, 0), self.out.at[self.number(0, 0)], self.local)

    def start(self):
        for a, b in self.steps:
            self.copy(a, b).start()
        self.own().start()

    def finish(self):
        for a, b in self.steps:
            self.copy(a, b).wait()
        self.own().wait()


def share_kernel(n_w, n_s, whole, x_ref, o_ref, send, recv, local_sem):
    share = Share(n_w, n_s, whole, x_ref, o_ref, send, recv, local_sem)
    greet(share.others())
    share.start()
    share.finish()


def exchange(x, n_w, n_s, whole, cid):
    count = n_w * n_s if whole else n_s
    return pl.pallas_call(
        functools.partial(share_kernel, n_w, n_s, whole),
        out_shape=jax.ShapeDtypeStruct((count, *x.shape[-2:]), x.dtype),
        in_specs=[VM],
        out_specs=VM,
        scratch_shapes=[DMA((count,)), DMA((count,)), DMA],
        compiler_params=params(cid),
        cost_estimate=cost(10),
    )(x)


class Halves:
    def __init__(self, n_w, natural, heads, send, recv, local):
        s = lax.axis_index("seq")
        c = lax.rem(s, 2)
        mate = {"seq": s + 1 - 2 * c}
        self.copies = []
        for i in range(n_w // 2):
            there = natural.at[c * (n_w // 2) + i]
            self.copies.append(remote(heads.at[i, 1 - c], there, send.at[i], recv.at[i], mate))
            self.copies.append(pltpu.make_async_copy(heads.at[i, c], there, local.at[i]))

    def start(self):
        for copy in self.copies:
            copy.start()

    def finish(self):
        for copy in self.copies:
            copy.wait()


def halves_sems(n_w):
    return [DMA((n_w // 2,))] * 3


def first_kernel(n_s, plan, qw, kw, vw, qkv, *sems):
    columns = Columns(n_s, plan, (qw, kw, vw), qkv, False, *sems)
    greet(seq_others(n_s))
    columns.start()
    columns.finish()


def first_exchange(weights, plan, cols, n_s, cid):
    return pl.pallas_call(
        functools.partial(first_kernel, n_s, plan),
        out_shape=jax.ShapeDtypeStruct((n_s, weights[0].shape[0], cols), bf16),
        in_specs=[ANY] * 3,
        out_specs=ANY,
        scratch_shapes=columns_sems(n_s),
        compiler_params=params(cid),
        cost_estimate=cost(20),
    )(*weights)


class Heads:
    def __init__(self, n_w, block, heads, send, recv, local):
        w, s = lax.axis_index("wide"), lax.axis_index("seq")
        half = n_w // 2
        c = lax.rem(s, 2)
        core = w // half
        self.lane = core == c
        dst = heads.at[lax.rem(w, half), c]
        self.sends = []
        for k in range(n_w):
            device = {"wide": lax.rem(w + k, n_w), "seq": s - c + core}
            self.sends.append(remote(block, dst, send.at[k], recv.at[lax.rem(w, half), c], device))
        self.stay = pltpu.make_async_copy(block, dst, local)
        self.arrivals = []
        for i in range(half):
            for there in range(2):
                own = self.lane & (lax.rem(w, half) == i) & (c == there)
                ref = heads.at[i, there]
                self.arrivals.append((jnp.logical_not(own), remote(ref, ref, send.at[0], recv.at[i, there], {"seq": s + 1 - 2 * c})))

    def start(self):
        for copy in self.sends[1:]:
            copy.start()

        @pl.when(self.lane)
        def _():
            self.stay.start()

        @pl.when(jnp.logical_not(self.lane))
        def _():
            self.sends[0].start()

    def finish(self):
        for come, copy in self.arrivals:

            @pl.when(come)
            def _():
                copy.wait_recv()

        for copy in self.sends[1:]:
            copy.wait_send()

        @pl.when(self.lane)
        def _():
            self.stay.wait()

        @pl.when(jnp.logical_not(self.lane))
        def _():
            self.sends[0].wait_send()


def second_kernel(n_w, n_s, chunks, plan, heads, x, gw, uw, gain, *refs):
    if heads:
        out_block, x_all, slots, gains, out_heads, own_sem, *sems = refs
    else:
        x_all, slots, gains, own_sem, *sems = refs
    line = Line(n_s)
    gather = Gather(line, x, x_all, chunks, *sems[:4])
    others = [Share(n_w, n_s, True, gain, gains, *sems[4:7])]
    if heads:
        others.append(Heads(n_w, out_block, out_heads, *sems[7:10]))
    others.append(Columns(n_s, plan, (gw, uw), slots, False, *sems[-3:]))
    greet(others[0].others())
    own = pltpu.make_async_copy(x, x_all.at[line.s], own_sem)
    for k in range(chunks):
        gather.start(k)
    own.start()
    for other in others:
        other.start()
    for d in range(1, line.nz):
        for k in range(chunks):
            gather.pass_on(d, k)
    gather.finish()
    own.wait()
    for other in others:
        other.finish()


def second_exchange(x, weights, gain, out_block, plan, cols, n_w, n_s, cid, chunks=4):
    rows, width = x.shape
    count = n_w * n_s
    shapes = [((n_s, rows, width), bf16), ((n_s, weights[0].shape[0], cols), bf16), ((count, *gain.shape), gain.dtype)]
    sems = [DMA] + line_sems(n_s // 2, chunks) + [DMA((count,)), DMA((count,)), DMA]
    extra = []
    if out_block is not None:
        extra = [out_block]
        shapes.append(((n_w // 2, 2, *out_block.shape), bf16))
        sems += [DMA((n_w,)), DMA((n_w // 2, 2)), DMA]
    return pl.pallas_call(
        functools.partial(second_kernel, n_w, n_s, chunks, plan, bool(extra)),
        out_shape=[jax.ShapeDtypeStruct(*o) for o in shapes],
        in_specs=[ANY] * 3 + [VM] + [ANY] * len(extra),
        out_specs=[ANY, ANY, VM] + [ANY] * len(extra),
        scratch_shapes=sems + columns_sems(n_s),
        compiler_params=params(cid),
        cost_estimate=cost(80),
    )(x, *weights, gain, *extra)


def unpack_kernel(n_s, plan, slots, *outs):
    for out, pieces in zip(outs, plan):
        for first, width, column in pieces:
            for s in range(n_s):
                out[:, first(s) : first(s) + width] = slots[s, :, column : column + width].astype(f32)


def unpack(slots, width, plan):
    n_s, rows, _ = slots.shape
    return pl.pallas_call(
        functools.partial(unpack_kernel, n_s, plan),
        out_shape=[jax.ShapeDtypeStruct((rows, width), f32)] * len(plan),
        in_specs=[VM],
        out_specs=[VM] * len(plan),
        compiler_params=pltpu.CompilerParams(vmem_limit_bytes=40 * 2**20),
        cost_estimate=cost(4),
    )(slots)


def sums_kernel(n_w, n_s, x, heads, all_x, natural, *sems):
    share = Share(n_w, n_s, False, x, all_x, *sems[:3])
    halves = Halves(n_w, natural, heads, *sems[3:])
    greet(share.others())
    share.start()
    halves.start()
    share.finish()
    halves.finish()


def sums_exchange(x, heads, n_w, n_s, cid):
    return pl.pallas_call(
        functools.partial(sums_kernel, n_w, n_s),
        out_shape=[jax.ShapeDtypeStruct((n_s, *x.shape), x.dtype), jax.ShapeDtypeStruct((n_w, *heads.shape[2:]), bf16)],
        in_specs=[VM, VM],
        out_specs=[VM, VM],
        scratch_shapes=[DMA((n_s,)), DMA((n_s,)), DMA] + halves_sems(n_w),
        compiler_params=params(cid),
        cost_estimate=cost(10),
    )(x, heads)


def final_kernel(n_w, n_s, qkv, qkv_own, *sems):
    share = Share(n_w, n_s, False, qkv, qkv_own, *sems)
    greet(seq_others(n_s))
    share.start()
    share.finish()


def final_exchange(qkv, n_w, n_s, cid):
    return pl.pallas_call(
        functools.partial(final_kernel, n_w, n_s),
        out_shape=jax.ShapeDtypeStruct(qkv.shape, qkv.dtype),
        in_specs=[ANY],
        out_specs=ANY,
        scratch_shapes=[DMA((n_s,)), DMA((n_s,)), DMA],
        compiler_params=params(cid),
        cost_estimate=cost(20),
    )(qkv)


def feed_kernel(hidden, gate_w, up_w, active, slope, swish):
    rows = hidden.shape[0] // 4
    for i in range(4):
        rs = pl.ds(i * rows, rows)
        gate, up = dot(hidden[rs], gate_w[...]), dot(hidden[rs], up_w[...])
        sigma = jax.nn.sigmoid(gate)
        silu = gate * sigma
        active[rs] = (silu * up).astype(bf16)
        slope[rs] = (up * sigma * (1.0 + gate * (1.0 - sigma))).astype(bf16)
        swish[rs] = silu.astype(bf16)


def feed_forward(hidden, weights, tile=256):
    tokens, width = hidden.shape
    half = weights.shape[1] // 2
    steps = half // tile
    out = pl.BlockSpec((tokens, tile), lambda j: (0, j))
    return pl.pallas_call(
        feed_kernel,
        grid=(steps,),
        out_shape=[jax.ShapeDtypeStruct((tokens, half), bf16)] * 3,
        in_specs=[
            pl.BlockSpec((tokens, width), lambda j: (0, 0)),
            pl.BlockSpec((width, tile), lambda j: (0, j)),
            pl.BlockSpec((width, tile), lambda j: (0, j + steps)),
        ],
        out_specs=[out] * 3,
        compiler_params=pltpu.CompilerParams(vmem_limit_bytes=48 * 2**20),
        cost_estimate=pl.CostEstimate(flops=4 * tokens * width * half, transcendentals=0, bytes_accessed=2 * (tokens * width + 2 * width * half)),
    )(hidden, weights, weights)


def feed_back_kernel(d_down, down_w, slope, swish, out):
    tile = down_w.shape[0]
    half = out.shape[1] // 2
    d_active = dot_t(d_down[...], down_w[...])
    at = pl.multiple_of(pl.program_id(0) * tile, tile)
    out[:, pl.ds(at, tile)] = (d_active * slope[...].astype(f32)).astype(bf16)
    out[:, pl.ds(pl.multiple_of(at + half, tile), tile)] = (d_active * swish[...].astype(f32)).astype(bf16)


def feed_back(d_down, down_w, slope, swish, tile=512):
    tokens, width = d_down.shape
    half = down_w.shape[0]
    cols = pl.BlockSpec((tokens, tile), lambda j: (0, j))
    return pl.pallas_call(
        feed_back_kernel,
        grid=(half // tile,),
        out_shape=jax.ShapeDtypeStruct((tokens, 2 * half), bf16),
        in_specs=[pl.BlockSpec((tokens, width), lambda j: (0, 0)), pl.BlockSpec((tile, width), lambda j: (j, 0)), cols, cols],
        out_specs=pl.BlockSpec((tokens, 2 * half), lambda j: (0, 0)),
        compiler_params=pltpu.CompilerParams(vmem_limit_bytes=48 * 2**20),
        cost_estimate=pl.CostEstimate(flops=2 * tokens * width * half, transcendentals=0, bytes_accessed=2 * (tokens * width + width * half)),
    )(d_down, down_w, slope, swish)


def rows_kernel(a, b, out):
    out[...] = lax.dot_general(a[...], b[...], (((1,), (1,)), ((), ())), preferred_element_type=f32).astype(bf16)


def columns_product(a, b, tile=512):
    (m, k), n = a.shape, b.shape[0]
    return pl.pallas_call(
        rows_kernel,
        grid=(n // tile,),
        out_shape=jax.ShapeDtypeStruct((m, n), bf16),
        in_specs=[pl.BlockSpec((m, k), lambda j: (0, 0)), pl.BlockSpec((tile, k), lambda j: (j, 0))],
        out_specs=pl.BlockSpec((m, tile), lambda j: (0, j)),
        compiler_params=pltpu.CompilerParams(vmem_limit_bytes=48 * 2**20),
        cost_estimate=pl.CostEstimate(flops=2 * m * n * k, transcendentals=0, bytes_accessed=2 * (m * k + k * n + m * n)),
    )(a, b)


def terms_kernel(a, b, out):
    out[...] = lax.dot_general(a[...], b[...], (((0,), (0,)), ((), ())), preferred_element_type=f32).astype(bf16)


def weight_product(a, b, tile=512):
    (k, m), n = a.shape, b.shape[1]
    return pl.pallas_call(
        terms_kernel,
        grid=(m // tile,),
        out_shape=jax.ShapeDtypeStruct((m, n), bf16),
        in_specs=[pl.BlockSpec((k, tile), lambda i: (0, i)), pl.BlockSpec((k, n), lambda i: (0, 0))],
        out_specs=pl.BlockSpec((tile, n), lambda i: (i, 0)),
        compiler_params=pltpu.CompilerParams(vmem_limit_bytes=48 * 2**20),
        cost_estimate=pl.CostEstimate(flops=2 * m * n * k, transcendentals=0, bytes_accessed=2 * (m * k + k * n + m * n)),
    )(a, b)


def dot(a, b):
    return jnp.dot(a, b, preferred_element_type=f32)


def dot_t(a, b):
    return lax.dot_general(a, b, (((1,), (1,)), ((), ())), preferred_element_type=f32)


def t_dot(a, b):
    return lax.dot_general(a, b, (((0,), (0,)), ((), ())), preferred_element_type=f32)


def turn(v, cosine, sine):
    return v * cosine + pltpu.roll(v, HEAD_DIM // 2, 1) * sine


def allowed_pairs(doc_q, doc_k, length):
    rows = lax.broadcasted_iota(jnp.int32, (length, length), 0)
    cols = lax.broadcasted_iota(jnp.int32, (length, length), 1)
    return (cols <= rows) & (doc_q == doc_k)


def attend_kernel(scale, ql, kl, vl, inv, gq, gk, cos, sin, doc_q, doc_k, att, q_out, k_out, v_out, lse):
    length = cos.shape[0]

    def flat(ref):
        return ref[...].reshape(length, -1)

    scales = flat(inv)
    q = turn(flat(ql) * scales[:, 0:1] * gq[...], cos[...], sin[...]).astype(bf16)
    k = turn(flat(kl) * scales[:, 1:2] * gk[...], cos[...], sin[...]).astype(bf16)
    v = flat(vl).astype(bf16)
    q_out[...] = q.reshape(q_out.shape)
    k_out[...] = k.reshape(k_out.shape)
    v_out[...] = v.reshape(v_out.shape)
    allowed = allowed_pairs(doc_q[0], doc_k[0], length)
    scores = jnp.where(allowed, dot_t(q, k) * scale, masked_value)
    top = jnp.max(scores, 1, keepdims=True)
    e = jnp.exp(scores - top)
    total = jnp.sum(e, 1, keepdims=True)
    probs = (e * (1.0 / total)).astype(bf16)
    att[...] = dot(probs, v).astype(bf16).reshape(att.shape)
    lse[...] = (top + jnp.log(total)).reshape(lse.shape)


def attend_back_kernel(scale, q, k, v, lse, da, cos, sin, doc_q, doc_k, dq_out, dk_out, dv_out):
    length = cos.shape[0]

    def flat(ref):
        return ref[...].reshape(length, -1)

    queries, keys, values, d_att = flat(q), flat(k), flat(v), flat(da)
    allowed = allowed_pairs(doc_q[0], doc_k[0], length)
    scores = jnp.where(allowed, dot_t(queries, keys) * scale, masked_value)
    probs = jnp.exp(scores - flat(lse))
    d_probs = dot_t(d_att, values)
    delta = jnp.sum(probs * d_probs, 1, keepdims=True)
    d_scores = (probs * (d_probs - delta)).astype(bf16)
    d_q = dot(d_scores, keys) * scale
    d_k = t_dot(d_scores, queries) * scale
    dv_out[...] = t_dot(probs.astype(bf16), d_att).astype(bf16).reshape(dv_out.shape)
    dq_out[...] = turn(d_q, cos[...], -sin[...]).reshape(dq_out.shape)
    dk_out[...] = turn(d_k, cos[...], -sin[...]).reshape(dk_out.shape)


def attention_specs(n_s, local, length):
    def tok(first):
        return pl.BlockSpec((n_s, 1, local, HEAD_DIM), lambda m, h: (0, m, 0, first + h))

    gain = pl.BlockSpec((1, HEAD_DIM), lambda m, h: (0, h))
    table = pl.BlockSpec((length, HEAD_DIM), lambda m, h: (0, 0))
    doc_q = pl.BlockSpec((1, length, 1), lambda m, h: (m, 0, 0))
    doc_k = pl.BlockSpec((1, 1, length), lambda m, h: (m, 0, 0))
    col = pl.BlockSpec((1, n_s, 1, local, 1), lambda m, h: (h, 0, m, 0, 0))
    return tok, gain, table, doc_q, doc_k, col


def attend(lin, inv, gains, tables, docs, heads, scale):
    n_s, micro, local, _ = lin.shape
    length = n_s * local
    tok, gain, table, doc_q, doc_k, col = attention_specs(n_s, local, length)
    inv_spec = pl.BlockSpec((n_s, 1, local, 2), lambda m, h: (0, m, 0, 0))
    out = jax.ShapeDtypeStruct((n_s, micro, local, heads * HEAD_DIM), bf16)
    return pl.pallas_call(
        functools.partial(attend_kernel, scale),
        grid=(micro, heads),
        out_shape=[out, out, out, out, jax.ShapeDtypeStruct((heads, n_s, micro, local, 1), f32)],
        in_specs=[tok(0), tok(heads), tok(2 * heads), inv_spec, gain, gain, table, table, doc_q, doc_k],
        out_specs=[tok(0)] * 4 + [col],
        compiler_params=pltpu.CompilerParams(vmem_limit_bytes=48 * 2**20),
    )(lin, lin, lin, inv, gains[0:1], gains[1:2], *tables, docs[:, :, None], docs[:, None, :])


def attend_back(q, k, v, lse, d_att, tables, docs, heads, scale):
    n_s, micro, local, width = q.shape
    length = n_s * local
    tok, gain, table, doc_q, doc_k, col = attention_specs(n_s, local, length)
    return pl.pallas_call(
        functools.partial(attend_back_kernel, scale),
        grid=(micro, heads),
        out_shape=[jax.ShapeDtypeStruct(q.shape, f32)] * 2 + [jax.ShapeDtypeStruct(q.shape, bf16)],
        in_specs=[tok(0)] * 3 + [col, tok(0), table, table, doc_q, doc_k],
        out_specs=[tok(0)] * 3,
        compiler_params=pltpu.CompilerParams(vmem_limit_bytes=48 * 2**20),
    )(q, k, v, lse, d_att, *tables, docs[:, :, None], docs[:, None, :])


def inverse_rms(values):
    return lax.rsqrt(jnp.mean(values * values, axis=-1, keepdims=True) + eps_norm)


def rotation_tables(positions):
    half_dim = HEAD_DIM // 2
    frequency = rope_base ** (-jnp.arange(half_dim, dtype=f32) * 2.0 / HEAD_DIM)
    angles = positions.astype(f32)[:, None] * frequency[None, :]
    cosine, sine = jnp.cos(angles), jnp.sin(angles)
    return jnp.concatenate([cosine, cosine], 1), jnp.concatenate([-sine, sine], 1)


def wide_gather(block):
    return lax.all_gather(block, "wide", axis=0, tiled=True)


def wide_scatter(partial):
    return lax.psum_scatter(partial.astype(bf16), "wide", scatter_dimension=0, tiled=True)


def after(value, *others):
    return lax.optimization_barrier((value, *others))[0]


def on_device(n_w, n_s, inputs, documents, cotangent, query_weight, key_weight, value_weight, output_weight,
              query_gain, key_gain, attention_gain, gate_weight, up_weight, down_weight, feed_gain):
    micro, _, local, width = inputs.shape
    tokens = micro * local
    all_tokens = n_s * tokens
    n_dev = n_w * n_s
    heads = HEADS // n_s
    cols = heads * HEAD_DIM
    row_len = documents.shape[2]
    feed = gate_weight.shape[1]
    feed_block = feed // n_dev
    half = n_w * feed_block
    rows = query_weight.shape[0]
    scale = HEAD_DIM ** (-0.5)
    s_index = lax.axis_index("seq")

    flat = inputs.reshape(tokens, width)
    cot = cotangent.reshape(tokens, width)
    halves = 2 * rows == HEAD_DIM and n_w == 2 * heads

    def head_of(s, i):
        return s // 2 + n_s // 2 * (s % 2 * heads + i) if halves else s * heads + i

    def head_column(i):
        return lambda s: head_of(s, i) * HEAD_DIM

    qkv_plan = [[(head_column(h), HEAD_DIM, i * cols + h * HEAD_DIM) for h in range(heads)] for i in range(3)]
    own_blocks = feed_block % 128 == 0
    moves = [(b, (b % n_w) * n_s + b // n_w) for b in range(n_dev)]
    back_moves = [(b, a) for a, b in moves]
    if own_blocks:
        feed_plan = [[(lambda s, a=a: (a * n_s + s) * feed_block, feed_block, i * half + a * feed_block) for a in range(n_w)] for i in range(2)]
    else:
        feed_plan = [[(lambda s: s * half, half, i * half)] for i in range(2)]

    own_gain = jnp.stack([query_gain, key_gain, attention_gain, feed_gain]).astype(f32)
    own_gain = jnp.pad(own_gain, ((0, 4), (0, 128 - rows)))
    qkv = first_exchange((query_weight, key_weight, value_weight), qkv_plan, 3 * cols, n_s, 0)
    qkv_all = wide_gather(qkv.reshape(n_s * rows, 3 * cols))
    if not halves:
        out_all = wide_gather(lax.ppermute(output_weight, ("wide", "seq"), moves))
    x_all, gate_up, gains, *out_heads = second_exchange(
        after(flat, qkv), (gate_weight, up_weight), own_gain, output_weight if halves else None, feed_plan, 2 * half, n_w, n_s, 1
    )
    if halves:
        out_all = out_heads[0].reshape(cols, width)
    x_all = x_all.reshape(all_tokens, width)
    gate_up_all = wide_gather(gate_up.reshape(n_s * rows, 2 * half))
    down_block = down_weight
    if not own_blocks:
        down_block = lax.ppermute(down_block, ("wide", "seq"), moves)
    down_all = wide_gather(down_block)

    gains = jnp.swapaxes(gains[:, :4, :rows], 0, 1).reshape(4, width)

    def own_heads(v):
        return jnp.concatenate([lax.dynamic_slice_in_dim(v, head_of(s_index, i) * HEAD_DIM, HEAD_DIM, 1) for i in range(heads)], 1)

    own_gains = own_heads(gains)

    x_all, down_all = lax.optimization_barrier((x_all, down_all))
    lin = dot(x_all, qkv_all)
    q_lin, k_lin = lin[:, :cols], lin[:, cols : 2 * cols]

    def stack_sums(a, b):
        return jnp.stack([a, b]).reshape(-1, 128)

    sums = exchange(stack_sums(jnp.sum(q_lin * q_lin, 1), jnp.sum(k_lin * k_lin, 1)), n_w, n_s, False, 2)
    inv = lax.rsqrt(jnp.sum(sums, 0).reshape(2, all_tokens) / width + eps_norm).T
    tables = rotation_tables(jnp.arange(row_len, dtype=jnp.int32))
    docs = documents[:, 0, :]
    shape4 = (n_s, micro, local, -1)
    attended, q, k, v, lse = attend(lin.reshape(shape4), inv.reshape(shape4), own_gains, tables, docs, heads, scale)
    attended = attended.reshape(all_tokens, cols)

    own_f32 = ((tokens, width), f32)
    vec_f32 = ((1, width), f32)
    hidden_all, hidden, mixed_n, mixed_inv = around(
        dot(attended, out_all).astype(bf16), (flat, gains[2:3]), mixed_rows, [own_f32, own_f32, ((tokens, 1), f32)], n_s, 3, False
    )
    hidden_all = hidden_all.reshape(all_tokens, width)
    active, slope, swish = feed_forward(hidden_all, gate_up_all)
    d_down_all, layer_out, feed_term = around(
        dot(active, down_all).astype(bf16), (hidden, cot, gains[3:4]), down_rows, [((tokens, width), bf16), vec_f32], n_s, 4, True
    )
    d_down_all = d_down_all.reshape(all_tokens, width)
    d_gate_up = feed_back(d_down_all, down_all, slope, swish)
    mlp_part = t_dot(hidden_all, d_gate_up).astype(bf16)
    mlp_grad = wide_scatter(mlp_part)
    d_mixed_all, d_hidden, attention_term, down_part = around(
        dot_t(after(d_gate_up, mlp_part), gate_up_all).astype(bf16), (cot, mixed_n, mixed_inv, gains[2:3]), hidden_rows, [own_f32, vec_f32],
        n_s, 5, True, (active, d_down_all),
    )
    mlp_grad, d_mixed_all, down_part = lax.optimization_barrier((mlp_grad, d_mixed_all, down_part))
    down_grad = wide_scatter(down_part)
    d_mixed_all = d_mixed_all.reshape(all_tokens, width)
    out_part = t_dot(attended, d_mixed_all).astype(bf16)
    d_attended = dot_t(d_mixed_all, out_all).astype(bf16).reshape(shape4)

    d_q, d_k, d_v = attend_back(q, k, v, lse, d_attended, tables, docs, heads, scale)
    d_q, d_k, d_v = (t.reshape(all_tokens, cols) for t in (d_q, d_k, d_v))
    q_n, k_n = q_lin * inv[:, 0:1], k_lin * inv[:, 1:2]
    d_qg, d_kg = d_q * own_gains[0], d_k * own_gains[1]
    mean_sums = stack_sums(jnp.sum(d_qg * q_n, 1), jnp.sum(d_kg * k_n, 1))
    if halves:
        mean_sums, out_part = sums_exchange(mean_sums, out_part.reshape(heads, 2, rows, width), n_w, n_s, 6)
    else:
        mean_sums = exchange(mean_sums, n_w, n_s, False, 6)
    mean_sums, mlp_grad = lax.optimization_barrier((mean_sums, mlp_grad))
    mlp_grad = lax.all_to_all(mlp_grad, "seq", 0, 0, tiled=True)
    means = jnp.sum(mean_sums, 0).reshape(2, all_tokens).T / width
    query_term = jnp.sum(d_q * q_n, 0)
    key_term = jnp.sum(d_k * k_n, 0)
    d_q_lin = (inv[:, 0:1] * (d_qg - q_n * means[:, 0:1])).astype(bf16)
    d_k_lin = (inv[:, 1:2] * (d_kg - k_n * means[:, 1:2])).astype(bf16)
    d_lin = jnp.concatenate([d_q_lin, d_k_lin, d_v], axis=1)
    qkv_part = t_dot(x_all, d_lin).astype(bf16)
    d_hidden, down_grad = lax.optimization_barrier((d_hidden, down_grad))
    def spread(term):
        full = jnp.zeros((width,), f32)
        for i in range(heads):
            full = lax.dynamic_update_slice_in_dim(full, term[i * HEAD_DIM : (i + 1) * HEAD_DIM], head_of(s_index, i) * HEAD_DIM, 0)
        return full

    terms = jnp.stack([spread(query_term), spread(key_term), attention_term[0], feed_term[0]])
    terms = jnp.swapaxes(terms.reshape(4, n_dev, rows), 0, 1)
    terms = jnp.pad(terms, ((0, 0), (0, 4), (0, 128 - rows)))
    input_grad, all_terms = last_sum(dot_t(after(d_lin, qkv_part), qkv_all).astype(bf16), d_hidden, terms, n_w, n_s, 7)
    input_grad = input_grad.reshape(inputs.shape)
    qkv_grad = wide_scatter(qkv_part)
    out_grad = wide_scatter(after(out_part, qkv_grad, input_grad).reshape(cols, width))
    if not halves:
        out_grad = lax.ppermute(out_grad, ("wide", "seq"), back_moves)

    qkv_grad = final_exchange(after(qkv_grad, input_grad).reshape(n_s, rows, 3 * cols), n_w, n_s, 8)
    gate_grad, up_grad = unpack(mlp_grad.reshape(n_s, rows, 2 * half), feed, feed_plan)
    query_grad, key_grad, value_grad = unpack(qkv_grad, width, qkv_plan)
    gain_grads = jnp.sum(all_terms, 0)[:4, :rows]
    if not own_blocks:
        down_grad = lax.ppermute(down_grad, ("wide", "seq"), back_moves)
    return (layer_out.reshape(inputs.shape), input_grad, query_grad, key_grad, value_grad, out_grad.astype(f32),
            gain_grads[0], gain_grads[1], gain_grads[2], gate_grad, up_grad, down_grad.astype(f32), gain_grads[3])


def solution(mesh):
    tok = P(None, "wide", "seq", None)
    docs = P(None, "wide", None)
    mat = P(("wide", "seq"), None)
    vec = P(("wide", "seq"))

    def body(*args):
        return on_device(mesh.shape["wide"], mesh.shape["seq"], *args)

    return jax.shard_map(
        body,
        mesh=mesh,
        in_specs=(tok, docs, tok, mat, mat, mat, mat, vec, vec, vec, mat, mat, mat, vec),
        out_specs=(tok, tok, mat, mat, mat, mat, vec, vec, vec, mat, mat, mat, vec),
        check_vma=False,
    )
```

```python
import functools

import jax
import jax.numpy as jnp
from jax import lax
from jax.experimental import pallas as pl
from jax.experimental.pallas import tpu as pltpu
from jax.sharding import PartitionSpec as P

HEADS = 16
HEAD_DIM = 128
eps_norm = 1e-06
rope_base = 500000.0
masked_value = -1e30
bf16 = jnp.bfloat16
f32 = jnp.float32
MESH = pl.DeviceIdType.MESH
ANY = pl.BlockSpec(memory_space=pl.ANY)
VM = pl.BlockSpec(memory_space=pltpu.VMEM)
DMA = pltpu.SemaphoreType.DMA
PACE = 1
CHUNKS = 4
SUB = 4


def params(cid, megabytes=None):
    limit = {} if megabytes is None else {"vmem_limit_bytes": megabytes * 2**20}
    return pltpu.CompilerParams(collective_id=cid, has_side_effects=True, **limit)


def cost(microseconds):
    return pl.CostEstimate(flops=0, transcendentals=0, bytes_accessed=int(microseconds * 3e6))


def far_first(n_s):
    return sorted(range(n_s), key=lambda k: -min(k, n_s - k))


def remote(src, dst, send, recv, device):
    return pltpu.make_async_remote_copy(src, dst, send, recv, device_id=device, device_id_type=MESH)


def greet(targets):
    barrier = pltpu.get_barrier_semaphore()
    count = 0
    for cond, dev in targets:
        if cond is None:
            pl.semaphore_signal(barrier, inc=1, device_id=dev, device_id_type=MESH)
            count = count + 1
        else:

            @pl.when(cond)
            def _():
                pl.semaphore_signal(barrier, inc=1, device_id=dev, device_id_type=MESH)

            count = count + cond.astype(jnp.int32)
    pl.semaphore_wait(barrier, count)


class Line:
    def __init__(self, n_s):
        self.s = lax.axis_index("seq")
        self.nz = n_s // 2
        self.z, self.c = self.s // 2, self.s % 2
        self.mate_slot = self.s + 1 - 2 * self.c
        self.mate = {"seq": self.mate_slot}
        self.steps = (1, -1)
        self.more = (self.z < self.nz - 1, self.z > 0)
        self.next = ({"seq": self.s + 2}, {"seq": self.s - 2})

    def neighbours(self):
        return [(self.more[0], self.next[0]), (self.more[1], self.next[1]), (None, self.mate)]


class Gather:
    def __init__(self, line, own, out, chunks, send, recv, mate_send, mate_recv):
        self.line, self.own, self.out = line, own, out
        self.chunks, self.rows = chunks, own.shape[0] // chunks
        self.send, self.recv, self.mate_send, self.mate_recv = send, recv, mate_send, mate_recv

    def part(self, slot, k):
        return self.out.at[slot, pl.ds(k * self.rows, self.rows)]

    def source(self, d, k, slot):
        return self.own.at[pl.ds(k * self.rows, self.rows)] if d == 0 else self.part(slot, k)

    def hop(self, i, d, k, slot):
        return remote(self.source(d, k, slot), self.part(slot, k), self.send.at[i, d, k], self.recv.at[i, d, k], self.line.next[i])

    def share(self, i, d, k, slot):
        return remote(self.source(d, k, slot), self.part(slot, k), self.mate_send.at[i, d, k], self.mate_recv.at[i, d, k], self.line.mate)

    def start(self, k):
        line = self.line
        for i in range(2):

            @pl.when(line.more[i])
            def _():
                self.hop(i, 0, k, line.s).start()

        self.share(0, 0, k, line.s).start()

    def each(self, d, mine=True):
        line = self.line
        for i in range(2):
            origin = line.z - line.steps[i] * d
            yield i, (origin >= 0) & (origin < line.nz), 2 * origin + (line.c if mine else 1 - line.c)

    def pass_on(self, d, k):
        for i, there, slot in self.each(d):

            @pl.when(there)
            def _():
                self.hop(i, d - 1, k, slot).wait_recv()
                if d < self.line.nz - 1:

                    @pl.when(self.line.more[i])
                    def _():
                        self.hop(i, d, k, slot).start()

                self.share(i, d, k, slot).start()

    def finish(self):
        line = self.line
        for k in range(self.chunks):
            self.share(0, 0, k, line.mate_slot).wait_recv()
            for d in range(1, line.nz):
                for i, there, slot in self.each(d, False):

                    @pl.when(there)
                    def _():
                        self.share(i, d, k, slot).wait_recv()

        for k in range(self.chunks):
            self.share(0, 0, k, line.s).wait_send()
            for i in range(2):

                @pl.when(line.more[i])
                def _():
                    self.hop(i, 0, k, line.s).wait_send()

            for d in range(1, line.nz):
                for i, there, slot in self.each(d):

                    @pl.when(there)
                    def _():
                        self.share(i, d, k, slot).wait_send()
                        if d < line.nz - 1:

                            @pl.when(line.more[i])
                            def _():
                                self.hop(i, d, k, slot).wait_send()


class Scatter:
    def __init__(self, line, part, from_mate, run, chunks, send, recv, mate_send, mate_recv):
        self.line, self.part, self.from_mate, self.run = line, part, from_mate, run
        self.chunks, self.rows = chunks, part.shape[1] // chunks
        self.send, self.recv, self.mate_send, self.mate_recv = send, recv, mate_send, mate_recv
        self.steps = line.nz - 1
        self.groups = chunks // SUB
        self.count = self.steps * self.groups

    def span(self, k):
        return pl.ds(pl.multiple_of(k * self.rows, self.rows), self.rows)

    def give(self, zd, k):
        line, rs = self.line, self.span(k)
        return remote(self.part.at[2 * zd + 1 - line.c, rs], self.from_mate.at[zd, rs], self.mate_send.at[zd, k], self.mate_recv.at[zd, k], line.mate)

    def hop(self, i, zd, k):
        ref = self.run.at[i, zd, self.span(k)]
        return remote(ref, ref, self.send.at[i, zd, k], self.recv.at[i, zd, k], self.line.next[i])

    def pair(self, zd, k):
        rs = self.span(k)
        return self.part[2 * zd + self.line.c, rs].astype(f32) + self.from_mate[zd, rs].astype(f32)

    def start(self, k):
        nz = self.line.nz
        for zd in sorted(range(nz), key=lambda zd: (min(zd, nz - 1 - zd), -zd)):
            self.give(zd, k).start()

    def item(self, i, q, j):
        group, step = q // self.steps, lax.rem(q, self.steps)
        return (self.line.nz - 1 - step if i == 0 else step), group * SUB + j

    def slot(self, t):
        line = self.line
        for j, i in ((j, i) for j in range(SUB) for i in range(2)):
            q = t - (line.z if i == 0 else line.nz - 1 - line.z)
            behind = line.z > 0 if i == 0 else line.z < line.nz - 1
            zd, k = self.item(i, jnp.clip(q, 0, self.count - 1), j)
            going = (q >= 0) & (q < self.count) & (line.z < zd if i == 0 else line.z > zd)

            @pl.when(going)
            def _():
                rs = self.span(k)
                self.give(zd, k).wait_recv()

                @pl.when(behind)
                def _():
                    self.hop(i, zd, k).wait_recv()
                    self.run[i, zd, rs] = (self.pair(zd, k) + self.run[i, zd, rs].astype(f32)).astype(bf16)

                @pl.when(jnp.logical_not(behind))
                def _():
                    self.run[i, zd, rs] = self.pair(zd, k).astype(bf16)
                    if t >= PACE:
                        self.hop(i, *self.item(i, jnp.int32(t - PACE), j)).wait_send()

                self.hop(i, zd, k).start()

    def total(self, k, use):
        line, rs = self.line, self.span(k)
        for zd in range(line.nz):

            @pl.when(line.z == zd)
            def _():
                self.give(zd, k).wait_recv()
                total = self.pair(zd, k)
                if zd > 0:
                    self.hop(0, zd, k).wait_recv()
                    total = total + self.run[0, zd, rs].astype(f32)
                if zd < line.nz - 1:
                    self.hop(1, zd, k).wait_recv()
                    total = total + self.run[1, zd, rs].astype(f32)
                use(total)

    def finish(self):
        line = self.line
        for k in range(self.chunks):
            for zd in range(line.nz):
                self.give(zd, k).wait_send()
        for q in range(self.count):
            step = q % self.steps
            for i, zd in ((0, line.nz - 1 - step), (1, step)):
                going = line.z < zd if i == 0 else line.z > zd
                behind = line.z > 0 if i == 0 else line.z < line.nz - 1

                @pl.when(going & behind if q < self.count - PACE else going)
                def _():
                    for j in range(SUB):
                        self.hop(i, zd, q // self.steps * SUB + j).wait_send()


def line_sems(nz, chunks):
    return [DMA((2, nz, chunks))] * 4


def scatter_scratch(n_s, rows, width, chunks):
    nz = n_s // 2
    sums = [pltpu.VMEM((nz, rows, width), bf16), pltpu.VMEM((2, nz, rows, width), bf16)]
    return sums + [DMA((2, nz, chunks))] * 2 + [DMA((nz, chunks))] * 2


def mixed_rows(rs, total, x, gain, hidden, normed, inverse, low):
    inv = inverse_rms(total)
    n = total * inv
    out = x[rs].astype(f32) + n * gain[...]
    hidden[rs] = out
    normed[rs] = n
    inverse[rs] = inv
    low[rs] = out.astype(bf16)


def down_rows(rs, total, hidden, cotangent, gain, out, term, low):
    inv = inverse_rms(total)
    n = total * inv
    g = gain[...]
    out[rs] = (hidden[rs] + n * g).astype(bf16)
    grad = cotangent[rs].astype(f32)
    low[rs], more = back_rows(grad, n, inv, g)
    term[...] += more


def hidden_rows(rs, total, cotangent, normed, inverse, gain, d_hidden, term, low):
    grad = cotangent[rs].astype(f32) + total
    d_hidden[rs] = grad
    low[rs], more = back_rows(grad, normed[rs], inverse[rs], gain[...])
    term[...] += more


def back_rows(grad, n, inv, gain):
    scaled = grad * gain
    d = inv * (scaled - n * jnp.mean(scaled * n, axis=-1, keepdims=True))
    return d.astype(bf16), jnp.sum(grad * n, axis=0, keepdims=True)


def run_slots(scatter, use, gather=None, work=None):
    steps, groups = scatter.steps, scatter.groups
    slots = steps * (groups + (1 if gather else 0)) + 1
    for t in range(slots):
        if t < steps * (groups + 1):
            scatter.slot(t)
        if gather:
            for group in range(groups):
                if 1 <= t - steps * (group + 1) <= steps:
                    for j in range(SUB):
                        gather.pass_on(t - steps * (group + 1), group * SUB + j)
        if t and t % steps == 0 and t // steps <= groups:
            for k in range((t // steps - 1) * SUB, t // steps * SUB):
                scatter.total(k, lambda total: use(k, total))
                if gather:
                    gather.start(k)
        if work:
            work(t, slots)


def product_work(left, right, out):
    size = 128
    count = out.shape[0] // size

    def work(t, slots):
        for i in range(count * t // slots, count * (t + 1) // slots):
            rs = pl.ds(i * size, size)
            out[rs] = lax.dot_general(left[:, rs], right[...], (((0,), (0,)), ((), ())), preferred_element_type=f32).astype(bf16)

    return work


def around_kernel(n_s, chunks, rows_fn, n_in, n_out, adds, with_work, *refs):
    part, extra = refs[0], refs[1 : 1 + n_in]
    refs = refs[1 + n_in :]
    work = None
    if with_work:
        left, right, gathered, *outs, made = refs[: 4 + n_out]
        work = product_work(left, right, made)
        refs = refs[4 + n_out :]
    else:
        gathered, *outs = refs[: 1 + n_out]
        refs = refs[1 + n_out :]
    low, local, from_mate, run, *sems = refs
    line = Line(n_s)
    scatter = Scatter(line, part, from_mate, run, chunks, *sems[:4])
    gather = Gather(line, low, gathered, chunks, *sems[4:])
    greet(line.neighbours())
    for k in range(chunks):
        scatter.start(k)
    if adds:
        outs[-1][...] = jnp.zeros_like(outs[-1])
    run_slots(scatter, lambda k, total: rows_fn(scatter.span(k), total, *extra, *outs, low), gather, work)
    own = pltpu.make_async_copy(low, gathered.at[line.s], local)
    own.start()
    gather.finish()
    scatter.finish()
    own.wait()


def around(terms, extra, rows_fn, outs, n_s, cid, adds, pair=(), chunks=CHUNKS):
    rows, width = terms.shape[0] // n_s, terms.shape[1]
    shapes = [((n_s, rows, width), bf16), *outs] + ([((pair[0].shape[1], pair[1].shape[1]), bf16)] if pair else [])
    return pl.pallas_call(
        functools.partial(around_kernel, n_s, chunks, rows_fn, len(extra), len(outs), adds, bool(pair)),
        out_shape=[jax.ShapeDtypeStruct(*o) for o in shapes],
        in_specs=[VM] * (1 + len(extra) + len(pair)),
        out_specs=[ANY] + [VM] * (len(shapes) - 1),
        scratch_shapes=[pltpu.VMEM((rows, width), bf16), DMA] + scatter_scratch(n_s, rows, width, chunks) + line_sems(n_s // 2, chunks),
        compiler_params=params(cid, 48),
        cost_estimate=cost(70),
    )(terms.reshape(n_s, rows, width), *extra, *pair)


def last_kernel(n_w, n_s, chunks, part, d_hidden, terms, out, all_terms, from_mate, run, *sems):
    line = Line(n_s)
    scatter = Scatter(line, part, from_mate, run, chunks, *sems[:4])
    share = Share(n_w, n_s, True, terms, all_terms, *sems[4:])
    greet(share.others())
    for k in range(chunks):
        scatter.start(k)

    def use(k, total):
        out[scatter.span(k)] = d_hidden[scatter.span(k)] + total

    share.start()
    run_slots(scatter, use)
    scatter.finish()
    share.finish()


def last_sum(part, d_hidden, terms, n_w, n_s, cid, chunks=CHUNKS):
    rows, width = part.shape[0] // n_s, part.shape[1]
    count = n_w * n_s
    return pl.pallas_call(
        functools.partial(last_kernel, n_w, n_s, chunks),
        out_shape=[jax.ShapeDtypeStruct((rows, width), f32), jax.ShapeDtypeStruct(terms.shape, terms.dtype)],
        in_specs=[VM] * 3,
        out_specs=[VM] * 2,
        scratch_shapes=scatter_scratch(n_s, rows, width, chunks) + [DMA((count,)), DMA((count,)), DMA],
        compiler_params=params(cid, 48),
        cost_estimate=cost(40),
    )(part.reshape(n_s, rows, width), d_hidden, terms)


class Columns:
    def __init__(self, n_s, plan, arrays, slots, back, send, recv, local):
        self.n_s, self.plan, self.arrays, self.slots, self.back = n_s, plan, arrays, slots, back
        self.send, self.recv, self.local = send, recv, local
        self.s = lax.axis_index("seq")

    def place(self, k):
        return lax.rem(self.s + k, self.n_s)

    def pieces(self, k):
        there = self.place(k)
        for array, parts in zip(self.arrays, self.plan):
            for first, width, column in parts:
                at = pl.ds(column, width)
                if self.back:
                    yield self.slots.at[there, :, at], array.at[:, pl.ds(pl.multiple_of(first(self.s), 128), width)]
                else:
                    yield array.at[:, pl.ds(pl.multiple_of(first(there), 128), width)], self.slots.at[self.s, :, at]

    def start(self):
        for k in far_first(self.n_s)[:-1]:
            for src, dst in self.pieces(k):
                remote(src, dst, self.send.at[k], self.recv.at[k], {"seq": self.place(k)}).start()
        for src, dst in self.pieces(0):
            pltpu.make_async_copy(src, dst, self.local).start()

    def finish(self):
        slot = self.slots.at[0]
        for k in range(1, self.n_s):
            done = remote(slot, slot, self.send.at[k], self.recv.at[k], {"seq": self.place(k)})
            done.wait_recv()
            done.wait_send()
        pltpu.make_async_copy(slot, slot, self.local).wait()


def columns_sems(n_s):
    return [DMA((n_s,)), DMA((n_s,)), DMA]


def seq_others(n_s):
    s = lax.axis_index("seq")
    return [(None, {"seq": lax.rem(s + k, n_s)}) for k in range(1, n_s)]


class Share:
    def __init__(self, n_w, n_s, whole, x, out, send, recv, local):
        self.n_w, self.n_s, self.whole = n_w, n_s, whole
        self.x, self.out, self.send, self.recv, self.local = x, out, send, recv, local
        self.w, self.s = lax.axis_index("wide"), lax.axis_index("seq")
        self.steps = [(a, b) for b in far_first(n_s) for a in (range(n_w) if whole else (0,)) if a or b]

    def at(self, a, b):
        return lax.rem(self.w + a, self.n_w), lax.rem(self.s + b, self.n_s)

    def number(self, a, b):
        w, s = self.at(a, b)
        return w * self.n_s + s if self.whole else s

    def name(self, a, b):
        w, s = self.at(a, b)
        return {"wide": w, "seq": s}

    def others(self):
        return [(None, self.name(a, b)) for a, b in self.steps]

    def block(self, a, b):
        return self.x.at[self.number(a, b)] if len(self.x.shape) == 3 else self.x

    def copy(self, a, b):
        i = a * self.n_s + b
        return remote(self.block(a, b), self.out.at[self.number(0, 0)], self.send.at[i], self.recv.at[i], self.name(a, b))

    def own(self):
        return pltpu.make_async_copy(self.block(0, 0), self.out.at[self.number(0, 0)], self.local)

    def start(self):
        for a, b in self.steps:
            self.copy(a, b).start()
        self.own().start()

    def finish(self):
        for a, b in self.steps:
            self.copy(a, b).wait()
        self.own().wait()


def share_kernel(n_w, n_s, whole, x_ref, o_ref, send, recv, local_sem):
    share = Share(n_w, n_s, whole, x_ref, o_ref, send, recv, local_sem)
    greet(share.others())
    share.start()
    share.finish()


def exchange(x, n_w, n_s, whole, cid):
    count = n_w * n_s if whole else n_s
    return pl.pallas_call(
        functools.partial(share_kernel, n_w, n_s, whole),
        out_shape=jax.ShapeDtypeStruct((count, *x.shape[-2:]), x.dtype),
        in_specs=[VM],
        out_specs=VM,
        scratch_shapes=[DMA((count,)), DMA((count,)), DMA],
        compiler_params=params(cid),
        cost_estimate=cost(10),
    )(x)


class Halves:
    def __init__(self, n_w, natural, heads, send, recv, local):
        s = lax.axis_index("seq")
        c = lax.rem(s, 2)
        mate = {"seq": s + 1 - 2 * c}
        self.copies = []
        for i in range(n_w // 2):
            there = natural.at[c * (n_w // 2) + i]
            self.copies.append(remote(heads.at[i, 1 - c], there, send.at[i], recv.at[i], mate))
            self.copies.append(pltpu.make_async_copy(heads.at[i, c], there, local.at[i]))

    def start(self):
        for copy in self.copies:
            copy.start()

    def finish(self):
        for copy in self.copies:
            copy.wait()


def halves_sems(n_w):
    return [DMA((n_w // 2,))] * 3


def first_kernel(n_s, plan, qw, kw, vw, qkv, *sems):
    columns = Columns(n_s, plan, (qw, kw, vw), qkv, False, *sems)
    greet(seq_others(n_s))
    columns.start()
    columns.finish()


def first_exchange(weights, plan, cols, n_s, cid):
    return pl.pallas_call(
        functools.partial(first_kernel, n_s, plan),
        out_shape=jax.ShapeDtypeStruct((n_s, weights[0].shape[0], cols), bf16),
        in_specs=[ANY] * 3,
        out_specs=ANY,
        scratch_shapes=columns_sems(n_s),
        compiler_params=params(cid),
        cost_estimate=cost(20),
    )(*weights)


class Heads:
    def __init__(self, n_w, block, heads, send, recv, local):
        w, s = lax.axis_index("wide"), lax.axis_index("seq")
        half = n_w // 2
        c = lax.rem(s, 2)
        core = w // half
        self.lane = core == c
        dst = heads.at[lax.rem(w, half), c]
        self.sends = []
        for k in range(n_w):
            device = {"wide": lax.rem(w + k, n_w), "seq": s - c + core}
            self.sends.append(remote(block, dst, send.at[k], recv.at[lax.rem(w, half), c], device))
        self.stay = pltpu.make_async_copy(block, dst, local)
        self.arrivals = []
        for i in range(half):
            for there in range(2):
                own = self.lane & (lax.rem(w, half) == i) & (c == there)
                ref = heads.at[i, there]
                self.arrivals.append((jnp.logical_not(own), remote(ref, ref, send.at[0], recv.at[i, there], {"seq": s + 1 - 2 * c})))

    def start(self):
        for copy in self.sends[1:]:
            copy.start()

        @pl.when(self.lane)
        def _():
            self.stay.start()

        @pl.when(jnp.logical_not(self.lane))
        def _():
            self.sends[0].start()

    def finish(self):
        for come, copy in self.arrivals:

            @pl.when(come)
            def _():
                copy.wait_recv()

        for copy in self.sends[1:]:
            copy.wait_send()

        @pl.when(self.lane)
        def _():
            self.stay.wait()

        @pl.when(jnp.logical_not(self.lane))
        def _():
            self.sends[0].wait_send()


def second_kernel(n_w, n_s, chunks, plan, heads, x, gw, uw, gain, *refs):
    if heads:
        out_block, x_all, slots, gains, out_heads, own_sem, *sems = refs
    else:
        x_all, slots, gains, own_sem, *sems = refs
    line = Line(n_s)
    gather = Gather(line, x, x_all, chunks, *sems[:4])
    others = [Share(n_w, n_s, True, gain, gains, *sems[4:7])]
    if heads:
        others.append(Heads(n_w, out_block, out_heads, *sems[7:10]))
    others.append(Columns(n_s, plan, (gw, uw), slots, False, *sems[-3:]))
    greet(others[0].others())
    own = pltpu.make_async_copy(x, x_all.at[line.s], own_sem)
    for k in range(chunks):
        gather.start(k)
    own.start()
    for other in others[:-1]:
        other.start()
    for d in range(1, line.nz):
        for k in range(chunks):
            gather.pass_on(d, k)
            if (d, k) == (1, chunks // 2 - 1):
                others[-1].start()
    gather.finish()
    own.wait()
    for other in others:
        other.finish()


def second_exchange(x, weights, gain, out_block, plan, cols, n_w, n_s, cid, chunks=4):
    rows, width = x.shape
    count = n_w * n_s
    shapes = [((n_s, rows, width), bf16), ((n_s, weights[0].shape[0], cols), bf16), ((count, *gain.shape), gain.dtype)]
    sems = [DMA] + line_sems(n_s // 2, chunks) + [DMA((count,)), DMA((count,)), DMA]
    extra = []
    if out_block is not None:
        extra = [out_block]
        shapes.append(((n_w // 2, 2, *out_block.shape), bf16))
        sems += [DMA((n_w,)), DMA((n_w // 2, 2)), DMA]
    return pl.pallas_call(
        functools.partial(second_kernel, n_w, n_s, chunks, plan, bool(extra)),
        out_shape=[jax.ShapeDtypeStruct(*o) for o in shapes],
        in_specs=[ANY] * 3 + [VM] + [ANY] * len(extra),
        out_specs=[ANY, ANY, VM] + [ANY] * len(extra),
        scratch_shapes=sems + columns_sems(n_s),
        compiler_params=params(cid),
        cost_estimate=cost(80),
    )(x, *weights, gain, *extra)


def unpack_kernel(n_s, plan, slots, *outs):
    for out, pieces in zip(outs, plan):
        for first, width, column in pieces:
            for s in range(n_s):
                out[:, first(s) : first(s) + width] = slots[s, :, column : column + width].astype(f32)


def unpack(slots, width, plan):
    n_s, rows, _ = slots.shape
    return pl.pallas_call(
        functools.partial(unpack_kernel, n_s, plan),
        out_shape=[jax.ShapeDtypeStruct((rows, width), f32)] * len(plan),
        in_specs=[VM],
        out_specs=[VM] * len(plan),
        compiler_params=pltpu.CompilerParams(vmem_limit_bytes=40 * 2**20),
        cost_estimate=cost(4),
    )(slots)


def sums_kernel(n_w, n_s, x, heads, all_x, natural, *sems):
    share = Share(n_w, n_s, False, x, all_x, *sems[:3])
    halves = Halves(n_w, natural, heads, *sems[3:])
    greet(share.others())
    share.start()
    halves.start()
    share.finish()
    halves.finish()


def sums_exchange(x, heads, n_w, n_s, cid):
    return pl.pallas_call(
        functools.partial(sums_kernel, n_w, n_s),
        out_shape=[jax.ShapeDtypeStruct((n_s, *x.shape), x.dtype), jax.ShapeDtypeStruct((n_w, *heads.shape[2:]), bf16)],
        in_specs=[VM, VM],
        out_specs=[VM, VM],
        scratch_shapes=[DMA((n_s,)), DMA((n_s,)), DMA] + halves_sems(n_w),
        compiler_params=params(cid),
        cost_estimate=cost(10),
    )(x, heads)


def final_kernel(n_w, n_s, qkv, qkv_own, *sems):
    share = Share(n_w, n_s, False, qkv, qkv_own, *sems)
    greet(seq_others(n_s))
    share.start()
    share.finish()


def final_exchange(qkv, n_w, n_s, cid):
    return pl.pallas_call(
        functools.partial(final_kernel, n_w, n_s),
        out_shape=jax.ShapeDtypeStruct(qkv.shape, qkv.dtype),
        in_specs=[ANY],
        out_specs=ANY,
        scratch_shapes=[DMA((n_s,)), DMA((n_s,)), DMA],
        compiler_params=params(cid),
        cost_estimate=cost(20),
    )(qkv)


def feed_kernel(hidden, gate_w, up_w, active, slope, swish):
    rows = hidden.shape[0] // 4
    for i in range(4):
        rs = pl.ds(i * rows, rows)
        gate, up = dot(hidden[rs], gate_w[...]), dot(hidden[rs], up_w[...])
        sigma = jax.nn.sigmoid(gate)
        silu = gate * sigma
        active[rs] = (silu * up).astype(bf16)
        slope[rs] = (up * sigma * (1.0 + gate * (1.0 - sigma))).astype(bf16)
        swish[rs] = silu.astype(bf16)


def feed_forward(hidden, weights, tile=256):
    tokens, width = hidden.shape
    half = weights.shape[1] // 2
    steps = half // tile
    out = pl.BlockSpec((tokens, tile), lambda j: (0, j))
    return pl.pallas_call(
        feed_kernel,
        grid=(steps,),
        out_shape=[jax.ShapeDtypeStruct((tokens, half), bf16)] * 3,
        in_specs=[
            pl.BlockSpec((tokens, width), lambda j: (0, 0)),
            pl.BlockSpec((width, tile), lambda j: (0, j)),
            pl.BlockSpec((width, tile), lambda j: (0, j + steps)),
        ],
        out_specs=[out] * 3,
        compiler_params=pltpu.CompilerParams(vmem_limit_bytes=48 * 2**20),
        cost_estimate=pl.CostEstimate(flops=4 * tokens * width * half, transcendentals=0, bytes_accessed=2 * (tokens * width + 2 * width * half)),
    )(hidden, weights, weights)


def feed_back_kernel(d_down, down_w, slope, swish, out):
    tile = down_w.shape[0]
    half = out.shape[1] // 2
    d_active = dot_t(d_down[...], down_w[...])
    at = pl.multiple_of(pl.program_id(0) * tile, tile)
    out[:, pl.ds(at, tile)] = (d_active * slope[...].astype(f32)).astype(bf16)
    out[:, pl.ds(pl.multiple_of(at + half, tile), tile)] = (d_active * swish[...].astype(f32)).astype(bf16)


def feed_back(d_down, down_w, slope, swish, tile=512):
    tokens, width = d_down.shape
    half = down_w.shape[0]
    cols = pl.BlockSpec((tokens, tile), lambda j: (0, j))
    return pl.pallas_call(
        feed_back_kernel,
        grid=(half // tile,),
        out_shape=jax.ShapeDtypeStruct((tokens, 2 * half), bf16),
        in_specs=[pl.BlockSpec((tokens, width), lambda j: (0, 0)), pl.BlockSpec((tile, width), lambda j: (j, 0)), cols, cols],
        out_specs=pl.BlockSpec((tokens, 2 * half), lambda j: (0, 0)),
        compiler_params=pltpu.CompilerParams(vmem_limit_bytes=48 * 2**20),
        cost_estimate=pl.CostEstimate(flops=2 * tokens * width * half, transcendentals=0, bytes_accessed=2 * (tokens * width + width * half)),
    )(d_down, down_w, slope, swish)


def rows_kernel(a, b, out):
    out[...] = lax.dot_general(a[...], b[...], (((1,), (1,)), ((), ())), preferred_element_type=f32).astype(bf16)


def columns_product(a, b, tile=512):
    (m, k), n = a.shape, b.shape[0]
    return pl.pallas_call(
        rows_kernel,
        grid=(n // tile,),
        out_shape=jax.ShapeDtypeStruct((m, n), bf16),
        in_specs=[pl.BlockSpec((m, k), lambda j: (0, 0)), pl.BlockSpec((tile, k), lambda j: (j, 0))],
        out_specs=pl.BlockSpec((m, tile), lambda j: (0, j)),
        compiler_params=pltpu.CompilerParams(vmem_limit_bytes=48 * 2**20),
        cost_estimate=pl.CostEstimate(flops=2 * m * n * k, transcendentals=0, bytes_accessed=2 * (m * k + k * n + m * n)),
    )(a, b)


def terms_kernel(a, b, out):
    out[...] = lax.dot_general(a[...], b[...], (((0,), (0,)), ((), ())), preferred_element_type=f32).astype(bf16)


def weight_product(a, b, tile=512):
    (k, m), n = a.shape, b.shape[1]
    return pl.pallas_call(
        terms_kernel,
        grid=(m // tile,),
        out_shape=jax.ShapeDtypeStruct((m, n), bf16),
        in_specs=[pl.BlockSpec((k, tile), lambda i: (0, i)), pl.BlockSpec((k, n), lambda i: (0, 0))],
        out_specs=pl.BlockSpec((tile, n), lambda i: (i, 0)),
        compiler_params=pltpu.CompilerParams(vmem_limit_bytes=48 * 2**20),
        cost_estimate=pl.CostEstimate(flops=2 * m * n * k, transcendentals=0, bytes_accessed=2 * (m * k + k * n + m * n)),
    )(a, b)


def dot(a, b):
    return jnp.dot(a, b, preferred_element_type=f32)


def dot_t(a, b):
    return lax.dot_general(a, b, (((1,), (1,)), ((), ())), preferred_element_type=f32)


def t_dot(a, b):
    return lax.dot_general(a, b, (((0,), (0,)), ((), ())), preferred_element_type=f32)


def turn(v, cosine, sine):
    return v * cosine + pltpu.roll(v, HEAD_DIM // 2, 1) * sine


def allowed_pairs(doc_q, doc_k, length):
    rows = lax.broadcasted_iota(jnp.int32, (length, length), 0)
    cols = lax.broadcasted_iota(jnp.int32, (length, length), 1)
    return (cols <= rows) & (doc_q == doc_k)


def attend_kernel(scale, ql, kl, vl, inv, gq, gk, cos, sin, doc_q, doc_k, att, q_out, k_out, v_out, lse):
    length = cos.shape[0]

    def flat(ref):
        return ref[...].reshape(length, -1)

    scales = flat(inv)
    q = turn(flat(ql) * scales[:, 0:1] * gq[...], cos[...], sin[...]).astype(bf16)
    k = turn(flat(kl) * scales[:, 1:2] * gk[...], cos[...], sin[...]).astype(bf16)
    v = flat(vl).astype(bf16)
    q_out[...] = q.reshape(q_out.shape)
    k_out[...] = k.reshape(k_out.shape)
    v_out[...] = v.reshape(v_out.shape)
    allowed = allowed_pairs(doc_q[0], doc_k[0], length)
    scores = jnp.where(allowed, dot_t(q, k) * scale, masked_value)
    top = jnp.max(scores, 1, keepdims=True)
    e = jnp.exp(scores - top)
    total = jnp.sum(e, 1, keepdims=True)
    probs = (e * (1.0 / total)).astype(bf16)
    att[...] = dot(probs, v).astype(bf16).reshape(att.shape)
    lse[...] = (top + jnp.log(total)).reshape(lse.shape)


def attend_back_kernel(scale, q, k, v, lse, da, cos, sin, doc_q, doc_k, dq_out, dk_out, dv_out):
    length = cos.shape[0]

    def flat(ref):
        return ref[...].reshape(length, -1)

    queries, keys, values, d_att = flat(q), flat(k), flat(v), flat(da)
    allowed = allowed_pairs(doc_q[0], doc_k[0], length)
    scores = jnp.where(allowed, dot_t(queries, keys) * scale, masked_value)
    probs = jnp.exp(scores - flat(lse))
    d_probs = dot_t(d_att, values)
    delta = jnp.sum(probs * d_probs, 1, keepdims=True)
    d_scores = (probs * (d_probs - delta)).astype(bf16)
    d_q = dot(d_scores, keys) * scale
    d_k = t_dot(d_scores, queries) * scale
    dv_out[...] = t_dot(probs.astype(bf16), d_att).astype(bf16).reshape(dv_out.shape)
    dq_out[...] = turn(d_q, cos[...], -sin[...]).reshape(dq_out.shape)
    dk_out[...] = turn(d_k, cos[...], -sin[...]).reshape(dk_out.shape)


def attention_specs(n_s, local, length):
    def tok(first):
        return pl.BlockSpec((n_s, 1, local, HEAD_DIM), lambda m, h: (0, m, 0, first + h))

    gain = pl.BlockSpec((1, HEAD_DIM), lambda m, h: (0, h))
    table = pl.BlockSpec((length, HEAD_DIM), lambda m, h: (0, 0))
    doc_q = pl.BlockSpec((1, length, 1), lambda m, h: (m, 0, 0))
    doc_k = pl.BlockSpec((1, 1, length), lambda m, h: (m, 0, 0))
    col = pl.BlockSpec((1, n_s, 1, local, 1), lambda m, h: (h, 0, m, 0, 0))
    return tok, gain, table, doc_q, doc_k, col


def attend(lin, inv, gains, tables, docs, heads, scale):
    n_s, micro, local, _ = lin.shape
    length = n_s * local
    tok, gain, table, doc_q, doc_k, col = attention_specs(n_s, local, length)
    inv_spec = pl.BlockSpec((n_s, 1, local, 2), lambda m, h: (0, m, 0, 0))
    out = jax.ShapeDtypeStruct((n_s, micro, local, heads * HEAD_DIM), bf16)
    return pl.pallas_call(
        functools.partial(attend_kernel, scale),
        grid=(micro, heads),
        out_shape=[out, out, out, out, jax.ShapeDtypeStruct((heads, n_s, micro, local, 1), f32)],
        in_specs=[tok(0), tok(heads), tok(2 * heads), inv_spec, gain, gain, table, table, doc_q, doc_k],
        out_specs=[tok(0)] * 4 + [col],
        compiler_params=pltpu.CompilerParams(vmem_limit_bytes=48 * 2**20),
    )(lin, lin, lin, inv, gains[0:1], gains[1:2], *tables, docs[:, :, None], docs[:, None, :])


def attend_back(q, k, v, lse, d_att, tables, docs, heads, scale):
    n_s, micro, local, width = q.shape
    length = n_s * local
    tok, gain, table, doc_q, doc_k, col = attention_specs(n_s, local, length)
    return pl.pallas_call(
        functools.partial(attend_back_kernel, scale),
        grid=(micro, heads),
        out_shape=[jax.ShapeDtypeStruct(q.shape, f32)] * 2 + [jax.ShapeDtypeStruct(q.shape, bf16)],
        in_specs=[tok(0)] * 3 + [col, tok(0), table, table, doc_q, doc_k],
        out_specs=[tok(0)] * 3,
        compiler_params=pltpu.CompilerParams(vmem_limit_bytes=48 * 2**20),
    )(q, k, v, lse, d_att, *tables, docs[:, :, None], docs[:, None, :])


def inverse_rms(values):
    return lax.rsqrt(jnp.mean(values * values, axis=-1, keepdims=True) + eps_norm)


def rotation_tables(positions):
    half_dim = HEAD_DIM // 2
    frequency = rope_base ** (-jnp.arange(half_dim, dtype=f32) * 2.0 / HEAD_DIM)
    angles = positions.astype(f32)[:, None] * frequency[None, :]
    cosine, sine = jnp.cos(angles), jnp.sin(angles)
    return jnp.concatenate([cosine, cosine], 1), jnp.concatenate([-sine, sine], 1)


def wide_gather(block):
    return lax.all_gather(block, "wide", axis=0, tiled=True)


def wide_scatter(partial):
    return lax.psum_scatter(partial.astype(bf16), "wide", scatter_dimension=0, tiled=True)


def after(value, *others):
    return lax.optimization_barrier((value, *others))[0]


def on_device(n_w, n_s, inputs, documents, cotangent, query_weight, key_weight, value_weight, output_weight,
              query_gain, key_gain, attention_gain, gate_weight, up_weight, down_weight, feed_gain):
    micro, _, local, width = inputs.shape
    tokens = micro * local
    all_tokens = n_s * tokens
    n_dev = n_w * n_s
    heads = HEADS // n_s
    cols = heads * HEAD_DIM
    row_len = documents.shape[2]
    feed = gate_weight.shape[1]
    feed_block = feed // n_dev
    half = n_w * feed_block
    rows = query_weight.shape[0]
    scale = HEAD_DIM ** (-0.5)
    s_index = lax.axis_index("seq")

    flat = inputs.reshape(tokens, width)
    cot = cotangent.reshape(tokens, width)
    halves = 2 * rows == HEAD_DIM and n_w == 2 * heads

    def head_of(s, i):
        return s // 2 + n_s // 2 * (s % 2 * heads + i) if halves else s * heads + i

    def head_column(i):
        return lambda s: head_of(s, i) * HEAD_DIM

    qkv_plan = [[(head_column(h), HEAD_DIM, i * cols + h * HEAD_DIM) for h in range(heads)] for i in range(3)]
    own_blocks = feed_block % 128 == 0
    moves = [(b, (b % n_w) * n_s + b // n_w) for b in range(n_dev)]
    back_moves = [(b, a) for a, b in moves]
    if own_blocks:
        feed_plan = [[(lambda s, a=a: (a * n_s + s) * feed_block, feed_block, i * half + a * feed_block) for a in range(n_w)] for i in range(2)]
    else:
        feed_plan = [[(lambda s: s * half, half, i * half)] for i in range(2)]

    own_gain = jnp.stack([query_gain, key_gain, attention_gain, feed_gain]).astype(f32)
    own_gain = jnp.pad(own_gain, ((0, 4), (0, 128 - rows)))
    qkv = first_exchange((query_weight, key_weight, value_weight), qkv_plan, 3 * cols, n_s, 0)
    qkv_all = wide_gather(qkv.reshape(n_s * rows, 3 * cols))
    if not halves:
        out_all = wide_gather(lax.ppermute(output_weight, ("wide", "seq"), moves))
    x_all, gate_up, gains, *out_heads = second_exchange(
        after(flat, qkv), (gate_weight, up_weight), own_gain, output_weight if halves else None, feed_plan, 2 * half, n_w, n_s, 1
    )
    if halves:
        out_all = out_heads[0].reshape(cols, width)
    x_all = x_all.reshape(all_tokens, width)
    gate_up_all = wide_gather(gate_up.reshape(n_s * rows, 2 * half))
    down_block = down_weight
    if not own_blocks:
        down_block = lax.ppermute(down_block, ("wide", "seq"), moves)
    down_all = wide_gather(down_block)

    gains = jnp.swapaxes(gains[:, :4, :rows], 0, 1).reshape(4, width)

    def own_heads(v):
        return jnp.concatenate([lax.dynamic_slice_in_dim(v, head_of(s_index, i) * HEAD_DIM, HEAD_DIM, 1) for i in range(heads)], 1)

    own_gains = own_heads(gains)

    x_all, down_all = lax.optimization_barrier((x_all, down_all))
    lin = dot(x_all, qkv_all)
    q_lin, k_lin = lin[:, :cols], lin[:, cols : 2 * cols]

    def stack_sums(a, b):
        return jnp.stack([a, b]).reshape(-1, 128)

    sums = exchange(stack_sums(jnp.sum(q_lin * q_lin, 1), jnp.sum(k_lin * k_lin, 1)), n_w, n_s, False, 2)
    inv = lax.rsqrt(jnp.sum(sums, 0).reshape(2, all_tokens) / width + eps_norm).T
    tables = rotation_tables(jnp.arange(row_len, dtype=jnp.int32))
    docs = documents[:, 0, :]
    shape4 = (n_s, micro, local, -1)
    attended, q, k, v, lse = attend(lin.reshape(shape4), inv.reshape(shape4), own_gains, tables, docs, heads, scale)
    attended = attended.reshape(all_tokens, cols)

    own_f32 = ((tokens, width), f32)
    vec_f32 = ((1, width), f32)
    hidden_all, hidden, mixed_n, mixed_inv = around(
        dot(attended, out_all).astype(bf16), (flat, gains[2:3]), mixed_rows, [own_f32, own_f32, ((tokens, 1), f32)], n_s, 3, False
    )
    hidden_all = hidden_all.reshape(all_tokens, width)
    active, slope, swish = feed_forward(hidden_all, gate_up_all)
    d_down_all, layer_out, feed_term = around(
        dot(active, down_all).astype(bf16), (hidden, cot, gains[3:4]), down_rows, [((tokens, width), bf16), vec_f32], n_s, 4, True
    )
    d_down_all = d_down_all.reshape(all_tokens, width)
    d_gate_up = feed_back(d_down_all, down_all, slope, swish)
    mlp_part = t_dot(hidden_all, d_gate_up).astype(bf16)
    mlp_grad = wide_scatter(mlp_part)
    d_mixed_all, d_hidden, attention_term, down_part = around(
        dot_t(after(d_gate_up, mlp_part), gate_up_all).astype(bf16), (cot, mixed_n, mixed_inv, gains[2:3]), hidden_rows, [own_f32, vec_f32],
        n_s, 5, True, (active, d_down_all),
    )
    mlp_grad, d_mixed_all, down_part = lax.optimization_barrier((mlp_grad, d_mixed_all, down_part))
    down_grad = wide_scatter(down_part)
    d_mixed_all = d_mixed_all.reshape(all_tokens, width)
    out_part = t_dot(attended, d_mixed_all).astype(bf16)
    d_attended = dot_t(d_mixed_all, out_all).astype(bf16).reshape(shape4)

    d_q, d_k, d_v = attend_back(q, k, v, lse, d_attended, tables, docs, heads, scale)
    d_q, d_k, d_v = (t.reshape(all_tokens, cols) for t in (d_q, d_k, d_v))
    q_n, k_n = q_lin * inv[:, 0:1], k_lin * inv[:, 1:2]
    d_qg, d_kg = d_q * own_gains[0], d_k * own_gains[1]
    mean_sums = stack_sums(jnp.sum(d_qg * q_n, 1), jnp.sum(d_kg * k_n, 1))
    if halves:
        mean_sums, out_part = sums_exchange(mean_sums, out_part.reshape(heads, 2, rows, width), n_w, n_s, 6)
    else:
        mean_sums = exchange(mean_sums, n_w, n_s, False, 6)
    mean_sums, mlp_grad = lax.optimization_barrier((mean_sums, mlp_grad))
    mlp_grad = lax.all_to_all(mlp_grad, "seq", 0, 0, tiled=True)
    means = jnp.sum(mean_sums, 0).reshape(2, all_tokens).T / width
    query_term = jnp.sum(d_q * q_n, 0)
    key_term = jnp.sum(d_k * k_n, 0)
    d_q_lin = (inv[:, 0:1] * (d_qg - q_n * means[:, 0:1])).astype(bf16)
    d_k_lin = (inv[:, 1:2] * (d_kg - k_n * means[:, 1:2])).astype(bf16)
    d_lin = jnp.concatenate([d_q_lin, d_k_lin, d_v], axis=1)
    qkv_part = t_dot(x_all, d_lin).astype(bf16)
    d_hidden, down_grad = lax.optimization_barrier((d_hidden, down_grad))
    def spread(term):
        full = jnp.zeros((width,), f32)
        for i in range(heads):
            full = lax.dynamic_update_slice_in_dim(full, term[i * HEAD_DIM : (i + 1) * HEAD_DIM], head_of(s_index, i) * HEAD_DIM, 0)
        return full

    terms = jnp.stack([spread(query_term), spread(key_term), attention_term[0], feed_term[0]])
    terms = jnp.swapaxes(terms.reshape(4, n_dev, rows), 0, 1)
    terms = jnp.pad(terms, ((0, 0), (0, 4), (0, 128 - rows)))
    input_grad, all_terms = last_sum(dot_t(after(d_lin, qkv_part), qkv_all).astype(bf16), d_hidden, terms, n_w, n_s, 7)
    input_grad = input_grad.reshape(inputs.shape)
    qkv_grad = wide_scatter(qkv_part)
    out_grad = wide_scatter(after(out_part, qkv_grad, input_grad).reshape(cols, width))
    if not halves:
        out_grad = lax.ppermute(out_grad, ("wide", "seq"), back_moves)

    qkv_grad = final_exchange(after(qkv_grad, input_grad).reshape(n_s, rows, 3 * cols), n_w, n_s, 8)
    gate_grad, up_grad = unpack(mlp_grad.reshape(n_s, rows, 2 * half), feed, feed_plan)
    query_grad, key_grad, value_grad = unpack(qkv_grad, width, qkv_plan)
    gain_grads = jnp.sum(all_terms, 0)[:4, :rows]
    if not own_blocks:
        down_grad = lax.ppermute(down_grad, ("wide", "seq"), back_moves)
    return (layer_out.reshape(inputs.shape), input_grad, query_grad, key_grad, value_grad, out_grad.astype(f32),
            gain_grads[0], gain_grads[1], gain_grads[2], gate_grad, up_grad, down_grad.astype(f32), gain_grads[3])


def solution(mesh):
    tok = P(None, "wide", "seq", None)
    docs = P(None, "wide", None)
    mat = P(("wide", "seq"), None)
    vec = P(("wide", "seq"))

    def body(*args):
        return on_device(mesh.shape["wide"], mesh.shape["seq"], *args)

    return jax.shard_map(
        body,
        mesh=mesh,
        in_specs=(tok, docs, tok, mat, mat, mat, mat, vec, vec, vec, mat, mat, mat, vec),
        out_specs=(tok, tok, mat, mat, mat, mat, vec, vec, vec, mat, mat, mat, vec),
        check_vma=False,
    )
```
